128 devices in a mesh: row: 16 (over z, x_hi, core), col: 8 (over y, x_lo).
Axes of the slice: x: 4 (x_hi: 2, x_lo: 2; x = x_hi * 2 + x_lo), y: 4, z: 4, core: 2. Of those that a mesh axis runs over, the one named last changes fastest.
Arguments:
- queries: bfloat16 [1024, 8192], P('col', 'row'), may hold values from -8 to 8
- cache_keys: bfloat16 [8, 131072, 128], P(None, ('row', 'col')), may hold values from -8 to 8
- cache_values: bfloat16 [8, 131072, 128], P(None, ('row', 'col')), may hold values from -6 to 6
- stretch_keys: bfloat16 [8, 1024, 128], P(None, 'col'), may hold values from -8 to 8
- stretch_values: bfloat16 [8, 1024, 128], P(None, 'col'), may hold values from -6 to 6
- block_lists: int32 [8, 8, 64], replicated, may hold values from 0 to 1023, as said below
- out_weight: bfloat16 [8192, 8192], P('row', 'col'), may hold values from -0.5 to 0.5
- residual: bfloat16 [1024, 8192], P('row', 'col'), may hold values from -6 to 6
- norm_gain: bfloat16 [8192], P('col'), may hold values from 0.25 to 1.75
- gate_weight: bfloat16 [8192, 28672], P('col', 'row'), may hold values from -0.0625 to 0.0625
- up_weight: bfloat16 [8192, 28672], P('col', 'row'), may hold values from -0.0625 to 0.0625
- down_weight: bfloat16 [28672, 8192], P('row', 'col'), may hold values from -0.03125 to 0.03125
Outputs:
- layer_out: bfloat16 [1024, 8192], P('row', 'col')
The draws below stay inside these ranges and needn't reach their ends.
Inputs may be any that keep to these rules, and one draw needn't show every extreme that they name: `block_lists`: each list names 64 different cache blocks; device k of row+col holds cache blocks k * (8) to (k + 1) * 8 - 1, and no two blocks of one list lie on the same device. Every list holds block 0 and block 1023.
All inputs are finite; a program needn't handle non-finite values.
Results may differ from the reference program's by a relative error of at most 0.0085.
Values may be sent and summed in bfloat16 or wider, within the bound.
No kernel may reach another device: no remote copies, remote signals or barrier semaphores. Data moves between devices by JAX's collectives and lax.ppermute only.
A program may use at most 128 MiB of HBM per device.

```python
import math
import jax
import jax.numpy as jnp
from jax import lax

D = 8192
FF = 28672
HEADS = 64
KV_HEADS = 8
HEAD_DIM = 128
BLK = 128
CTX_DEV = 1024
NSEL = 64
GROUP = 8
CTX = 131072
TOKENS = 1024
DEVICES = 128


def draw_queries(key, part):
    shape_full = (TOKENS, HEADS, HEAD_DIM)
    base_draw = jnp.clip(jax.random.normal(jax.random.fold_in(key, 21), shape_full, jnp.float32), -8.0, 8.0)
    return base_draw.reshape(TOKENS, HEADS * HEAD_DIM).astype(jnp.bfloat16)


def draw_cache_keys(key, part):
    shape_full = (KV_HEADS, CTX, HEAD_DIM)
    drawn = jnp.clip(2.0 * jax.random.normal(jax.random.fold_in(key, 31), shape_full, jnp.float32), -8.0, 8.0)
    return drawn.astype(jnp.bfloat16)


def draw_block_lists(key, part):
    list_count = TOKENS // BLK * KV_HEADS
    per_device = CTX_DEV // BLK
    list_keys = jax.random.split(jax.random.fold_in(key, 41), list_count)

    def one_list(list_key):
        middle = jax.random.permutation(list_key, DEVICES - 2)[:NSEL - 2] + 1
        offsets = jax.random.randint(jax.random.fold_in(list_key, 1), (NSEL - 2,), 0, per_device)
        anchored = jnp.array([0, DEVICES * per_device - 1], dtype=jnp.int32)
        return jnp.concatenate([anchored, (middle * per_device + offsets).astype(jnp.int32)])
    return jax.vmap(one_list)(list_keys).reshape(TOKENS // BLK, KV_HEADS, NSEL)


def steps_of(own_key, extent, cuts, smallest, largest):
    def one(dim, shards_of):
        steps = jax.random.uniform(jax.random.fold_in(jax.random.fold_in(own_key, 6), dim), (shards_of,), jnp.float32, smallest / len(cuts), largest / len(cuts))
        return jnp.repeat(jnp.exp(steps), extent[dim] // shards_of).reshape((-1,) + (1,) * (len(extent) - dim - 1))

    gain = one(*cuts[0])
    for cut in cuts[1:]:
        gain = gain * one(*cut)
    return gain


def noise(key, dims, spread, most, pieces=(), kind=jnp.bfloat16):
    entries = jax.random.normal(key, dims, jnp.float32) * spread
    if len(pieces) > 0:
        entries = steps_of(key, dims, pieces, -0.22, 0.18) * entries
    return jnp.clip(entries, min=-most, max=most).astype(kind)


def setup_inputs(seed: int = 0) -> dict:
    keys = jax.random.split(jax.random.key(seed), 13)
    return {
        "queries": draw_queries(jax.random.fold_in(keys[12], 71), 0),
        "cache_keys": draw_cache_keys(jax.random.fold_in(keys[12], 71), 0),
        "cache_values": noise(keys[2], (KV_HEADS, CTX, HEAD_DIM), 1.0, 6.0, ((1, 128),)),
        "stretch_keys": noise(keys[3], (KV_HEADS, TOKENS, HEAD_DIM), 2.0, 8.0, ((1, 8),)),
        "stretch_values": noise(keys[4], (KV_HEADS, TOKENS, HEAD_DIM), 1.0, 6.0, ((1, 8),)),
        "block_lists": draw_block_lists(jax.random.fold_in(keys[12], 71), 0),
        "out_weight": noise(keys[6], (HEADS * HEAD_DIM, D), (HEADS * HEAD_DIM // 64) ** -0.5, 0.5, ((0, 16), (1, 8))),
        "residual": noise(keys[7], (TOKENS, D), 1.0, 6.0, ((0, 16), (1, 8))),
        "norm_gain": jnp.clip(1.0 + 0.15 * jax.random.normal(keys[8], (D,), jnp.float32), 0.25, 1.75).astype(jnp.bfloat16),
        "gate_weight": noise(keys[9], (D, FF), D ** -0.5, 0.0625, ((0, 8), (1, 16))),
        "up_weight": noise(keys[10], (D, FF), D ** -0.5, 0.0625, ((0, 8), (1, 16))),
        "down_weight": noise(keys[11], (FF, D), FF ** -0.5, 0.03125, ((0, 16), (1, 8))),
    }


def reference(queries, cache_keys, cache_values, stretch_keys, stretch_values, block_lists, out_weight, residual, norm_gain, gate_weight, up_weight, down_weight):
    scaling = 1.0 / math.sqrt(HEAD_DIM)
    query_blocks = TOKENS // BLK
    keys_blocked = cache_keys.reshape(KV_HEADS, CTX // BLK, BLK, HEAD_DIM)
    values_blocked = cache_values.reshape(KV_HEADS, CTX // BLK, BLK, HEAD_DIM)
    grouped = queries.reshape(query_blocks, BLK, KV_HEADS, GROUP, HEAD_DIM)
    row_pos = jnp.arange(BLK * GROUP, dtype=jnp.int32) // GROUP
    key_pos = jnp.arange(TOKENS, dtype=jnp.int32)

    def attend(item_index):
        block_index = item_index // KV_HEADS
        head_index = item_index % KV_HEADS
        query_rows = grouped[block_index, :, head_index].reshape(BLK * GROUP, HEAD_DIM)
        chosen = block_lists[block_index, head_index]
        far_keys = keys_blocked[head_index][chosen].reshape(NSEL * BLK, HEAD_DIM)
        far_values = values_blocked[head_index][chosen].reshape(NSEL * BLK, HEAD_DIM)
        near_keys = stretch_keys[head_index]
        near_values = stretch_values[head_index]
        far_scores = jnp.dot(query_rows, far_keys.T, preferred_element_type=jnp.float32) * scaling
        near_scores = jnp.dot(query_rows, near_keys.T, preferred_element_type=jnp.float32) * scaling
        allowed = key_pos[None, :] <= (block_index * BLK + row_pos)[:, None]
        near_scores = jnp.where(allowed, near_scores, -1e+30)
        row_top = jnp.maximum(lax.optimization_barrier(jnp.max(far_scores, axis=1)), lax.optimization_barrier(jnp.max(near_scores, axis=1)))
        far_exp = jnp.exp(far_scores - row_top[:, None])
        near_exp = jnp.where(allowed, jnp.exp(near_scores - row_top[:, None]), 0.0)
        totals = lax.optimization_barrier(jnp.sum(far_exp, axis=1)) + lax.optimization_barrier(jnp.sum(near_exp, axis=1))
        mixed_rows = jnp.dot(far_exp.astype(jnp.bfloat16), far_values, preferred_element_type=jnp.float32)
        mixed_rows = mixed_rows + jnp.dot(near_exp.astype(jnp.bfloat16), near_values, preferred_element_type=jnp.float32)
        return (mixed_rows / totals[:, None]).astype(jnp.bfloat16).reshape(BLK, GROUP * HEAD_DIM)
    outputs = lax.map(attend, jnp.arange(query_blocks * KV_HEADS, dtype=jnp.int32))
    outputs = outputs.reshape(query_blocks, KV_HEADS, BLK, GROUP * HEAD_DIM)
    attended = jnp.transpose(outputs, (0, 2, 1, 3)).reshape(TOKENS, HEADS * HEAD_DIM)
    stream = residual.astype(jnp.float32) + jnp.dot(attended, out_weight, preferred_element_type=jnp.float32)
    squares = lax.optimization_barrier(jnp.mean(stream * stream, axis=1))
    normed = (stream * lax.rsqrt(squares + 1e-05)[:, None] * norm_gain.astype(jnp.float32)).astype(jnp.bfloat16)
    gate_proj = jnp.dot(normed, gate_weight, preferred_element_type=jnp.float32)
    up_proj = jnp.dot(normed, up_weight, preferred_element_type=jnp.float32)
    hidden = (jax.nn.silu(gate_proj) * up_proj).astype(jnp.bfloat16)
    lowered = jnp.dot(hidden, down_weight, preferred_element_type=jnp.float32)
    return (stream + lowered).astype(jnp.bfloat16)
```

```python
import functools
import math

import jax
import jax.numpy as jnp
from jax import lax
from jax.experimental import pallas as pl
from jax.experimental.pallas import tpu as pltpu
from jax.sharding import Mesh, PartitionSpec as P

D = 8192
KV_HEADS = 8
HEAD_DIM = 128
BLK = 128
GROUP = 8
AXES = ("z", "xh", "core", "y", "xl")
ROW = ("z", "xh", "core")
ZXH = ("z", "xh")
COL = ("y", "xl")
CHIP = ("z", "xh", "y", "xl")
NEG = -1e30
bf16 = jnp.bfloat16
f32 = jnp.float32


def nt_dot(a, b):
    return lax.dot_general(a, b, (((1,), (1,)), ((), ())), preferred_element_type=f32)


def tn_dot(a, b):
    return lax.dot_general(a, b, (((0,), (0,)), ((), ())), preferred_element_type=f32)


def attend_kernel(
    scale,
    per_step,
    local_blocks,
    list_ref,
    place_ref,
    own_q_ref,
    other_q_ref,
    keys_ref,
    values_ref,
    near_keys_ref,
    near_values_ref,
    own_ref,
    send_ref,
    order_ref,
    q_ref,
    top_ref,
    sum_ref,
    acc_ref,
):
    core = place_ref[0]
    block = place_ref[1]
    length = list_ref.shape[0]
    heads = own_q_ref.shape[1] // HEAD_DIM
    rows = heads * BLK
    for h in range(heads):
        cols = pl.ds(h * HEAD_DIM, HEAD_DIM)
        q_ref[pl.ds(h * BLK, BLK), :] = own_q_ref[:, cols]
        q_ref[pl.ds(rows + h * BLK, BLK), :] = other_q_ref[:, cols]
    top_ref[...] = jnp.full_like(top_ref, NEG)
    sum_ref[...] = jnp.zeros_like(sum_ref)
    acc_ref[...] = jnp.zeros_like(acc_ref)

    def collect(i, count):
        device = list_ref[i] // local_blocks
        row = device // 8
        order_ref[count] = (row // 2) * 8 + device % 8
        return count + jnp.where(row % 2 == core, 1, 0)

    count = lax.fori_loop(0, length, collect, jnp.int32(0))

    def update(half, keys, values, bias):
        part = pl.ds(half * rows, rows)
        scores = nt_dot(keys, q_ref[part, :]) * scale
        if bias is not None:
            scores = scores + bias
        old = top_ref[half]
        new = jnp.maximum(old, jnp.max(scores, axis=0, keepdims=True))
        weights = jnp.exp(scores - new)
        decay = jnp.exp(old - new)
        top_ref[half] = new
        sum_ref[half] = sum_ref[half] * decay + jnp.sum(weights, axis=0, keepdims=True)
        acc_ref[half] = acc_ref[half] * decay + tn_dot(values, weights.astype(bf16))

    def far(step, carry):
        slots = [jnp.minimum(step * per_step + i, count - 1) for i in range(per_step)]
        keys = jnp.concatenate([keys_ref[order_ref[s]] for s in slots], axis=0)
        values = jnp.concatenate([values_ref[order_ref[s]] for s in slots], axis=0)
        bias = jnp.concatenate(
            [
                jnp.full((BLK, 1), jnp.where(step * per_step + i < count, 0.0, NEG), f32)
                for i in range(per_step)
            ],
            axis=0,
        )
        for half in range(2):
            update(half, keys, values, bias)
        return carry

    lax.fori_loop(0, (count + per_step - 1) // per_step, far, 0)

    def near(j, carry):
        which = core + 2 * j
        shift = (block - which) * BLK
        key_pos = lax.broadcasted_iota(jnp.int32, (BLK, rows), 0)
        token = lax.broadcasted_iota(jnp.int32, (BLK, rows), 1) % BLK
        bias = jnp.where(key_pos <= token + shift, 0.0, NEG)
        for half in range(2):
            update(half, near_keys_ref[which], near_values_ref[which], bias)
        return carry

    lax.fori_loop(0, (block - core + 2) // 2, near, 0)
    own_ref[0:HEAD_DIM, :] = acc_ref[0]
    own_ref[HEAD_DIM : HEAD_DIM + 1, :] = top_ref[0]
    own_ref[HEAD_DIM + 1 : HEAD_DIM + 2, :] = sum_ref[0]
    send_ref[0:HEAD_DIM, :] = acc_ref[1]
    send_ref[HEAD_DIM : HEAD_DIM + 1, :] = top_ref[1]
    send_ref[HEAD_DIM + 1 : HEAD_DIM + 2, :] = sum_ref[1]


def attend(my_list, place, own_q, other_q, keys, values, near_keys, near_values, local_blocks):
    heads = own_q.shape[1] // HEAD_DIM
    rows = heads * BLK
    packed = jax.ShapeDtypeStruct((HEAD_DIM + 8, rows), f32)
    smem = pl.BlockSpec(memory_space=pltpu.SMEM)
    vmem = pl.BlockSpec(memory_space=pltpu.VMEM)
    return pl.pallas_call(
        functools.partial(attend_kernel, 1.0 / math.sqrt(HEAD_DIM), 2, local_blocks),
        out_shape=(packed, packed),
        in_specs=[smem, smem] + [vmem] * 6,
        out_specs=(vmem, vmem),
        scratch_shapes=[
            pltpu.SMEM((my_list.shape[0] + 1,), jnp.int32),
            pltpu.VMEM((2 * rows, HEAD_DIM), bf16),
            pltpu.VMEM((2, 1, rows), f32),
            pltpu.VMEM((2, 1, rows), f32),
            pltpu.VMEM((2, HEAD_DIM, rows), f32),
        ],
        compiler_params=pltpu.CompilerParams(vmem_limit_bytes=48 * 1024 * 1024),
        cost_estimate=pl.CostEstimate(
            flops=4 * 2 * rows * 40 * BLK * HEAD_DIM,
            bytes_accessed=2 * keys.size * 2,
            transcendentals=2 * rows * 40 * BLK,
        ),
    )(my_list, place, own_q, other_q, keys, values, near_keys, near_values)


def merge_kernel(own_ref, got_ref, out_ref):
    own_top = own_ref[HEAD_DIM : HEAD_DIM + 1, :]
    got_top = got_ref[HEAD_DIM : HEAD_DIM + 1, :]
    top = jnp.maximum(own_top, got_top)
    own_w = jnp.exp(own_top - top)
    got_w = jnp.exp(got_top - top)
    total = own_w * own_ref[HEAD_DIM + 1 : HEAD_DIM + 2, :] + got_w * got_ref[HEAD_DIM + 1 : HEAD_DIM + 2, :]
    mixed = (own_ref[0:HEAD_DIM, :] * own_w + got_ref[0:HEAD_DIM, :] * got_w) / total
    heads = mixed.shape[1] // BLK
    for h in range(heads):
        piece = mixed[:, h * BLK : (h + 1) * BLK].T.astype(bf16)
        for i in range(out_ref.shape[0]):
            out_ref[i, :, pl.ds(h * HEAD_DIM, HEAD_DIM)] = piece


def merge(own, got, copies):
    heads = own.shape[1] // BLK
    vmem = pl.BlockSpec(memory_space=pltpu.VMEM)
    return pl.pallas_call(
        merge_kernel,
        out_shape=jax.ShapeDtypeStruct((copies, BLK, heads * HEAD_DIM), bf16),
        in_specs=[vmem, vmem],
        out_specs=vmem,
    )(own, got)


def exchange(x, axes):
    return lax.all_to_all(x, axes, split_axis=0, concat_axis=0, tiled=True)


def swap(x):
    return lax.ppermute(x, "core", [(0, 1), (1, 0)])


def spread(x, copies):
    return jnp.broadcast_to(x[None], (copies,) + x.shape)


def mm(a, b):
    return jnp.dot(a, b, preferred_element_type=f32)


def local(
    queries,
    cache_keys,
    cache_values,
    stretch_keys,
    stretch_values,
    block_lists,
    out_weight,
    residual,
    norm_gain,
    gate_weight,
    up_weight,
    down_weight,
):
    core = lax.axis_index("core")
    col = lax.axis_index(COL)
    row = lax.axis_index(ROW)
    group = lax.axis_index(ZXH)
    me = row * 8 + col
    local_blocks = cache_keys.shape[1] // BLK
    tokens_here = residual.shape[0]

    matched = block_lists // local_blocks == me
    within = jnp.sum(jnp.where(matched, block_lists % local_blocks, 0), axis=2)
    source = (jnp.arange(KV_HEADS, dtype=jnp.int32)[:, None] * local_blocks + within.T).reshape(-1)
    flat_keys = cache_keys.reshape(KV_HEADS * local_blocks, BLK, HEAD_DIM)
    flat_values = cache_values.reshape(KV_HEADS * local_blocks, BLK, HEAD_DIM)
    keys = exchange(flat_keys[source], CHIP)
    values = exchange(flat_values[source], CHIP)
    near_keys = exchange(spread(lax.dynamic_index_in_dim(stretch_keys, group, 0, keepdims=False), 8), COL)
    near_values = exchange(spread(lax.dynamic_index_in_dim(stretch_values, group, 0, keepdims=False), 8), COL)
    my_list = block_lists[col, group]
    place = jnp.stack([core, col]).astype(jnp.int32)
    own, send = attend(
        my_list, place, queries, swap(queries), keys, values,
        near_keys.reshape(8, BLK, HEAD_DIM), near_values.reshape(8, BLK, HEAD_DIM), local_blocks,
    )
    attended = exchange(merge(own, swap(send), 8), COL)

    def halves(x):
        x = x.reshape(8, 2, tokens_here, x.shape[-1])
        mine = lax.dynamic_index_in_dim(x, core, 1, keepdims=False)
        theirs = lax.dynamic_index_in_dim(x, 1 - core, 1, keepdims=False)
        return mine, theirs

    def row_sum(mine, theirs, weight):
        give = mm(theirs, weight).astype(bf16)
        both = mm(mine, weight) + swap(give).astype(f32)
        return jnp.sum(exchange(both.astype(bf16), ZXH).astype(f32), axis=0)

    stream = residual.astype(f32) + row_sum(*halves(attended), out_weight)
    gain = norm_gain.astype(f32)[None, :]
    scaled = (stream * gain).astype(bf16)
    own_rows = exchange(spread(scaled, 8), ZXH)
    other_rows = swap(own_rows)

    def squares(x):
        plain = x.astype(f32) / gain[None]
        return jnp.sum(plain * plain, axis=2)

    parts = jnp.stack([squares(own_rows), squares(other_rows)], axis=1)
    totals = jnp.sum(exchange(parts, COL), axis=0)
    factor = lax.rsqrt(totals.reshape(2, tokens_here) / D + 1e-05)

    def hidden_of(x, factor):
        gate = jnp.sum(exchange(mm(x, gate_weight).astype(bf16), COL).astype(f32), axis=0)
        up = jnp.sum(exchange(mm(x, up_weight).astype(bf16), COL).astype(f32), axis=0)
        gate = gate * factor[:, None]
        hidden = (jax.nn.silu(gate) * (up * factor[:, None])).astype(bf16)
        return exchange(spread(hidden, 8), COL)

    own_hidden = hidden_of(own_rows, factor[0])
    other_hidden = hidden_of(other_rows, factor[1])
    return (stream + row_sum(own_hidden, other_hidden, down_weight)).astype(bf16)


def solution(mesh):
    mesh = Mesh(mesh.devices.reshape(4, 2, 2, 4, 2), AXES)
    in_specs = (
        P(COL, ROW),
        P(None, ROW + COL, None),
        P(None, ROW + COL, None),
        P(None, COL, None),
        P(None, COL, None),
        P(),
        P(ROW, COL),
        P(ROW, COL),
        P(COL),
        P(COL, ROW),
        P(COL, ROW),
        P(ROW, COL),
    )
    return jax.shard_map(local, mesh=mesh, in_specs=in_specs, out_specs=P(ROW, COL), check_vma=False)
```

```python
import functools
import math

import jax
import jax.numpy as jnp
from jax import lax
from jax.experimental import pallas as pl
from jax.experimental.pallas import tpu as pltpu
from jax.sharding import Mesh, PartitionSpec as P

D = 8192
KV_HEADS = 8
HEAD_DIM = 128
BLK = 128
GROUP = 8
AXES = ("z", "xh", "core", "y", "xl")
ROW = ("z", "xh", "core")
ZXH = ("z", "xh")
COL = ("y", "xl")
CHIP = ("z", "xh", "y", "xl")
NEG = -1e30
bf16 = jnp.bfloat16
f32 = jnp.float32


def nt_dot(a, b):
    return lax.dot_general(a, b, (((1,), (1,)), ((), ())), preferred_element_type=f32)


def tn_dot(a, b):
    return lax.dot_general(a, b, (((0,), (0,)), ((), ())), preferred_element_type=f32)


def attend_kernel(
    scale,
    per_step,
    local_blocks,
    list_ref,
    place_ref,
    own_q_ref,
    other_q_ref,
    keys_ref,
    values_ref,
    own_ref,
    send_ref,
    order_ref,
    q_ref,
    top_ref,
    sum_ref,
    acc_ref,
):
    core = place_ref[0]
    block = place_ref[1]
    length = list_ref.shape[0]
    heads = own_q_ref.shape[1] // HEAD_DIM
    rows = heads * BLK
    for h in range(heads):
        cols = pl.ds(h * HEAD_DIM, HEAD_DIM)
        q_ref[pl.ds(h * BLK, BLK), :] = own_q_ref[:, cols]
        q_ref[pl.ds(rows + h * BLK, BLK), :] = other_q_ref[:, cols]
    top_ref[...] = jnp.full_like(top_ref, NEG)
    sum_ref[...] = jnp.zeros_like(sum_ref)
    acc_ref[...] = jnp.zeros_like(acc_ref)

    def collect(i, count):
        device = list_ref[i] // local_blocks
        row = device // 8
        order_ref[count] = (row // 2) * 8 + device % 8
        return count + jnp.where(row % 2 == core, 1, 0)

    count = lax.fori_loop(0, length, collect, jnp.int32(0))

    def update(half, keys, values, bias):
        part = pl.ds(half * rows, rows)
        scores = nt_dot(keys, q_ref[part, :]) * scale
        if bias is not None:
            scores = scores + bias
        old = top_ref[half]
        new = jnp.maximum(old, jnp.max(scores, axis=0, keepdims=True))
        weights = jnp.exp2(scores - new)
        decay = jnp.exp2(old - new)
        top_ref[half] = new
        sum_ref[half] = sum_ref[half] * decay + jnp.sum(weights, axis=0, keepdims=True)
        acc_ref[half] = acc_ref[half] * decay + tn_dot(values, weights.astype(bf16))

    def far(step, carry):
        slots = [jnp.minimum(step * per_step + i, count - 1) for i in range(per_step)]
        keys = jnp.concatenate([keys_ref[order_ref[s], 0:BLK] for s in slots], axis=0)
        values = jnp.concatenate([values_ref[order_ref[s], 0:BLK] for s in slots], axis=0)
        bias = jnp.concatenate(
            [
                jnp.full((BLK, 1), jnp.where(step * per_step + i < count, 0.0, NEG), f32)
                for i in range(per_step)
            ],
            axis=0,
        )
        for half in range(2):
            update(half, keys, values, bias)
        return carry

    lax.fori_loop(0, (count + per_step - 1) // per_step, far, 0)

    def near(j, carry):
        which = core + 2 * j
        shift = (block - which) * BLK
        key_pos = lax.broadcasted_iota(jnp.int32, (BLK, rows), 0)
        token = lax.broadcasted_iota(jnp.int32, (BLK, rows), 1) % BLK
        bias = jnp.where(key_pos <= token + shift, 0.0, NEG)
        keys = jnp.concatenate([keys_ref[i * 8 + which, BLK:] for i in range(8)], axis=0)
        values = jnp.concatenate([values_ref[i * 8 + which, BLK:] for i in range(8)], axis=0)
        for half in range(2):
            update(half, keys, values, bias)
        return carry

    lax.fori_loop(0, (block - core + 2) // 2, near, 0)
    own_ref[0:HEAD_DIM, :] = acc_ref[0]
    own_ref[HEAD_DIM : HEAD_DIM + 1, :] = top_ref[0]
    own_ref[HEAD_DIM + 1 : HEAD_DIM + 2, :] = sum_ref[0]
    send_ref[0:HEAD_DIM, :] = acc_ref[1]
    send_ref[HEAD_DIM : HEAD_DIM + 1, :] = top_ref[1]
    send_ref[HEAD_DIM + 1 : HEAD_DIM + 2, :] = sum_ref[1]


def attend(my_list, place, own_q, other_q, keys, values, local_blocks):
    heads = own_q.shape[1] // HEAD_DIM
    rows = heads * BLK
    packed = jax.ShapeDtypeStruct((HEAD_DIM + 8, rows), f32)
    smem = pl.BlockSpec(memory_space=pltpu.SMEM)
    vmem = pl.BlockSpec(memory_space=pltpu.VMEM)
    return pl.pallas_call(
        functools.partial(attend_kernel, math.log2(math.e) / math.sqrt(HEAD_DIM), 4, local_blocks),
        out_shape=(packed, packed),
        in_specs=[smem, smem] + [vmem] * 4,
        out_specs=(vmem, vmem),
        scratch_shapes=[
            pltpu.SMEM((my_list.shape[0] + 1,), jnp.int32),
            pltpu.VMEM((2 * rows, HEAD_DIM), bf16),
            pltpu.VMEM((2, 1, rows), f32),
            pltpu.VMEM((2, 1, rows), f32),
            pltpu.VMEM((2, HEAD_DIM, rows), f32),
        ],
        cost_estimate=pl.CostEstimate(
            flops=4 * 2 * rows * 40 * BLK * HEAD_DIM,
            bytes_accessed=2 * keys.size * 2,
            transcendentals=2 * rows * 40 * BLK,
        ),
    )(my_list, place, own_q, other_q, keys, values)


def merge_kernel(own_ref, got_ref, out_ref):
    own_top = own_ref[HEAD_DIM : HEAD_DIM + 1, :]
    got_top = got_ref[HEAD_DIM : HEAD_DIM + 1, :]
    top = jnp.maximum(own_top, got_top)
    own_w = jnp.exp2(own_top - top)
    got_w = jnp.exp2(got_top - top)
    total = own_w * own_ref[HEAD_DIM + 1 : HEAD_DIM + 2, :] + got_w * got_ref[HEAD_DIM + 1 : HEAD_DIM + 2, :]
    mixed = (own_ref[0:HEAD_DIM, :] * own_w + got_ref[0:HEAD_DIM, :] * got_w) / total
    heads = mixed.shape[1] // BLK
    for h in range(heads):
        piece = mixed[:, h * BLK : (h + 1) * BLK].T.astype(bf16)
        for i in range(out_ref.shape[0]):
            out_ref[i, :, pl.ds(h * HEAD_DIM, HEAD_DIM)] = piece


def merge(own, got, copies):
    heads = own.shape[1] // BLK
    vmem = pl.BlockSpec(memory_space=pltpu.VMEM)
    return pl.pallas_call(
        merge_kernel,
        out_shape=jax.ShapeDtypeStruct((copies, BLK, heads * HEAD_DIM), bf16),
        in_specs=[vmem, vmem],
        out_specs=vmem,
    )(own, got)


def product_kernel(tiles, pick_ref, x_ref, *refs):
    weight_refs, add_ref, out_ref = refs[:tiles[0]], refs[tiles[0] : -1], refs[-1]
    x = x_ref[...].reshape(-1, x_ref.shape[-1])
    step = pl.program_id(0)

    def put(weight_ref):
        total = jnp.dot(x, weight_ref[...], preferred_element_type=f32)
        if add_ref:
            total = total + add_ref[0][...].reshape(total.shape).astype(f32)
        out_ref[...] = total.astype(out_ref.dtype).reshape(out_ref.shape)

    for i, weight_ref in enumerate(weight_refs):
        pl.when(step // tiles[1] == i)(functools.partial(put, weight_ref))


def product(x, weights, tile, pick=None, add=None):
    blocks, pair, tokens, inputs = x.shape
    width = weights[0].shape[1]
    count = width // tile
    taken = pair if pick is None else 1
    pick = jnp.zeros((1,), jnp.int32) if pick is None else pick.astype(jnp.int32).reshape(1)
    out_block = (blocks, taken, tokens, tile)

    def weight_spec(i):
        return pl.BlockSpec((inputs, tile), lambda n, p, i=i: (0, jnp.clip(n - i * count, 0, count - 1)))

    by_column = pl.BlockSpec(out_block, lambda n, p: (0, 0, 0, n))
    specs = [pl.BlockSpec((blocks, taken, tokens, inputs), lambda n, p: (0, p[0], 0, 0))]
    specs += [weight_spec(i) for i in range(len(weights))]
    operands = [x, *weights]
    if add is not None:
        specs.append(by_column)
        operands.append(add)
    rows = blocks * taken * tokens
    columns = width * len(weights)
    return pl.pallas_call(
        functools.partial(product_kernel, (len(weights), count)),
        out_shape=jax.ShapeDtypeStruct((blocks, taken, tokens, columns), bf16),
        grid_spec=pltpu.PrefetchScalarGridSpec(
            num_scalar_prefetch=1, grid=(count * len(weights),), in_specs=specs, out_specs=by_column
        ),
        cost_estimate=pl.CostEstimate(
            flops=2 * rows * inputs * columns,
            bytes_accessed=2 * (rows * inputs + inputs * columns + rows * columns),
            transcendentals=0,
        ),
    )(pick, *operands)


def split_sum_kernel(side_ref, x_ref, give_ref, keep_ref):
    side = side_ref[0]
    give_ref[...] = jnp.sum(x_ref[:, 1 - side].astype(f32), axis=0).astype(bf16)
    keep_ref[...] = jnp.sum(x_ref[:, side].astype(f32), axis=0)


def split_sum(x, side):
    count, _, tokens, width = x.shape
    tile = 896
    by_column = pl.BlockSpec((tokens, tile), lambda n, p: (0, n))
    return pl.pallas_call(
        split_sum_kernel,
        out_shape=(
            jax.ShapeDtypeStruct((tokens, width), bf16),
            jax.ShapeDtypeStruct((tokens, width), f32),
        ),
        grid_spec=pltpu.PrefetchScalarGridSpec(
            num_scalar_prefetch=1,
            grid=(width // tile,),
            in_specs=[pl.BlockSpec((count, 2, tokens, tile), lambda n, p: (0, 0, 0, n))],
            out_specs=(by_column, by_column),
        ),
        cost_estimate=pl.CostEstimate(flops=x.size, bytes_accessed=x.size * 3, transcendentals=0),
    )(side.astype(jnp.int32).reshape(1), x)


def gated_kernel(gate_refs, up_refs, factor_ref, out_ref):
    factor = factor_ref[...]
    gate = sum(jnp.sum(r[...].astype(f32), axis=0) for r in gate_refs) * factor
    up = sum(jnp.sum(r[...].astype(f32), axis=0) for r in up_refs) * factor
    out_ref[...] = (gate / (1.0 + jnp.exp(-gate)) * up).astype(bf16)


def gated(x, extra, factor):
    parts = [x] if extra is None else [x, extra]
    tokens, width = x.shape[1], x.shape[2] // 2
    tile = 896
    count = width // tile

    def kernel(*refs):
        n = len(parts)
        gated_kernel(refs[:n], refs[n : 2 * n], refs[2 * n], refs[2 * n + 1])

    specs = [
        pl.BlockSpec((p.shape[0], tokens, tile), lambda n, first=first: (0, 0, n + first))
        for first in (0, count)
        for p in parts
    ]
    return pl.pallas_call(
        kernel,
        grid=(count,),
        out_shape=jax.ShapeDtypeStruct((tokens, width), bf16),
        in_specs=specs + [pl.BlockSpec((tokens, 1), lambda n: (0, 0))],
        out_specs=pl.BlockSpec((tokens, tile), lambda n: (0, n)),
        cost_estimate=pl.CostEstimate(
            flops=8 * x.size, bytes_accessed=3 * x.size, transcendentals=tokens * width
        ),
    )(*parts, *parts, factor[:, None])


def pair_kernel(side_ref, mine_ref, got_ref, out_ref):
    side = side_ref[0]
    for i in range(out_ref.shape[0]):
        out_ref[i, side] = mine_ref[...]
        out_ref[i, 1 - side] = got_ref[...]


def pair_up(mine, got, side):
    tokens, width = mine.shape
    vmem = pl.BlockSpec(memory_space=pltpu.VMEM)
    return pl.pallas_call(
        pair_kernel,
        out_shape=jax.ShapeDtypeStruct((4, 2, tokens, width), bf16),
        in_specs=[pl.BlockSpec(memory_space=pltpu.SMEM), vmem, vmem],
        out_specs=vmem,
        cost_estimate=pl.CostEstimate(flops=0, bytes_accessed=mine.size * 20, transcendentals=0),
    )(side.astype(jnp.int32).reshape(1), mine, got)


def exchange(x, axes):
    return lax.all_to_all(x, axes, split_axis=0, concat_axis=0, tiled=True)


def swap(x, axis="core"):
    return lax.ppermute(x, axis, [(0, 1), (1, 0)])


def spread(x, copies):
    return jnp.broadcast_to(x[None], (copies,) + x.shape)


def take(x, index, axis):
    return lax.dynamic_index_in_dim(x, index, axis, keepdims=False)


def local(
    queries,
    cache_keys,
    cache_values,
    stretch_keys,
    stretch_values,
    block_lists,
    out_weight,
    residual,
    norm_gain,
    gate_weight,
    up_weight,
    down_weight,
):
    core = lax.axis_index("core")
    side = lax.axis_index("xl")
    col = lax.axis_index(COL)
    group = lax.axis_index(ZXH)
    me = lax.axis_index(ROW) * 8 + col
    local_blocks = cache_keys.shape[1] // BLK
    tokens_here = residual.shape[0]

    matched = block_lists // local_blocks == me
    within = jnp.sum(jnp.where(matched, block_lists % local_blocks, 0), axis=2)
    source = (jnp.arange(KV_HEADS, dtype=jnp.int32)[:, None] * local_blocks + within.T).reshape(-1)

    def fetch(cache, stretch):
        flat = cache.reshape(KV_HEADS * local_blocks, BLK, HEAD_DIM)
        part = BLK // 8
        near = lax.dynamic_slice_in_dim(stretch, group * part, part, 1)
        near = jnp.broadcast_to(near[:, None], (KV_HEADS, 8, part, HEAD_DIM)).reshape(64, part, HEAD_DIM)
        return exchange(jnp.concatenate([flat[source], near], axis=1), CHIP)

    keys = fetch(cache_keys, stretch_keys)
    values = fetch(cache_values, stretch_values)
    my_list = block_lists[col, group]
    place = jnp.stack([core, col]).astype(jnp.int32)
    own, send = attend(my_list, place, queries, swap(queries), keys, values, local_blocks)
    attended = exchange(merge(own, swap(send), 8), COL).reshape(8, 2, tokens_here, -1)

    def row_sum(give, mine, pick, weight):
        both = product(mine, (weight,), 256, pick, add=swap(give))
        return jnp.sum(exchange(both.reshape(8, tokens_here, -1), ZXH).astype(f32), axis=0)

    give = product(attended, (out_weight,), 256, 1 - core)
    stream = residual.astype(f32) + row_sum(give, attended, core, out_weight)
    gain = norm_gain.astype(f32)[None, :]
    scaled = (stream * gain).astype(bf16)
    own_rows = exchange(spread(scaled, 8), ZXH)
    other_rows = swap(own_rows)

    def squares(x):
        plain = x.astype(f32) / gain[None]
        return jnp.sum(plain * plain, axis=2)

    parts = jnp.stack([squares(own_rows), squares(other_rows)], axis=1)
    totals = jnp.sum(exchange(parts, COL), axis=0)
    factor = lax.rsqrt(totals.reshape(2, tokens_here) / D + 1e-05)

    both = (gate_weight, up_weight)
    by_pair = (4, 2, tokens_here, own_rows.shape[-1])
    own_rows = own_rows.reshape(by_pair)
    own_give = product(own_rows, both, 896, 1 - side)
    other_part = exchange(product(other_rows.reshape(by_pair), both, 896), "y")
    own_part = product(own_rows, both, 896, side, add=swap(own_give, "xl"))
    other_give, other_keep = split_sum(other_part, side)
    own_part = exchange(own_part.reshape(4, tokens_here, -1), "y")
    other_hidden = gated(other_keep[None], swap(other_give, "xl")[None], factor[1])
    other_pair = pair_up(other_hidden, swap(other_hidden, "xl"), side)
    own_part, other_pair = lax.optimization_barrier((own_part, other_pair))
    other_all = exchange(other_pair, "y").reshape(8, 1, tokens_here, -1)
    own_hidden = gated(own_part, None, factor[0])
    own_pair = pair_up(own_hidden, swap(own_hidden, "xl"), side)
    own_all = exchange(own_pair, "y").reshape(8, 1, tokens_here, -1)
    give = product(other_all, (down_weight,), 256)
    return (stream + row_sum(give, own_all, None, down_weight)).astype(bf16)


def solution(mesh):
    mesh = Mesh(mesh.devices.reshape(4, 2, 2, 4, 2), AXES)
    in_specs = (
        P(COL, ROW),
        P(None, ROW + COL, None),
        P(None, ROW + COL, None),
        P(None, COL, None),
        P(None, COL, None),
        P(),
        P(ROW, COL),
        P(ROW, COL),
        P(COL),
        P(COL, ROW),
        P(COL, ROW),
        P(ROW, COL),
    )
    return jax.shard_map(local, mesh=mesh, in_specs=in_specs, out_specs=P(ROW, COL), check_vma=False)
```

```python
import functools
import math

import jax
import jax.numpy as jnp
from jax import lax
from jax.experimental import pallas as pl
from jax.experimental.pallas import tpu as pltpu
from jax.sharding import Mesh, PartitionSpec as P

D = 8192
KV_HEADS = 8
HEAD_DIM = 128
BLK = 128
GROUP = 8
AXES = ("z", "xh", "core", "y", "xl")
ROW = ("z", "xh", "core")
ZXH = ("z", "xh")
COL = ("y", "xl")
CHIP = ("z", "xh", "y", "xl")
NEG = -1e30
bf16 = jnp.bfloat16
f32 = jnp.float32


def nt_dot(a, b):
    return lax.dot_general(a, b, (((1,), (1,)), ((), ())), preferred_element_type=f32)


def tn_dot(a, b):
    return lax.dot_general(a, b, (((0,), (0,)), ((), ())), preferred_element_type=f32)


def attend_kernel(
    scale,
    per_step,
    local_blocks,
    list_ref,
    place_ref,
    own_q_ref,
    other_q_ref,
    keys_ref,
    values_ref,
    own_ref,
    send_ref,
    order_ref,
    q_ref,
    top_ref,
    sum_ref,
    acc_ref,
):
    core = place_ref[0]
    block = place_ref[1]
    length = list_ref.shape[0]
    heads = own_q_ref.shape[1] // HEAD_DIM
    rows = heads * BLK
    for h in range(heads):
        cols = pl.ds(h * HEAD_DIM, HEAD_DIM)
        q_ref[pl.ds(h * BLK, BLK), :] = own_q_ref[:, cols]
        q_ref[pl.ds(rows + h * BLK, BLK), :] = other_q_ref[:, cols]
    top_ref[...] = jnp.full_like(top_ref, NEG)
    sum_ref[...] = jnp.zeros_like(sum_ref)
    acc_ref[...] = jnp.zeros_like(acc_ref)

    def collect(i, count):
        device = list_ref[i] // local_blocks
        row = device // 8
        order_ref[count] = (row // 2) * 8 + device % 8
        return count + jnp.where(row % 2 == core, 1, 0)

    count = lax.fori_loop(0, length, collect, jnp.int32(0))

    def update(half, keys, values, bias):
        part = pl.ds(half * rows, rows)
        scores = nt_dot(keys, q_ref[part, :]) * scale
        if bias is not None:
            scores = scores + bias
        old = top_ref[half]
        new = jnp.maximum(old, jnp.max(scores, axis=0, keepdims=True))
        weights = jnp.exp2(scores - new)
        decay = jnp.exp2(old - new)
        top_ref[half] = new
        sum_ref[half] = sum_ref[half] * decay + jnp.sum(weights, axis=0, keepdims=True)
        acc_ref[half] = acc_ref[half] * decay + tn_dot(values, weights.astype(bf16))

    def far(step, carry):
        slots = [jnp.minimum(step * per_step + i, count - 1) for i in range(per_step)]
        keys = jnp.concatenate([keys_ref[order_ref[s], 0:BLK] for s in slots], axis=0)
        values = jnp.concatenate([values_ref[order_ref[s], 0:BLK] for s in slots], axis=0)
        bias = jnp.concatenate(
            [
                jnp.full((BLK, 1), jnp.where(step * per_step + i < count, 0.0, NEG), f32)
                for i in range(per_step)
            ],
            axis=0,
        )
        for half in range(2):
            update(half, keys, values, bias)
        return carry

    lax.fori_loop(0, (count + per_step - 1) // per_step, far, 0)

    def near(j, carry):
        which = core + 2 * j
        shift = (block - which) * BLK
        key_pos = lax.broadcasted_iota(jnp.int32, (BLK, rows), 0)
        token = lax.broadcasted_iota(jnp.int32, (BLK, rows), 1) % BLK
        bias = jnp.where(key_pos <= token + shift, 0.0, NEG)
        keys = jnp.concatenate([keys_ref[i * 8 + which, BLK:] for i in range(8)], axis=0)
        values = jnp.concatenate([values_ref[i * 8 + which, BLK:] for i in range(8)], axis=0)
        for half in range(2):
            update(half, keys, values, bias)
        return carry

    lax.fori_loop(0, (block - core + 2) // 2, near, 0)
    own_ref[0:HEAD_DIM, :] = acc_ref[0]
    own_ref[HEAD_DIM : HEAD_DIM + 1, :] = top_ref[0]
    own_ref[HEAD_DIM + 1 : HEAD_DIM + 2, :] = sum_ref[0]
    send_ref[0:HEAD_DIM, :] = acc_ref[1]
    send_ref[HEAD_DIM : HEAD_DIM + 1, :] = top_ref[1]
    send_ref[HEAD_DIM + 1 : HEAD_DIM + 2, :] = sum_ref[1]


def attend(my_list, place, own_q, other_q, keys, values, local_blocks):
    heads = own_q.shape[1] // HEAD_DIM
    rows = heads * BLK
    packed = jax.ShapeDtypeStruct((HEAD_DIM + 8, rows), f32)
    smem = pl.BlockSpec(memory_space=pltpu.SMEM)
    vmem = pl.BlockSpec(memory_space=pltpu.VMEM)
    return pl.pallas_call(
        functools.partial(attend_kernel, math.log2(math.e) / math.sqrt(HEAD_DIM), 4, local_blocks),
        out_shape=(packed, packed),
        in_specs=[smem, smem] + [vmem] * 4,
        out_specs=(vmem, vmem),
        scratch_shapes=[
            pltpu.SMEM((my_list.shape[0] + 1,), jnp.int32),
            pltpu.VMEM((2 * rows, HEAD_DIM), bf16),
            pltpu.VMEM((2, 1, rows), f32),
            pltpu.VMEM((2, 1, rows), f32),
            pltpu.VMEM((2, HEAD_DIM, rows), f32),
        ],
        compiler_params=pltpu.CompilerParams(vmem_limit_bytes=20 * 1024 * 1024),
        cost_estimate=pl.CostEstimate(
            flops=4 * 2 * rows * 40 * BLK * HEAD_DIM,
            bytes_accessed=2 * keys.size * 2,
            transcendentals=2 * rows * 40 * BLK,
        ),
    )(my_list, place, own_q, other_q, keys, values)


def merge_kernel(own_ref, got_ref, out_ref):
    own_top = own_ref[HEAD_DIM : HEAD_DIM + 1, :]
    got_top = got_ref[HEAD_DIM : HEAD_DIM + 1, :]
    top = jnp.maximum(own_top, got_top)
    own_w = jnp.exp2(own_top - top)
    got_w = jnp.exp2(got_top - top)
    total = own_w * own_ref[HEAD_DIM + 1 : HEAD_DIM + 2, :] + got_w * got_ref[HEAD_DIM + 1 : HEAD_DIM + 2, :]
    mixed = (own_ref[0:HEAD_DIM, :] * own_w + got_ref[0:HEAD_DIM, :] * got_w) / total
    heads = mixed.shape[1] // BLK
    for h in range(heads):
        piece = mixed[:, h * BLK : (h + 1) * BLK].T.astype(bf16)
        for i in range(out_ref.shape[0]):
            out_ref[i, :, pl.ds(h * HEAD_DIM, HEAD_DIM)] = piece


def merge(own, got, copies):
    heads = own.shape[1] // BLK
    vmem = pl.BlockSpec(memory_space=pltpu.VMEM)
    return pl.pallas_call(
        merge_kernel,
        out_shape=jax.ShapeDtypeStruct((copies, BLK, heads * HEAD_DIM), bf16),
        in_specs=[vmem, vmem],
        out_specs=vmem,
        compiler_params=pltpu.CompilerParams(vmem_limit_bytes=12 * 1024 * 1024),
    )(own, got)


def product_kernel(tile, weight_count, pick_ref, x_ref, *refs):
    weight_refs, add_ref, out_ref = refs[:weight_count], refs[weight_count:-1], refs[-1]
    x = x_ref[:, pick_ref[0]] if x_ref.shape[1] > out_ref.shape[1] else x_ref[...]
    x = x.reshape(-1, x.shape[-1])
    width = weight_refs[0].shape[1]
    block = out_ref.shape[:-1] + (tile,)
    for i, weight_ref in enumerate(weight_refs):
        for first in range(0, width, tile):
            total = jnp.dot(x, weight_ref[:, first : first + tile], preferred_element_type=f32)
            columns = slice(i * width + first, i * width + first + tile)
            if add_ref:
                total = total + add_ref[0][..., columns].reshape(total.shape).astype(f32)
            out_ref[..., columns] = total.astype(bf16).reshape(block)


def product(x, weights, tile, pick=None, add=None):
    blocks, pair, tokens, inputs = x.shape
    taken = pair if pick is None else 1
    pick = jnp.zeros((1,), jnp.int32) if pick is None else pick.astype(jnp.int32).reshape(1)
    vmem = pl.BlockSpec(memory_space=pltpu.VMEM)
    operands = [x, *weights] if add is None else [x, *weights, add]
    rows = blocks * taken * tokens
    columns = weights[0].shape[1] * len(weights)
    return pl.pallas_call(
        functools.partial(product_kernel, tile, len(weights)),
        out_shape=jax.ShapeDtypeStruct((blocks, taken, tokens, columns), bf16),
        in_specs=[pl.BlockSpec(memory_space=pltpu.SMEM)] + [vmem] * len(operands),
        out_specs=vmem,
        compiler_params=pltpu.CompilerParams(vmem_limit_bytes=20 * 1024 * 1024),
        cost_estimate=pl.CostEstimate(
            flops=2 * rows * inputs * columns,
            bytes_accessed=2 * (rows * inputs + inputs * columns + rows * columns),
            transcendentals=0,
        ),
    )(pick, *operands)


VMEM = pl.BlockSpec(memory_space=pltpu.VMEM)
SMEM = pl.BlockSpec(memory_space=pltpu.SMEM)


def small_call(kernel, outs, scalars, arrays, moved):
    return pl.pallas_call(
        kernel,
        out_shape=outs,
        in_specs=[SMEM] * len(scalars) + [VMEM] * len(arrays),
        out_specs=jax.tree.map(lambda _: VMEM, outs),
        compiler_params=pltpu.CompilerParams(vmem_limit_bytes=16 * 1024 * 1024),
        cost_estimate=pl.CostEstimate(flops=moved, bytes_accessed=moved, transcendentals=0),
    )(*scalars, *arrays)


def spread_kernel(place_ref, mine_ref, theirs_ref, gate_ref, up_ref, *out_refs):
    y, side = place_ref[0], place_ref[1]
    give_ref, keep_ref, self_ref, right_ref, left_ref, opposite_ref, far_ref = out_refs
    order = [(y + i) % 4 for i in range(4)]
    sides = (side, 1 - side)
    n = mine_ref.shape[2]
    x = jnp.concatenate(
        [mine_ref[i, 1 - side] for i in order]
        + [theirs_ref[i, s] for i in order for s in sides]
        + [mine_ref[i, side] for i in order],
        axis=0,
    )
    step = pl.program_id(0)

    def put(weight_ref):
        total = jnp.dot(x, weight_ref[...], preferred_element_type=f32).astype(bf16)
        for i in range(4):
            give_ref[i] = total[i * n : (i + 1) * n]
            keep_ref[i] = total[(12 + i) * n : (13 + i) * n]
        for first, ref in ((4, self_ref), (6, right_ref), (10, left_ref)):
            for j in range(2):
                ref[j] = total[(first + j) * n : (first + j + 1) * n]
        opposite_ref[...] = total[8 * n : 9 * n]
        far_ref[...] = total[9 * n : 10 * n]

    half = pl.num_programs(0) // 2
    pl.when(step < half)(functools.partial(put, gate_ref))
    pl.when(step >= half)(functools.partial(put, up_ref))


def partial_columns(place, mine, theirs, gate, up):
    tile = 896
    inputs, width = gate.shape
    count = width // tile
    tokens = mine.shape[2]
    whole = pl.BlockSpec(mine.shape, lambda n, p: (0, 0, 0, 0))

    def out(*lead):
        block = pl.BlockSpec((*lead, tokens, tile), lambda n, p: (0,) * (len(lead) + 1) + (n,))
        return jax.ShapeDtypeStruct((*lead, tokens, 2 * width), bf16), block

    shapes, blocks = zip(*[out(4), out(4), out(2), out(2), out(2), out(), out()])
    rows = 16 * tokens
    return pl.pallas_call(
        spread_kernel,
        out_shape=shapes,
        grid_spec=pltpu.PrefetchScalarGridSpec(
            num_scalar_prefetch=1,
            grid=(2 * count,),
            in_specs=[
                whole,
                whole,
                pl.BlockSpec((inputs, tile), lambda n, p: (0, jnp.minimum(n, count - 1))),
                pl.BlockSpec((inputs, tile), lambda n, p: (0, jnp.maximum(n - count, 0))),
            ],
            out_specs=blocks,
        ),
        compiler_params=pltpu.CompilerParams(vmem_limit_bytes=40 * 1024 * 1024),
        cost_estimate=pl.CostEstimate(
            flops=4 * rows * inputs * width,
            bytes_accessed=2 * (rows * inputs + 2 * inputs * width + 2 * rows * width),
            transcendentals=0,
        ),
    )(place, mine, theirs, gate, up)


def arranged_sum(got, keep):
    tokens, width = keep.shape[1] // 2, keep.shape[2]

    def kernel(got_ref, keep_ref, self_ref, right_ref, left_ref, opposite_ref, far_ref):
        def block(i, j):
            rows = pl.ds(j * tokens, tokens)
            return (got_ref[i, rows].astype(f32) + keep_ref[i, rows].astype(f32)).astype(bf16)

        for i, ref in ((0, self_ref), (1, right_ref), (3, left_ref)):
            for j in range(2):
                ref[j] = block(i, j)
        opposite_ref[...] = block(2, 0)
        far_ref[...] = block(2, 1)

    two = jax.ShapeDtypeStruct((2, tokens, width), bf16)
    one = jax.ShapeDtypeStruct((tokens, width), bf16)
    return small_call(kernel, (two, two, two, one, one), (), (got, keep), 4 * keep.size)


def add_pieces(*pieces):
    def kernel(*refs):
        refs[-1][...] = sum(r[...].astype(f32) for r in refs[:-1]).astype(bf16)

    first = pieces[0]
    return small_call(kernel, jax.ShapeDtypeStruct(first.shape, bf16), (), pieces, 2 * first.size)


def gated(groups, factor):
    counts = [len(g) for g in groups]
    tokens, width = groups[0][0].shape[0], groups[0][0].shape[1] // 2

    def kernel(*refs):
        factor_ref, out_ref = refs[-2], refs[-1]
        at = 0
        for i, count in enumerate(counts):
            rows = pl.ds(i * tokens, tokens)
            mine = refs[at : at + count]
            at += count
            scale = factor_ref[rows, :]
            gate = sum(r[:, 0:width].astype(f32) for r in mine) * scale
            up = sum(r[:, width:].astype(f32) for r in mine) * scale
            out_ref[rows, :] = (gate / (1.0 + jnp.exp(-gate)) * up).astype(bf16)

    out = jax.ShapeDtypeStruct((tokens * len(groups), width), bf16)
    arrays = [p for g in groups for p in g] + [factor[:, None]]
    return small_call(kernel, out, (), arrays, 8 * tokens * width * len(groups))


def down_kernel(tile, place_ref, *refs):
    y, side = place_ref[0], place_ref[1]
    pieces, weight_ref, add_ref, out_ref = refs[:8], refs[8], refs[9:-1], refs[-1]
    n = pieces[0].shape[0]
    x = jnp.concatenate([p[...] for p in pieces], axis=0)
    total = jnp.dot(x, weight_ref[...], preferred_element_type=f32)
    for i in range(4):
        for j in range(2):
            at = 2 * ((y + i) % 4) + (side if j == 0 else 1 - side)
            part = total[(2 * i + j) * n : (2 * i + j + 1) * n]
            if add_ref:
                part = part + add_ref[0][at].astype(f32)
            out_ref[at] = part.astype(bf16)


def down_product(place, pieces, weight, add=None):
    tile = 256
    tokens, inputs = pieces[0].shape
    width = weight.shape[1]
    piece = pl.BlockSpec((tokens, inputs), lambda n, p: (0, 0))
    by_column = pl.BlockSpec((8, tokens, tile), lambda n, p: (0, 0, n))
    operands = [*pieces, weight] + ([] if add is None else [add])
    specs = [piece] * 8 + [pl.BlockSpec((inputs, tile), lambda n, p: (0, n))]
    specs += [] if add is None else [by_column]
    return pl.pallas_call(
        functools.partial(down_kernel, tile),
        out_shape=jax.ShapeDtypeStruct((8, tokens, width), bf16),
        grid_spec=pltpu.PrefetchScalarGridSpec(
            num_scalar_prefetch=1, grid=(width // tile,), in_specs=specs, out_specs=by_column
        ),
        compiler_params=pltpu.CompilerParams(vmem_limit_bytes=20 * 1024 * 1024),
        cost_estimate=pl.CostEstimate(
            flops=16 * tokens * inputs * width,
            bytes_accessed=2 * (8 * tokens * inputs + inputs * width + 8 * tokens * width),
            transcendentals=0,
        ),
    )(place, *operands)


def to_right(x):
    return lax.ppermute(x, "y", [(i, (i + 1) % 4) for i in range(4)])


def to_left(x):
    return lax.ppermute(x, "y", [(i, (i + 3) % 4) for i in range(4)])


def ring_sum(own, right, left, opposite, far):
    from_left = to_right(opposite)
    from_right = to_left(far)
    second_left = to_right(right[1])
    second_right = to_left(left[0])
    third_left = to_right(add_pieces(right[0], from_left))
    third_right = to_left(add_pieces(left[1], from_right))
    return (own[0], second_right, third_left), (own[1], second_left, third_right)


def ring_gather(mine, got):
    mine_left, mine_right = to_right(mine), to_left(mine)
    got_left, got_right = to_right(got), to_left(got)
    mine_far, got_far = to_right(mine_left), to_left(got_right)
    return mine, got, mine_right, got_right, mine_far, got_far, mine_left, got_left


def exchange(x, axes):
    return lax.all_to_all(x, axes, split_axis=0, concat_axis=0, tiled=True)


def swap(x, axis="core"):
    return lax.ppermute(x, axis, [(0, 1), (1, 0)])


def spread(x, copies):
    return jnp.broadcast_to(x[None], (copies,) + x.shape)


def take(x, index, axis):
    return lax.dynamic_index_in_dim(x, index, axis, keepdims=False)


def local(
    queries,
    cache_keys,
    cache_values,
    stretch_keys,
    stretch_values,
    block_lists,
    out_weight,
    residual,
    norm_gain,
    gate_weight,
    up_weight,
    down_weight,
):
    core = lax.axis_index("core")
    side = lax.axis_index("xl")
    col = lax.axis_index(COL)
    group = lax.axis_index(ZXH)
    me = lax.axis_index(ROW) * 8 + col
    local_blocks = cache_keys.shape[1] // BLK
    tokens_here = residual.shape[0]

    matched = block_lists // local_blocks == me
    within = jnp.sum(jnp.where(matched, block_lists % local_blocks, 0), axis=2)
    source = (jnp.arange(KV_HEADS, dtype=jnp.int32)[:, None] * local_blocks + within.T).reshape(-1)

    def fetch(cache, stretch):
        flat = cache.reshape(KV_HEADS * local_blocks, BLK, HEAD_DIM)
        part = BLK // 8
        near = lax.dynamic_slice_in_dim(stretch, group * part, part, 1)
        near = jnp.broadcast_to(near[:, None], (KV_HEADS, 8, part, HEAD_DIM)).reshape(64, part, HEAD_DIM)
        return exchange(jnp.concatenate([flat[source], near], axis=1), CHIP)

    keys = fetch(cache_keys, stretch_keys)
    values = fetch(cache_values, stretch_values)
    my_list = block_lists[col, group]
    place = jnp.stack([core, col]).astype(jnp.int32)
    other_queries = swap(queries)
    own, send = attend(my_list, place, queries, other_queries, keys, values, local_blocks)
    attended = exchange(merge(own, swap(send), 8), COL).reshape(8, 2, tokens_here, -1)

    def row_sum(give, mine, pick, weight):
        both = product(mine, (weight,), 512, pick, add=swap(give))
        return jnp.sum(exchange(both.reshape(8, tokens_here, -1), ZXH).astype(f32), axis=0)

    give = product(attended, (out_weight,), 512, 1 - core)
    stream = residual.astype(f32) + row_sum(give, attended, core, out_weight)
    gain = norm_gain.astype(f32)[None, :]
    scaled = (stream * gain).astype(bf16)
    own_rows = exchange(spread(scaled, 8), ZXH)
    other_rows = swap(own_rows)

    def squares(x):
        plain = x.astype(f32) / gain[None]
        return jnp.sum(plain * plain, axis=2)

    parts = jnp.stack([squares(own_rows), squares(other_rows)], axis=1)
    totals = jnp.sum(exchange(parts, COL), axis=0)
    factor = lax.rsqrt(totals.reshape(2, tokens_here) / D + 1e-05)

    by_pair = (4, 2, tokens_here, own_rows.shape[-1])
    where = jnp.stack([lax.axis_index("y"), side]).astype(jnp.int32)
    give, keep, *pieces = partial_columns(
        where, own_rows.reshape(by_pair), other_rows.reshape(by_pair), gate_weight, up_weight
    )
    got = swap(give, "xl")
    here, there = ring_sum(*pieces)
    other_give = add_pieces(*there)
    got, other_give = lax.optimization_barrier((got, other_give))
    own_here, own_there = ring_sum(*arranged_sum(got, keep))
    other_hidden = gated([(*here, swap(other_give, "xl"))], factor[1])
    other_all = ring_gather(other_hidden, swap(other_hidden, "xl"))
    own_hidden = gated([own_here, own_there], factor[0])
    own_all = ring_gather(own_hidden, swap(own_hidden, "xl"))
    given = down_product(where, other_all, down_weight)
    down = down_product(where, own_all, down_weight, add=swap(given))
    mlp = jnp.sum(exchange(down, ZXH).astype(f32), axis=0)
    return (stream + mlp).astype(bf16)


def solution(mesh):
    mesh = Mesh(mesh.devices.reshape(4, 2, 2, 4, 2), AXES)
    in_specs = (
        P(COL, ROW),
        P(None, ROW + COL, None),
        P(None, ROW + COL, None),
        P(None, COL, None),
        P(None, COL, None),
        P(),
        P(ROW, COL),
        P(ROW, COL),
        P(COL),
        P(COL, ROW),
        P(COL, ROW),
        P(ROW, COL),
    )
    return jax.shard_map(local, mesh=mesh, in_specs=in_specs, out_specs=P(ROW, COL), check_vma=False)
```

```python
import functools
import math

import jax
import jax.numpy as jnp
from jax import lax
from jax.experimental import pallas as pl
from jax.experimental.pallas import tpu as pltpu
from jax.sharding import Mesh, PartitionSpec as P

D = 8192
KV_HEADS = 8
HEAD_DIM = 128
BLK = 128
GROUP = 8
MOVED = 16
AXES = ("z", "xh", "core", "y", "xl")
ROW = ("z", "xh", "core")
ZXH = ("z", "xh")
COL = ("y", "xl")
CHIP = ("z", "xh", "y", "xl")
NEG = -1e30
bf16 = jnp.bfloat16
f32 = jnp.float32


def nt_dot(a, b):
    return lax.dot_general(a, b, (((1,), (1,)), ((), ())), preferred_element_type=f32)


def tn_dot(a, b):
    return lax.dot_general(a, b, (((0,), (0,)), ((), ())), preferred_element_type=f32)


def attend_kernel(scale, local_blocks, last, list_ref, place_ref, own_q_ref, other_q_ref, *refs):
    per_step = 8
    half_blk = BLK // 2
    if last:
        first_ref, chunk_ref, own_in_ref, send_in_ref = refs[:4]
    else:
        chunk_ref = refs[0]
    own_ref, send_ref, order_ref, q_ref, top_ref, sum_ref, acc_ref = refs[-7:]
    core = place_ref[0]
    block = place_ref[1]
    length = list_ref.shape[0]
    heads = own_q_ref.shape[1] // HEAD_DIM
    rows = heads * BLK
    for h in range(heads):
        cols = pl.ds(h * HEAD_DIM, HEAD_DIM)
        q_ref[pl.ds(h * BLK, BLK), :] = own_q_ref[:, cols]
        q_ref[pl.ds(rows + h * BLK, BLK), :] = other_q_ref[:, cols]
    if last:
        for half, ref in ((0, own_in_ref), (1, send_in_ref)):
            acc_ref[half] = ref[0:HEAD_DIM, :]
            top_ref[half] = ref[HEAD_DIM : HEAD_DIM + 1, :]
            sum_ref[half] = ref[HEAD_DIM + 1 : HEAD_DIM + 2, :]
    else:
        top_ref[...] = jnp.full_like(top_ref, NEG)
        sum_ref[...] = jnp.zeros_like(sum_ref)
        acc_ref[...] = jnp.zeros_like(acc_ref)

    def collect(i, count):
        device = list_ref[i] // local_blocks
        row = device // 8
        order_ref[count] = (row // 2) * 8 + device % 8
        return count + jnp.where(row % 2 == core, 1, 0)

    count = lax.fori_loop(0, length, collect, jnp.int32(0))

    def update(half, keys, values, bias):
        part = pl.ds(half * rows, rows)
        scores = nt_dot(keys, q_ref[part, :]) * scale + bias
        old = top_ref[half]
        new = jnp.maximum(old, jnp.max(scores, axis=0, keepdims=True))
        weights = jnp.exp2(scores - new)
        decay = jnp.exp2(old - new)
        top_ref[half] = new
        sum_ref[half] = sum_ref[half] * decay + jnp.sum(weights, axis=0, keepdims=True)
        acc_ref[half] = acc_ref[half] * decay + tn_dot(values, weights.astype(bf16))

    def far(step, carry):
        slots = [order_ref[jnp.minimum(step * per_step + i, count - 1)] for i in range(per_step)]
        keys = jnp.concatenate([chunk_ref[s, 0:half_blk] for s in slots], axis=0)
        values = jnp.concatenate([chunk_ref[s, half_blk : 2 * half_blk] for s in slots], axis=0)
        bias = jnp.concatenate(
            [
                jnp.full((half_blk, 1), jnp.where(step * per_step + i < count, 0.0, NEG), f32)
                for i in range(per_step)
            ],
            axis=0,
        )
        for half in range(2):
            update(half, keys, values, bias)
        return carry

    lax.fori_loop(0, (count + per_step - 1) // per_step, far, 0)

    def near(j, carry):
        which = core + 2 * j
        shift = (block - which) * BLK
        key_pos = lax.broadcasted_iota(jnp.int32, (BLK, rows), 0)
        token = lax.broadcasted_iota(jnp.int32, (BLK, rows), 1) % BLK
        bias = jnp.where(key_pos <= token + shift, 0.0, NEG)
        keys = jnp.concatenate([first_ref[i * 8 + which, BLK:] for i in range(8)], axis=0)
        values = jnp.concatenate([chunk_ref[i * 8 + which, BLK:] for i in range(8)], axis=0)
        for half in range(2):
            update(half, keys, values, bias)
        return carry

    if last:
        lax.fori_loop(0, (block - core + 2) // 2, near, 0)
    for half, ref in ((0, own_ref), (1, send_ref)):
        ref[0:HEAD_DIM, :] = acc_ref[half]
        ref[HEAD_DIM : HEAD_DIM + 1, :] = top_ref[half]
        ref[HEAD_DIM + 1 : HEAD_DIM + 2, :] = sum_ref[half]


def attend(my_list, place, own_q, other_q, chunks, state, local_blocks):
    heads = own_q.shape[1] // HEAD_DIM
    rows = heads * BLK
    packed = jax.ShapeDtypeStruct((HEAD_DIM + 8, rows), f32)
    smem = pl.BlockSpec(memory_space=pltpu.SMEM)
    vmem = pl.BlockSpec(memory_space=pltpu.VMEM)
    scale = math.log2(math.e) / math.sqrt(HEAD_DIM)
    arrays = [own_q, other_q, *chunks, *state]
    return pl.pallas_call(
        functools.partial(attend_kernel, scale, local_blocks, len(state) > 0),
        out_shape=(packed, packed),
        in_specs=[smem, smem] + [vmem] * len(arrays),
        out_specs=(vmem, vmem),
        scratch_shapes=[
            pltpu.SMEM((my_list.shape[0] + 1,), jnp.int32),
            pltpu.VMEM((2 * rows, HEAD_DIM), bf16),
            pltpu.VMEM((2, 1, rows), f32),
            pltpu.VMEM((2, 1, rows), f32),
            pltpu.VMEM((2, HEAD_DIM, rows), f32),
        ],
        compiler_params=pltpu.CompilerParams(vmem_limit_bytes=24 * 1024 * 1024),
        cost_estimate=pl.CostEstimate(
            flops=4 * 2 * rows * 20 * BLK * HEAD_DIM,
            bytes_accessed=2 * chunks[-1].size * 2,
            transcendentals=2 * rows * 20 * BLK,
        ),
    )(my_list, place, *arrays)


def merge_kernel(own_ref, got_ref, out_ref):
    own_top = own_ref[HEAD_DIM : HEAD_DIM + 1, :]
    got_top = got_ref[HEAD_DIM : HEAD_DIM + 1, :]
    top = jnp.maximum(own_top, got_top)
    own_w = jnp.exp2(own_top - top)
    got_w = jnp.exp2(got_top - top)
    total = own_w * own_ref[HEAD_DIM + 1 : HEAD_DIM + 2, :] + got_w * got_ref[HEAD_DIM + 1 : HEAD_DIM + 2, :]
    mixed = (own_ref[0:HEAD_DIM, :] * own_w + got_ref[0:HEAD_DIM, :] * got_w) / total
    heads = mixed.shape[1] // BLK
    for h in range(heads):
        piece = mixed[:, h * BLK : (h + 1) * BLK].T.astype(bf16)
        for i in range(out_ref.shape[0]):
            out_ref[i, :, pl.ds(h * HEAD_DIM, HEAD_DIM)] = piece


def merge(own, got, copies):
    heads = own.shape[1] // BLK
    vmem = pl.BlockSpec(memory_space=pltpu.VMEM)
    return pl.pallas_call(
        merge_kernel,
        out_shape=jax.ShapeDtypeStruct((copies, BLK, heads * HEAD_DIM), bf16),
        in_specs=[vmem, vmem],
        out_specs=vmem,
        compiler_params=pltpu.CompilerParams(vmem_limit_bytes=12 * 1024 * 1024),
    )(own, got)


def product_kernel(tile, weight_count, pick_ref, x_ref, *refs):
    weight_refs, add_ref, out_ref = refs[:weight_count], refs[weight_count:-1], refs[-1]
    x = x_ref[:, pick_ref[0]] if x_ref.shape[1] > out_ref.shape[1] else x_ref[...]
    x = x.reshape(-1, x.shape[-1])
    width = weight_refs[0].shape[1]
    block = out_ref.shape[:-1] + (tile,)
    for i, weight_ref in enumerate(weight_refs):
        for first in range(0, width, tile):
            total = jnp.dot(x, weight_ref[:, first : first + tile], preferred_element_type=f32)
            columns = slice(i * width + first, i * width + first + tile)
            if add_ref:
                total = total + add_ref[0][..., columns].reshape(total.shape).astype(f32)
            out_ref[..., columns] = total.astype(bf16).reshape(block)


def product(x, weights, tile, pick=None, add=None):
    blocks, pair, tokens, inputs = x.shape
    taken = pair if pick is None else 1
    pick = jnp.zeros((1,), jnp.int32) if pick is None else pick.astype(jnp.int32).reshape(1)
    vmem = pl.BlockSpec(memory_space=pltpu.VMEM)
    operands = [x, *weights] if add is None else [x, *weights, add]
    rows = blocks * taken * tokens
    columns = weights[0].shape[1] * len(weights)
    return pl.pallas_call(
        functools.partial(product_kernel, tile, len(weights)),
        out_shape=jax.ShapeDtypeStruct((blocks, taken, tokens, columns), bf16),
        in_specs=[pl.BlockSpec(memory_space=pltpu.SMEM)] + [vmem] * len(operands),
        out_specs=vmem,
        compiler_params=pltpu.CompilerParams(vmem_limit_bytes=20 * 1024 * 1024),
        cost_estimate=pl.CostEstimate(
            flops=2 * rows * inputs * columns,
            bytes_accessed=2 * (rows * inputs + inputs * columns + rows * columns),
            transcendentals=0,
        ),
    )(pick, *operands)


VMEM = pl.BlockSpec(memory_space=pltpu.VMEM)
SMEM = pl.BlockSpec(memory_space=pltpu.SMEM)


def small_call(kernel, outs, scalars, arrays, moved):
    return pl.pallas_call(
        kernel,
        out_shape=outs,
        in_specs=[SMEM] * len(scalars) + [VMEM] * len(arrays),
        out_specs=jax.tree.map(lambda _: VMEM, outs),
        compiler_params=pltpu.CompilerParams(vmem_limit_bytes=16 * 1024 * 1024),
        cost_estimate=pl.CostEstimate(flops=moved, bytes_accessed=moved, transcendentals=0),
    )(*scalars, *arrays)


def spread_kernel(place_ref, mine_ref, theirs_ref, gain_ref, gate_ref, up_ref, *out_refs):
    y, side = place_ref[0], place_ref[1]
    give_ref, keep_ref, self_ref, right_ref, left_ref, opposite_ref, far_ref, squares_ref = out_refs
    order = [(y + i) % 4 for i in range(4)]
    sides = (side, 1 - side)
    n = mine_ref.shape[2]
    kept = n - MOVED
    joint = n + MOVED
    rows = [mine_ref[i, 1 - side, MOVED:] for i in order]
    for i in order:
        for s in sides:
            rows += [theirs_ref[i, s], mine_ref[i, s, :MOVED]]
    rows += [mine_ref[i, side, MOVED:] for i in order]
    x = jnp.concatenate(rows, axis=0)
    base = 4 * kept
    end = base + 8 * joint
    step = pl.program_id(0)

    @pl.when(step == pl.num_programs(0) - 1)
    def _():
        ones = jnp.ones((8, x.shape[1]), f32)
        plain = x.astype(f32) / gain_ref[...]
        sums = lax.dot_general(
            ones, plain * plain, (((1,), (1,)), ((), ())),
            precision=lax.Precision.HIGHEST, preferred_element_type=f32,
        )
        for i in range(4):
            for j, (first, k) in enumerate(((0, 1), (end, 0))):
                at = base + (2 * i + k) * joint
                squares_ref[j, i, :, 0:joint] = sums[:, at : at + joint]
                squares_ref[j, i, :, joint:] = sums[:, first + i * kept : first + (i + 1) * kept]

    def put(weight_ref):
        total = jnp.dot(x, weight_ref[...], preferred_element_type=f32).astype(bf16)
        for i in range(4):
            give_ref[i] = total[i * kept : (i + 1) * kept]
            keep_ref[i] = total[end + i * kept : end + (i + 1) * kept]
        for first, ref in ((0, self_ref), (2, right_ref), (6, left_ref)):
            for j in range(2):
                at = base + (first + j) * joint
                ref[j] = total[at : at + joint]
        opposite_ref[...] = total[base + 4 * joint : base + 5 * joint]
        far_ref[...] = total[base + 5 * joint : base + 6 * joint]

    half = pl.num_programs(0) // 2
    pl.when(step < half)(functools.partial(put, gate_ref))
    pl.when(step >= half)(functools.partial(put, up_ref))


def partial_columns(place, mine, theirs, gain, gate, up):
    tile = 896
    inputs, width = gate.shape
    count = width // tile
    tokens = mine.shape[2]
    whole = pl.BlockSpec(mine.shape, lambda n, p: (0, 0, 0, 0))

    def out(*lead):
        block = pl.BlockSpec((*lead, tile), lambda n, p: (0,) * len(lead) + (n,))
        return jax.ShapeDtypeStruct((*lead, 2 * width), bf16), block

    kept, joint = tokens - MOVED, tokens + MOVED
    shapes, blocks = zip(*[out(4, kept)] * 2, *[out(2, joint)] * 3, *[out(joint)] * 2)
    shapes += (jax.ShapeDtypeStruct((2, 4, 8, 2 * tokens), f32),)
    blocks += (pl.BlockSpec((2, 4, 8, 2 * tokens), lambda n, p: (0, 0, 0, 0)),)
    rows = 16 * tokens
    return pl.pallas_call(
        spread_kernel,
        out_shape=shapes,
        grid_spec=pltpu.PrefetchScalarGridSpec(
            num_scalar_prefetch=1,
            grid=(2 * count,),
            in_specs=[
                whole,
                whole,
                pl.BlockSpec((1, inputs), lambda n, p: (0, 0)),
                pl.BlockSpec((inputs, tile), lambda n, p: (0, jnp.minimum(n, count - 1))),
                pl.BlockSpec((inputs, tile), lambda n, p: (0, jnp.maximum(n - count, 0))),
            ],
            out_specs=blocks,
        ),
        compiler_params=pltpu.CompilerParams(vmem_limit_bytes=40 * 1024 * 1024),
        cost_estimate=pl.CostEstimate(
            flops=4 * rows * inputs * width,
            bytes_accessed=2 * (rows * inputs + 2 * inputs * width + 2 * rows * width),
            transcendentals=0,
        ),
    )(place, mine, theirs, gain, gate, up)


def arranged_sum(got, keep):
    tokens, width = keep.shape[1], keep.shape[2] // 2

    def kernel(got_ref, keep_ref, self_ref, right_ref, left_ref, opposite_ref, far_ref):
        def block(i, j):
            columns = pl.ds(j * width, width)
            return (got_ref[i, :, columns].astype(f32) + keep_ref[i, :, columns].astype(f32)).astype(bf16)

        for i, ref in ((0, self_ref), (1, right_ref), (3, left_ref)):
            for j in range(2):
                ref[j] = block(i, j)
        opposite_ref[...] = block(2, 0)
        far_ref[...] = block(2, 1)

    two = jax.ShapeDtypeStruct((2, tokens, width), bf16)
    one = jax.ShapeDtypeStruct((tokens, width), bf16)
    return small_call(kernel, (two, two, two, one, one), (), (got, keep), 4 * keep.size)


def add_pieces(*pieces):
    def kernel(*refs):
        refs[-1][...] = sum(r[...].astype(f32) for r in refs[:-1]).astype(bf16)

    first = pieces[0]
    return small_call(kernel, jax.ShapeDtypeStruct(first.shape, bf16), (), pieces, 2 * first.size)


def gated(gates, ups, factor):
    pieces = list(gates) + ([] if ups is None else list(ups))
    tokens = pieces[0].shape[0]
    width = pieces[0].shape[1] // (2 if ups is None else 1)

    def kernel(*refs):
        scale = refs[-2][...]
        if ups is None:
            gate = sum(r[:, 0:width].astype(f32) for r in refs[:-2]) * scale
            up = sum(r[:, width:].astype(f32) for r in refs[:-2]) * scale
        else:
            gate = sum(r[...].astype(f32) for r in refs[: len(gates)]) * scale
            up = sum(r[...].astype(f32) for r in refs[len(gates) : -2]) * scale
        refs[-1][...] = (gate / (1.0 + jnp.exp(-gate)) * up).astype(bf16)

    out = jax.ShapeDtypeStruct((tokens, width), bf16)
    return small_call(kernel, out, (), [*pieces, factor[:, None]], 8 * tokens * width)


def down_product(place, pieces, weight, rest=()):
    tile = 256
    n, inputs = pieces[0].shape
    width = weight.shape[1]
    tokens = n - MOVED if not rest else n + MOVED

    def kernel(place_ref, *refs):
        y, side = place_ref[0], place_ref[1]
        x = jnp.concatenate([p[...] for p in refs[:8]], axis=0)
        total = jnp.dot(x, refs[8][...], preferred_element_type=f32)
        for i in range(4):
            for j in range(2):
                at = 2 * ((y + i) % 4) + (side if j == 0 else 1 - side)
                part = total[(2 * i + j) * n : (2 * i + j + 1) * n]
                if rest:
                    before_ref, add_ref, out_ref = refs[9:]
                    add = add_ref[at].astype(f32)
                    out_ref[at, :MOVED] = (before_ref[at] + add[:MOVED]).astype(bf16)
                    out_ref[at, MOVED:] = (part + add[MOVED:]).astype(bf16)
                else:
                    give_ref, first_ref = refs[9:]
                    give_ref[at] = part[:tokens].astype(bf16)
                    first_ref[at] = part[tokens:]

    def by_column(rows):
        return pl.BlockSpec((8, rows, tile), lambda c, p: (0, 0, c))

    specs = [pl.BlockSpec((n, inputs), lambda c, p: (0, 0))] * 8
    specs += [pl.BlockSpec((inputs, tile), lambda c, p: (0, c))]
    specs += [by_column(MOVED), by_column(tokens)] if rest else []
    whole = jax.ShapeDtypeStruct((8, tokens, width), bf16)
    first = jax.ShapeDtypeStruct((8, MOVED, width), f32)
    return pl.pallas_call(
        kernel,
        out_shape=whole if rest else (whole, first),
        grid_spec=pltpu.PrefetchScalarGridSpec(
            num_scalar_prefetch=1,
            grid=(width // tile,),
            in_specs=specs,
            out_specs=by_column(tokens) if rest else (by_column(tokens), by_column(MOVED)),
        ),
        compiler_params=pltpu.CompilerParams(vmem_limit_bytes=20 * 1024 * 1024),
        cost_estimate=pl.CostEstimate(
            flops=16 * n * inputs * width,
            bytes_accessed=2 * (8 * n * inputs + inputs * width + 8 * n * width),
            transcendentals=0,
        ),
    )(place, *pieces, weight, *rest)


def to_right(x):
    return lax.ppermute(x, "y", [(i, (i + 1) % 4) for i in range(4)])


def to_left(x):
    return lax.ppermute(x, "y", [(i, (i + 3) % 4) for i in range(4)])


def ring_start(pieces):
    _, right, left, opposite, far = pieces
    return to_right(opposite), to_left(far), to_right(right[1]), to_left(left[0])


def ring_middle(pieces, from_left, from_right):
    return add_pieces(pieces[1][0], from_left), add_pieces(pieces[2][1], from_right)


def ring_end(pieces, arrived, sums):
    third_left, third_right = to_right(sums[0]), to_left(sums[1])
    own = pieces[0]
    return (own[0], arrived[3], third_left), (own[1], arrived[2], third_right)


def ring_gather(mine, got):
    mine_left, mine_right = to_right(mine), to_left(mine)
    got_left, got_right = to_right(got), to_left(got)
    mine_far, got_far = to_right(mine_left), to_left(got_right)
    return mine, got, mine_right, got_right, mine_far, got_far, mine_left, got_left


def exchange(x, axes):
    return lax.all_to_all(x, axes, split_axis=0, concat_axis=0, tiled=True)


def swap(x, axis="core"):
    return lax.ppermute(x, axis, [(0, 1), (1, 0)])


def spread(x, copies):
    return jnp.broadcast_to(x[None], (copies,) + x.shape)


def take(x, index, axis):
    return lax.dynamic_index_in_dim(x, index, axis, keepdims=False)


def local(
    queries,
    cache_keys,
    cache_values,
    stretch_keys,
    stretch_values,
    block_lists,
    out_weight,
    residual,
    norm_gain,
    gate_weight,
    up_weight,
    down_weight,
):
    core = lax.axis_index("core")
    side = lax.axis_index("xl")
    col = lax.axis_index(COL)
    group = lax.axis_index(ZXH)
    me = lax.axis_index(ROW) * 8 + col
    local_blocks = cache_keys.shape[1] // BLK
    tokens_here = residual.shape[0]

    matched = block_lists // local_blocks == me
    within = jnp.sum(jnp.where(matched, block_lists % local_blocks, 0), axis=2)
    source = (jnp.arange(KV_HEADS, dtype=jnp.int32)[:, None] * local_blocks + within.T).reshape(-1)

    flat_keys = cache_keys.reshape(2 * KV_HEADS * local_blocks, BLK // 2, HEAD_DIM)
    flat_values = cache_values.reshape(2 * KV_HEADS * local_blocks, BLK // 2, HEAD_DIM)

    def fetch(half, stretch):
        part = BLK // 8
        near = lax.dynamic_slice_in_dim(stretch, group * part, part, 1)
        near = jnp.broadcast_to(near[:, None], (KV_HEADS, 8, part, HEAD_DIM)).reshape(64, part, HEAD_DIM)
        picked = 2 * source + half
        return exchange(jnp.concatenate([flat_keys[picked], flat_values[picked], near], axis=1), CHIP)

    first = fetch(0, stretch_keys)
    second = fetch(1, stretch_values)
    my_list = block_lists[col, group]
    place = jnp.stack([core, col]).astype(jnp.int32)
    other_queries = swap(queries)
    state = attend(my_list, place, queries, other_queries, (first,), (), local_blocks)
    own, send = attend(my_list, place, queries, other_queries, (first, second), state, local_blocks)
    attended = exchange(merge(own, swap(send), 8), COL).reshape(8, 2, tokens_here, -1)

    def row_sum(give, mine, pick, weight):
        both = product(mine, (weight,), 512, pick, add=swap(give))
        return jnp.sum(exchange(both.reshape(8, tokens_here, -1), ZXH).astype(f32), axis=0)

    give = product(attended, (out_weight,), 512, 1 - core)
    stream = residual.astype(f32) + row_sum(give, attended, core, out_weight)
    gain = norm_gain.astype(f32)[None, :]
    scaled = (stream * gain).astype(bf16)
    own_rows = exchange(spread(scaled, 8), ZXH)
    other_rows = swap(own_rows)

    by_pair = (4, 2, tokens_here, own_rows.shape[-1])
    where = jnp.stack([lax.axis_index("y"), side]).astype(jnp.int32)
    give, keep, *pieces, squares = partial_columns(
        where, own_rows.reshape(by_pair), other_rows.reshape(by_pair), gain, gate_weight, up_weight
    )
    got = swap(give, "xl")
    arrived = ring_start(pieces)
    here, there = ring_end(pieces, arrived, ring_middle(pieces, *arrived[:2]))
    squares = squares[1] + swap(squares[0], "xl")
    across = lax.ppermute(squares[2], "y", [(i, (i + 2) % 4) for i in range(4)])
    totals = squares[0] + across + to_right(squares[1]) + to_left(squares[3])
    factor = lax.rsqrt(totals[0] / D + 1e-05)
    joint = tokens_here + MOVED
    other_give = add_pieces(*there)
    got, other_give, factor = lax.optimization_barrier((got, other_give, factor))
    pieces = arranged_sum(got, keep)
    arrived = ring_start(pieces)
    near_sums, other_got = lax.optimization_barrier((arrived[:2], swap(other_give, "xl")))
    sums = ring_middle(pieces, *near_sums)
    other_hidden = gated((*here, other_got), None, factor[:joint])
    other_pair = (other_hidden, swap(other_hidden, "xl"))
    gates, ups, other_pair = lax.optimization_barrier((*ring_end(pieces, arrived, sums), other_pair))
    own_hidden = gated(gates, ups, factor[joint:])
    other_all = ring_gather(*other_pair)
    own_all = ring_gather(own_hidden, swap(own_hidden, "xl"))
    given, before = down_product(where, other_all, down_weight)
    down = down_product(where, own_all, down_weight, (before, swap(given)))
    mlp = jnp.sum(exchange(down, ZXH).astype(f32), axis=0)
    return (stream + mlp).astype(bf16)


def solution(mesh):
    mesh = Mesh(mesh.devices.reshape(4, 2, 2, 4, 2), AXES)
    in_specs = (
        P(COL, ROW),
        P(None, ROW + COL, None),
        P(None, ROW + COL, None),
        P(None, COL, None),
        P(None, COL, None),
        P(),
        P(ROW, COL),
        P(ROW, COL),
        P(COL),
        P(COL, ROW),
        P(COL, ROW),
        P(ROW, COL),
    )
    return jax.shard_map(local, mesh=mesh, in_specs=in_specs, out_specs=P(ROW, COL), check_vma=False)
```

```python
import functools
import math

import jax
import jax.numpy as jnp
from jax import lax
from jax.experimental import pallas as pl
from jax.experimental.pallas import tpu as pltpu
from jax.sharding import Mesh, PartitionSpec as P

D = 8192
KV_HEADS = 8
HEAD_DIM = 128
BLK = 128
GROUP = 8
AXES = ("z", "xh", "core", "y", "xl")
ROW = ("z", "xh", "core")
ZXH = ("z", "xh")
COL = ("y", "xl")
CHIP = ("z", "xh", "y", "xl")
NEG = -1e30
bf16 = jnp.bfloat16
f32 = jnp.float32


def nt_dot(a, b):
    return lax.dot_general(a, b, (((1,), (1,)), ((), ())), preferred_element_type=f32)


def tn_dot(a, b):
    return lax.dot_general(a, b, (((0,), (0,)), ((), ())), preferred_element_type=f32)


def attend_kernel(scale, per_step, local_blocks, last, *refs):
    if last:
        order_ref, own_q_ref, other_q_ref, chunk_ref, own_in_ref, send_in_ref = refs[:6]
    else:
        list_ref, place_ref, own_q_ref, other_q_ref, chunk_ref = refs[:5]
        order_ref = refs[7]
    own_ref, send_ref = refs[6:8] if last else refs[5:7]
    q_ref, top_ref, sum_ref, acc_ref = refs[-4:]
    length = order_ref.shape[0] - 1
    part_rows = (chunk_ref.shape[1] - (0 if last else BLK // 4)) // 2
    heads = own_q_ref.shape[1] // HEAD_DIM
    rows = heads * BLK
    for h in range(heads):
        cols = pl.ds(h * HEAD_DIM, HEAD_DIM)
        q_ref[pl.ds(h * BLK, BLK), :] = own_q_ref[:, cols]
        q_ref[pl.ds(rows + h * BLK, BLK), :] = other_q_ref[:, cols]
    if last:
        for half, ref in ((0, own_in_ref), (1, send_in_ref)):
            acc_ref[half] = ref[0:HEAD_DIM, :]
            top_ref[half] = ref[HEAD_DIM : HEAD_DIM + 1, :]
            sum_ref[half] = ref[HEAD_DIM + 1 : HEAD_DIM + 2, :]
        count = order_ref[length]
    else:
        core = place_ref[0]
        block = place_ref[1]
        top_ref[...] = jnp.full_like(top_ref, NEG)
        sum_ref[...] = jnp.zeros_like(sum_ref)
        acc_ref[...] = jnp.zeros_like(acc_ref)

        def collect(i, count):
            device = list_ref[i] // local_blocks
            row = device // 8
            order_ref[count] = (row // 2) * 8 + device % 8
            return count + jnp.where(row % 2 == core, 1, 0)

        count = lax.fori_loop(0, length, collect, jnp.int32(0))
        order_ref[length] = count

    def update(half, keys, values, bias):
        part = pl.ds(half * rows, rows)
        scores = nt_dot(keys, q_ref[part, :]) * scale + bias
        old = top_ref[half]
        new = jnp.maximum(old, jnp.max(scores, axis=0, keepdims=True))
        weights = jnp.exp2(scores - new)
        decay = jnp.exp2(old - new)
        top_ref[half] = new
        sum_ref[half] = sum_ref[half] * decay + jnp.sum(weights, axis=0, keepdims=True)
        acc_ref[half] = acc_ref[half] * decay + tn_dot(values, weights.astype(bf16))

    def far(step, carry):
        slots = [order_ref[jnp.minimum(step * per_step + i, count - 1)] for i in range(per_step)]
        keys = jnp.concatenate([chunk_ref[s, 0:part_rows] for s in slots], axis=0)
        values = jnp.concatenate([chunk_ref[s, part_rows : 2 * part_rows] for s in slots], axis=0)
        bias = jnp.concatenate(
            [
                jnp.full((part_rows, 1), jnp.where(step * per_step + i < count, 0.0, NEG), f32)
                for i in range(per_step)
            ],
            axis=0,
        )
        for half in range(2):
            update(half, keys, values, bias)
        return carry

    lax.fori_loop(0, (count + per_step - 1) // per_step, far, 0)

    def near(j, carry):
        which = core + 2 * j
        shift = (block - which) * BLK
        key_pos = lax.broadcasted_iota(jnp.int32, (BLK, rows), 0)
        token = lax.broadcasted_iota(jnp.int32, (BLK, rows), 1) % BLK
        bias = jnp.where(key_pos <= token + shift, 0.0, NEG)
        at = 2 * part_rows
        eighth = BLK // 8
        keys = jnp.concatenate([chunk_ref[i * 8 + which, at : at + eighth] for i in range(8)], axis=0)
        values = jnp.concatenate([chunk_ref[i * 8 + which, at + eighth :] for i in range(8)], axis=0)
        for half in range(2):
            update(half, keys, values, bias)
        return carry

    if not last:
        lax.fori_loop(0, (block - core + 2) // 2, near, 0)
    for half, ref in ((0, own_ref), (1, send_ref)):
        ref[0:HEAD_DIM, :] = acc_ref[half]
        ref[HEAD_DIM : HEAD_DIM + 1, :] = top_ref[half]
        ref[HEAD_DIM + 1 : HEAD_DIM + 2, :] = sum_ref[half]


def attend(scalars, own_q, other_q, chunk, state, local_blocks, per_step):
    heads = own_q.shape[1] // HEAD_DIM
    rows = heads * BLK
    length = scalars[0].shape[0] - len(state) // 2
    packed = jax.ShapeDtypeStruct((HEAD_DIM + 8, rows), f32)
    smem = pl.BlockSpec(memory_space=pltpu.SMEM)
    vmem = pl.BlockSpec(memory_space=pltpu.VMEM)
    scale = math.log2(math.e) / math.sqrt(HEAD_DIM)
    arrays = [own_q, other_q, chunk, *state]
    outs = [packed, packed]
    if not state:
        outs.append(jax.ShapeDtypeStruct((length + 1,), jnp.int32))
    return pl.pallas_call(
        functools.partial(attend_kernel, scale, per_step, local_blocks, len(state) > 0),
        out_shape=outs,
        in_specs=[smem] * len(scalars) + [vmem] * len(arrays),
        out_specs=[vmem, vmem, smem][: len(outs)],
        scratch_shapes=[
            pltpu.VMEM((2 * rows, HEAD_DIM), bf16),
            pltpu.VMEM((2, 1, rows), f32),
            pltpu.VMEM((2, 1, rows), f32),
            pltpu.VMEM((2, HEAD_DIM, rows), f32),
        ],
        compiler_params=pltpu.CompilerParams(vmem_limit_bytes=24 * 1024 * 1024),
        cost_estimate=pl.CostEstimate(
            flops=2 * rows * 40 * chunk.shape[1] * HEAD_DIM,
            bytes_accessed=2 * chunk.size,
            transcendentals=rows * 40 * chunk.shape[1],
        ),
    )(*scalars, *arrays)


def merge_kernel(own_ref, got_ref, out_ref):
    own_top = own_ref[HEAD_DIM : HEAD_DIM + 1, :]
    got_top = got_ref[HEAD_DIM : HEAD_DIM + 1, :]
    top = jnp.maximum(own_top, got_top)
    own_w = jnp.exp2(own_top - top)
    got_w = jnp.exp2(got_top - top)
    total = own_w * own_ref[HEAD_DIM + 1 : HEAD_DIM + 2, :] + got_w * got_ref[HEAD_DIM + 1 : HEAD_DIM + 2, :]
    mixed = (own_ref[0:HEAD_DIM, :] * own_w + got_ref[0:HEAD_DIM, :] * got_w) / total
    heads = mixed.shape[1] // BLK
    for h in range(heads):
        piece = mixed[:, h * BLK : (h + 1) * BLK].T.astype(bf16)
        for i in range(out_ref.shape[0]):
            out_ref[i, :, pl.ds(h * HEAD_DIM, HEAD_DIM)] = piece


def merge(own, got, copies):
    heads = own.shape[1] // BLK
    vmem = pl.BlockSpec(memory_space=pltpu.VMEM)
    return pl.pallas_call(
        merge_kernel,
        out_shape=jax.ShapeDtypeStruct((copies, BLK, heads * HEAD_DIM), bf16),
        in_specs=[vmem, vmem],
        out_specs=vmem,
        compiler_params=pltpu.CompilerParams(vmem_limit_bytes=12 * 1024 * 1024),
    )(own, got)


def product_kernel(tile, weight_count, pick_ref, x_ref, *refs):
    weight_refs, add_ref, out_ref = refs[:weight_count], refs[weight_count:-1], refs[-1]
    x = x_ref[:, pick_ref[0]] if x_ref.shape[1] > out_ref.shape[1] else x_ref[...]
    x = x.reshape(-1, x.shape[-1])
    width = weight_refs[0].shape[1]
    block = out_ref.shape[:-1] + (tile,)
    for i, weight_ref in enumerate(weight_refs):
        for first in range(0, width, tile):
            total = jnp.dot(x, weight_ref[:, first : first + tile], preferred_element_type=f32)
            columns = slice(i * width + first, i * width + first + tile)
            if add_ref:
                total = total + add_ref[0][..., columns].reshape(total.shape).astype(f32)
            out_ref[..., columns] = total.astype(bf16).reshape(block)


def product(x, weights, tile, pick=None, add=None):
    blocks, pair, tokens, inputs = x.shape
    taken = pair if pick is None else 1
    pick = jnp.zeros((1,), jnp.int32) if pick is None else pick.astype(jnp.int32).reshape(1)
    vmem = pl.BlockSpec(memory_space=pltpu.VMEM)
    operands = [x, *weights] if add is None else [x, *weights, add]
    rows = blocks * taken * tokens
    columns = weights[0].shape[1] * len(weights)
    return pl.pallas_call(
        functools.partial(product_kernel, tile, len(weights)),
        out_shape=jax.ShapeDtypeStruct((blocks, taken, tokens, columns), bf16),
        in_specs=[pl.BlockSpec(memory_space=pltpu.SMEM)] + [vmem] * len(operands),
        out_specs=vmem,
        compiler_params=pltpu.CompilerParams(vmem_limit_bytes=20 * 1024 * 1024),
        cost_estimate=pl.CostEstimate(
            flops=2 * rows * inputs * columns,
            bytes_accessed=2 * (rows * inputs + inputs * columns + rows * columns),
            transcendentals=0,
        ),
    )(pick, *operands)


VMEM = pl.BlockSpec(memory_space=pltpu.VMEM)
SMEM = pl.BlockSpec(memory_space=pltpu.SMEM)


def small_call(kernel, outs, scalars, arrays, moved):
    return pl.pallas_call(
        kernel,
        out_shape=outs,
        in_specs=[SMEM] * len(scalars) + [VMEM] * len(arrays),
        out_specs=jax.tree.map(lambda _: VMEM, outs),
        compiler_params=pltpu.CompilerParams(vmem_limit_bytes=16 * 1024 * 1024),
        cost_estimate=pl.CostEstimate(flops=moved, bytes_accessed=moved, transcendentals=0),
    )(*scalars, *arrays)


def spread_kernel(place_ref, mine_ref, theirs_ref, gate_ref, up_ref, *out_refs):
    y, side = place_ref[0], place_ref[1]
    give_ref, keep_ref, self_ref, right_ref, left_ref, opposite_ref, far_ref = out_refs
    order = [(y + i) % 4 for i in range(4)]
    sides = (side, 1 - side)
    n = mine_ref.shape[2]
    x = jnp.concatenate(
        [mine_ref[i, 1 - side] for i in order]
        + [theirs_ref[i, s] for i in order for s in sides]
        + [mine_ref[i, side] for i in order],
        axis=0,
    )
    step = pl.program_id(0)

    def put(weight_ref):
        total = jnp.dot(x, weight_ref[...], preferred_element_type=f32).astype(bf16)
        for i in range(4):
            give_ref[i] = total[i * n : (i + 1) * n]
            keep_ref[i] = total[(12 + i) * n : (13 + i) * n]
        for first, ref in ((4, self_ref), (6, right_ref), (10, left_ref)):
            for j in range(2):
                ref[j] = total[(first + j) * n : (first + j + 1) * n]
        opposite_ref[...] = total[8 * n : 9 * n]
        far_ref[...] = total[9 * n : 10 * n]

    half = pl.num_programs(0) // 2
    pl.when(step < half)(functools.partial(put, gate_ref))
    pl.when(step >= half)(functools.partial(put, up_ref))


def partial_columns(place, mine, theirs, gate, up):
    tile = 896
    inputs, width = gate.shape
    count = width // tile
    tokens = mine.shape[2]
    whole = pl.BlockSpec(mine.shape, lambda n, p: (0, 0, 0, 0))

    def out(*lead):
        block = pl.BlockSpec((*lead, tokens, tile), lambda n, p: (0,) * (len(lead) + 1) + (n,))
        return jax.ShapeDtypeStruct((*lead, tokens, 2 * width), bf16), block

    shapes, blocks = zip(*[out(4), out(4), out(2), out(2), out(2), out(), out()])
    rows = 16 * tokens
    return pl.pallas_call(
        spread_kernel,
        out_shape=shapes,
        grid_spec=pltpu.PrefetchScalarGridSpec(
            num_scalar_prefetch=1,
            grid=(2 * count,),
            in_specs=[
                whole,
                whole,
                pl.BlockSpec((inputs, tile), lambda n, p: (0, jnp.minimum(n, count - 1))),
                pl.BlockSpec((inputs, tile), lambda n, p: (0, jnp.maximum(n - count, 0))),
            ],
            out_specs=blocks,
        ),
        compiler_params=pltpu.CompilerParams(vmem_limit_bytes=40 * 1024 * 1024),
        cost_estimate=pl.CostEstimate(
            flops=4 * rows * inputs * width,
            bytes_accessed=2 * (rows * inputs + 2 * inputs * width + 2 * rows * width),
            transcendentals=0,
        ),
    )(place, mine, theirs, gate, up)


def arranged_sum(got, keep):
    tokens, width = keep.shape[1] // 2, keep.shape[2]

    def kernel(got_ref, keep_ref, self_ref, right_ref, left_ref, opposite_ref, far_ref):
        def block(i, j):
            rows = pl.ds(j * tokens, tokens)
            return (got_ref[i, rows].astype(f32) + keep_ref[i, rows].astype(f32)).astype(bf16)

        for i, ref in ((0, self_ref), (1, right_ref), (3, left_ref)):
            for j in range(2):
                ref[j] = block(i, j)
        opposite_ref[...] = block(2, 0)
        far_ref[...] = block(2, 1)

    two = jax.ShapeDtypeStruct((2, tokens, width), bf16)
    one = jax.ShapeDtypeStruct((tokens, width), bf16)
    return small_call(kernel, (two, two, two, one, one), (), (got, keep), 4 * keep.size)


def add_pieces(*pieces):
    def kernel(*refs):
        refs[-1][...] = sum(r[...].astype(f32) for r in refs[:-1]).astype(bf16)

    first = pieces[0]
    return small_call(kernel, jax.ShapeDtypeStruct(first.shape, bf16), (), pieces, 2 * first.size)


def gated(groups):
    counts = [len(g) for g in groups]
    tokens, width = groups[0][0].shape[0], groups[0][0].shape[1] // 2

    def kernel(*refs):
        out_ref = refs[-1]
        at = 0
        for i, count in enumerate(counts):
            mine = refs[at : at + count]
            at += count
            gate = sum(r[:, 0:width].astype(f32) for r in mine)
            up = sum(r[:, width:].astype(f32) for r in mine)
            out_ref[i * tokens : (i + 1) * tokens, :] = (gate / (1.0 + jnp.exp(-gate)) * up).astype(bf16)

    out = jax.ShapeDtypeStruct((tokens * len(groups), width), bf16)
    arrays = [p for g in groups for p in g]
    return small_call(kernel, out, (), arrays, 8 * tokens * width * len(groups))


def down_kernel(tile, place_ref, *refs):
    y, side = place_ref[0], place_ref[1]
    pieces, weight_ref, add_ref, out_ref = refs[:8], refs[8], refs[9:-1], refs[-1]
    n = pieces[0].shape[0]
    x = jnp.concatenate([p[...] for p in pieces], axis=0)
    total = jnp.dot(x, weight_ref[...], preferred_element_type=f32)
    for i in range(4):
        for j in range(2):
            at = 2 * ((y + i) % 4) + (side if j == 0 else 1 - side)
            part = total[(2 * i + j) * n : (2 * i + j + 1) * n]
            if add_ref:
                part = part + add_ref[0][at].astype(f32)
            out_ref[at] = part.astype(bf16)


def down_product(place, pieces, weight, add=None):
    tile = 256
    tokens, inputs = pieces[0].shape
    width = weight.shape[1]
    piece = pl.BlockSpec((tokens, inputs), lambda n, p: (0, 0))
    by_column = pl.BlockSpec((8, tokens, tile), lambda n, p: (0, 0, n))
    operands = [*pieces, weight] + ([] if add is None else [add])
    specs = [piece] * 8 + [pl.BlockSpec((inputs, tile), lambda n, p: (0, n))]
    specs += [] if add is None else [by_column]
    return pl.pallas_call(
        functools.partial(down_kernel, tile),
        out_shape=jax.ShapeDtypeStruct((8, tokens, width), bf16),
        grid_spec=pltpu.PrefetchScalarGridSpec(
            num_scalar_prefetch=1, grid=(width // tile,), in_specs=specs, out_specs=by_column
        ),
        compiler_params=pltpu.CompilerParams(vmem_limit_bytes=20 * 1024 * 1024),
        cost_estimate=pl.CostEstimate(
            flops=16 * tokens * inputs * width,
            bytes_accessed=2 * (8 * tokens * inputs + inputs * width + 8 * tokens * width),
            transcendentals=0,
        ),
    )(place, *operands)


def to_right(x):
    return lax.ppermute(x, "y", [(i, (i + 1) % 4) for i in range(4)])


def to_left(x):
    return lax.ppermute(x, "y", [(i, (i + 3) % 4) for i in range(4)])


def ring_start(pieces):
    _, right, left, opposite, far = pieces
    return to_right(opposite), to_left(far), to_right(right[1]), to_left(left[0])


def ring_middle(pieces, from_left, from_right):
    return add_pieces(pieces[1][0], from_left), add_pieces(pieces[2][1], from_right)


def ring_end(pieces, arrived, sums):
    third_left, third_right = to_right(sums[0]), to_left(sums[1])
    own = pieces[0]
    return (own[0], arrived[3], third_left), (own[1], arrived[2], third_right)


def gather_start(mine):
    return to_right(mine), to_left(mine)


def gather_middle(got, mine_left):
    return to_right(got), to_left(got), to_right(mine_left)


def gather_end(mine, got, mine_left, mine_right, got_left, got_right, mine_far):
    return mine, got, mine_right, got_right, mine_far, to_left(got_right), mine_left, got_left


def exchange(x, axes):
    return lax.all_to_all(x, axes, split_axis=0, concat_axis=0, tiled=True)


def swap(x, axis="core"):
    return lax.ppermute(x, axis, [(0, 1), (1, 0)])


def spread(x, copies):
    return jnp.broadcast_to(x[None], (copies,) + x.shape)


def take(x, index, axis):
    return lax.dynamic_index_in_dim(x, index, axis, keepdims=False)


def local(
    queries,
    cache_keys,
    cache_values,
    stretch_keys,
    stretch_values,
    block_lists,
    out_weight,
    residual,
    norm_gain,
    gate_weight,
    up_weight,
    down_weight,
):
    core = lax.axis_index("core")
    side = lax.axis_index("xl")
    col = lax.axis_index(COL)
    group = lax.axis_index(ZXH)
    me = lax.axis_index(ROW) * 8 + col
    local_blocks = cache_keys.shape[1] // BLK
    tokens_here = residual.shape[0]

    matched = block_lists // local_blocks == me
    within = jnp.sum(jnp.where(matched, block_lists % local_blocks, 0), axis=2)
    source = (jnp.arange(KV_HEADS, dtype=jnp.int32)[:, None] * local_blocks + within.T).reshape(-1)

    piece = BLK // 4
    flat_keys = cache_keys.reshape(4 * KV_HEADS * local_blocks, piece, HEAD_DIM)
    flat_values = cache_values.reshape(4 * KV_HEADS * local_blocks, piece, HEAD_DIM)

    def pick(flat, first, count):
        index = 4 * source[:, None] + jnp.arange(first, first + count, dtype=jnp.int32)[None, :]
        return flat[index].reshape(64, count * piece, HEAD_DIM)

    def near(stretch):
        part = BLK // 8
        rows = lax.dynamic_slice_in_dim(stretch, group * part, part, 1)
        return jnp.broadcast_to(rows[:, None], (KV_HEADS, 8, part, HEAD_DIM)).reshape(64, part, HEAD_DIM)

    first = [pick(flat_keys, 0, 3), pick(flat_values, 0, 3), near(stretch_keys), near(stretch_values)]
    first = exchange(jnp.concatenate(first, axis=1), CHIP)
    second = [pick(flat_keys, 3, 1), pick(flat_values, 3, 1)]
    second = exchange(jnp.concatenate(second, axis=1), CHIP)
    my_list = block_lists[col, group]
    place = jnp.stack([core, col]).astype(jnp.int32)
    other_queries = swap(queries)
    own, send, order = attend((my_list, place), queries, other_queries, first, (), local_blocks, 5)
    own, send = attend((order,), queries, other_queries, second, (own, send), local_blocks, 16)
    attended = exchange(merge(own, swap(send), 8), COL).reshape(8, 2, tokens_here, -1)

    def row_sum(give, mine, pick, weight):
        both = product(mine, (weight,), 512, pick, add=swap(give))
        return jnp.sum(exchange(both.reshape(8, tokens_here, -1), ZXH).astype(f32), axis=0)

    give = product(attended, (out_weight,), 512, 1 - core)
    stream = residual.astype(f32) + row_sum(give, attended, core, out_weight)
    squares = jnp.broadcast_to(jnp.sum(stream * stream, axis=1)[None], (8, tokens_here))
    squares = squares + swap(squares, "xl")
    across = lax.ppermute(squares, "y", [(i, (i + 2) % 4) for i in range(4)])
    squares = squares + across + to_right(squares) + to_left(squares)
    normed = stream * lax.rsqrt(squares[0] / D + 1e-05)[:, None] * norm_gain.astype(f32)[None, :]
    own_rows = exchange(spread(normed.astype(bf16), 8), ZXH)
    other_rows = swap(own_rows)

    by_pair = (4, 2, tokens_here, own_rows.shape[-1])
    where = jnp.stack([lax.axis_index("y"), side]).astype(jnp.int32)
    give, keep, *pieces = partial_columns(
        where, own_rows.reshape(by_pair), other_rows.reshape(by_pair), gate_weight, up_weight
    )
    got = swap(give, "xl")
    arrived = ring_start(pieces)
    here, there = ring_end(pieces, arrived, ring_middle(pieces, *arrived[:2]))
    other_give = add_pieces(*there)
    got, other_give = lax.optimization_barrier((got, other_give))
    pieces = arranged_sum(got, keep)
    arrived, other_got = lax.optimization_barrier((ring_start(pieces), swap(other_give, "xl")))
    sums = ring_middle(pieces, *arrived[:2])
    other_hidden = gated([(*here, other_got)])
    own_sums = ring_end(pieces, arrived, sums)
    own_sums, other_first = lax.optimization_barrier((own_sums, gather_start(other_hidden)))
    own_hidden = gated(own_sums)
    other_got = swap(other_hidden, "xl")
    other_second, own_first, own_got = lax.optimization_barrier(
        (gather_middle(other_got, other_first[0]), gather_start(own_hidden), swap(own_hidden, "xl"))
    )
    other_all = gather_end(other_hidden, other_got, *other_first, *other_second)
    own_second = gather_middle(own_got, own_first[0])
    own_all = gather_end(own_hidden, own_got, *own_first, *own_second)
    given = down_product(where, other_all, down_weight)
    down = down_product(where, own_all, down_weight, add=swap(given))
    mlp = jnp.sum(exchange(down, ZXH).astype(f32), axis=0)
    return (stream + mlp).astype(bf16)


def solution(mesh):
    mesh = Mesh(mesh.devices.reshape(4, 2, 2, 4, 2), AXES)
    in_specs = (
        P(COL, ROW),
        P(None, ROW + COL, None),
        P(None, ROW + COL, None),
        P(None, COL, None),
        P(None, COL, None),
        P(),
        P(ROW, COL),
        P(ROW, COL),
        P(COL),
        P(COL, ROW),
        P(COL, ROW),
        P(ROW, COL),
    )
    return jax.shard_map(local, mesh=mesh, in_specs=in_specs, out_specs=P(ROW, COL), check_vma=False)
```

```python
import functools
import math

import jax
import jax.numpy as jnp
from jax import lax
from jax.experimental import pallas as pl
from jax.experimental.pallas import tpu as pltpu
from jax.sharding import Mesh, PartitionSpec as P

D = 8192
KV_HEADS = 8
HEAD_DIM = 128
BLK = 128
GROUP = 8
AXES = ("z", "xh", "core", "y", "xl")
ROW = ("z", "xh", "core")
ZXH = ("z", "xh")
COL = ("y", "xl")
CHIP = ("z", "xh", "y", "xl")
NEG = -1e30
bf16 = jnp.bfloat16
f32 = jnp.float32


def nt_dot(a, b):
    return lax.dot_general(a, b, (((1,), (1,)), ((), ())), preferred_element_type=f32)


def tn_dot(a, b):
    return lax.dot_general(a, b, (((0,), (0,)), ((), ())), preferred_element_type=f32)


def attend_kernel(scale, per_step, local_blocks, last, *refs):
    if last:
        order_ref, own_q_ref, other_q_ref, chunk_ref, own_in_ref, send_in_ref = refs[:6]
    else:
        list_ref, place_ref, own_q_ref, other_q_ref, chunk_ref = refs[:5]
        order_ref = refs[7]
    own_ref, send_ref = refs[6:8] if last else refs[5:7]
    q_ref, top_ref, sum_ref, acc_ref = refs[-4:]
    length = order_ref.shape[0] - 1
    part_rows = (chunk_ref.shape[1] - (0 if last else BLK // 4)) // 2
    heads = own_q_ref.shape[1] // HEAD_DIM
    rows = heads * BLK
    for h in range(heads):
        cols = pl.ds(h * HEAD_DIM, HEAD_DIM)
        q_ref[pl.ds(h * BLK, BLK), :] = own_q_ref[:, cols]
        q_ref[pl.ds(rows + h * BLK, BLK), :] = other_q_ref[:, cols]
    if last:
        for half, ref in ((0, own_in_ref), (1, send_in_ref)):
            acc_ref[half] = ref[0:HEAD_DIM, :]
            top_ref[half] = ref[HEAD_DIM : HEAD_DIM + 1, :]
            sum_ref[half] = ref[HEAD_DIM + 1 : HEAD_DIM + 2, :]
        count = order_ref[length]
    else:
        core = place_ref[0]
        block = place_ref[1]
        top_ref[...] = jnp.full_like(top_ref, NEG)
        sum_ref[...] = jnp.zeros_like(sum_ref)
        acc_ref[...] = jnp.zeros_like(acc_ref)

        def collect(i, count):
            device = list_ref[i] // local_blocks
            row = device // 8
            order_ref[count] = (row // 2) * 8 + device % 8
            return count + jnp.where(row % 2 == core, 1, 0)

        count = lax.fori_loop(0, length, collect, jnp.int32(0))
        order_ref[length] = count

    def update(half, keys, values, bias):
        part = pl.ds(half * rows, rows)
        scores = nt_dot(keys, q_ref[part, :]) * scale + bias
        old = top_ref[half]
        new = jnp.maximum(old, jnp.max(scores, axis=0, keepdims=True))
        weights = jnp.exp2(scores - new)
        decay = jnp.exp2(old - new)
        top_ref[half] = new
        sum_ref[half] = sum_ref[half] * decay + jnp.sum(weights, axis=0, keepdims=True)
        acc_ref[half] = acc_ref[half] * decay + tn_dot(values, weights.astype(bf16))

    def far(step, carry):
        slots = [order_ref[jnp.minimum(step * per_step + i, count - 1)] for i in range(per_step)]
        keys = jnp.concatenate([chunk_ref[s, 0:part_rows] for s in slots], axis=0)
        values = jnp.concatenate([chunk_ref[s, part_rows : 2 * part_rows] for s in slots], axis=0)
        bias = jnp.concatenate(
            [
                jnp.full((part_rows, 1), jnp.where(step * per_step + i < count, 0.0, NEG), f32)
                for i in range(per_step)
            ],
            axis=0,
        )
        for half in range(2):
            update(half, keys, values, bias)
        return carry

    lax.fori_loop(0, (count + per_step - 1) // per_step, far, 0)

    def near(j, carry):
        which = core + 2 * j
        shift = (block - which) * BLK
        key_pos = lax.broadcasted_iota(jnp.int32, (BLK, rows), 0)
        token = lax.broadcasted_iota(jnp.int32, (BLK, rows), 1) % BLK
        bias = jnp.where(key_pos <= token + shift, 0.0, NEG)
        at = 2 * part_rows
        eighth = BLK // 8
        keys = jnp.concatenate([chunk_ref[i * 8 + which, at : at + eighth] for i in range(8)], axis=0)
        values = jnp.concatenate([chunk_ref[i * 8 + which, at + eighth :] for i in range(8)], axis=0)
        for half in range(2):
            update(half, keys, values, bias)
        return carry

    if not last:
        lax.fori_loop(0, (block - core + 2) // 2, near, 0)
    for half, ref in ((0, own_ref), (1, send_ref)):
        ref[0:HEAD_DIM, :] = acc_ref[half]
        ref[HEAD_DIM : HEAD_DIM + 1, :] = top_ref[half]
        ref[HEAD_DIM + 1 : HEAD_DIM + 2, :] = sum_ref[half]


def attend(scalars, own_q, other_q, chunk, state, local_blocks, per_step):
    heads = own_q.shape[1] // HEAD_DIM
    rows = heads * BLK
    length = scalars[0].shape[0] - len(state) // 2
    packed = jax.ShapeDtypeStruct((HEAD_DIM + 8, rows), f32)
    smem = pl.BlockSpec(memory_space=pltpu.SMEM)
    vmem = pl.BlockSpec(memory_space=pltpu.VMEM)
    scale = math.log2(math.e) / math.sqrt(HEAD_DIM)
    arrays = [own_q, other_q, chunk, *state]
    outs = [packed, packed]
    if not state:
        outs.append(jax.ShapeDtypeStruct((length + 1,), jnp.int32))
    return pl.pallas_call(
        functools.partial(attend_kernel, scale, per_step, local_blocks, len(state) > 0),
        out_shape=outs,
        in_specs=[smem] * len(scalars) + [vmem] * len(arrays),
        out_specs=[vmem, vmem, smem][: len(outs)],
        scratch_shapes=[
            pltpu.VMEM((2 * rows, HEAD_DIM), bf16),
            pltpu.VMEM((2, 1, rows), f32),
            pltpu.VMEM((2, 1, rows), f32),
            pltpu.VMEM((2, HEAD_DIM, rows), f32),
        ],
        compiler_params=pltpu.CompilerParams(vmem_limit_bytes=24 * 1024 * 1024),
        cost_estimate=pl.CostEstimate(
            flops=2 * rows * 40 * chunk.shape[1] * HEAD_DIM,
            bytes_accessed=2 * chunk.size,
            transcendentals=rows * 40 * chunk.shape[1],
        ),
    )(*scalars, *arrays)


def merge_kernel(own_ref, got_ref, out_ref):
    own_top = own_ref[HEAD_DIM : HEAD_DIM + 1, :]
    got_top = got_ref[HEAD_DIM : HEAD_DIM + 1, :]
    top = jnp.maximum(own_top, got_top)
    own_w = jnp.exp2(own_top - top)
    got_w = jnp.exp2(got_top - top)
    total = own_w * own_ref[HEAD_DIM + 1 : HEAD_DIM + 2, :] + got_w * got_ref[HEAD_DIM + 1 : HEAD_DIM + 2, :]
    mixed = (own_ref[0:HEAD_DIM, :] * own_w + got_ref[0:HEAD_DIM, :] * got_w) / total
    heads = mixed.shape[1] // BLK
    for h in range(heads):
        piece = mixed[:, h * BLK : (h + 1) * BLK].T.astype(bf16)
        for i in range(out_ref.shape[0]):
            out_ref[i, :, pl.ds(h * HEAD_DIM, HEAD_DIM)] = piece


def merge(own, got, copies):
    heads = own.shape[1] // BLK
    vmem = pl.BlockSpec(memory_space=pltpu.VMEM)
    return pl.pallas_call(
        merge_kernel,
        out_shape=jax.ShapeDtypeStruct((copies, BLK, heads * HEAD_DIM), bf16),
        in_specs=[vmem, vmem],
        out_specs=vmem,
        compiler_params=pltpu.CompilerParams(vmem_limit_bytes=12 * 1024 * 1024),
    )(own, got)


def product_kernel(tile, weight_count, pick_ref, x_ref, *refs):
    weight_refs, add_ref, out_ref = refs[:weight_count], refs[weight_count:-1], refs[-1]
    x = x_ref[:, pick_ref[0]] if x_ref.shape[1] > out_ref.shape[1] else x_ref[...]
    x = x.reshape(-1, x.shape[-1])
    width = weight_refs[0].shape[1]
    block = out_ref.shape[:-1] + (tile,)
    for i, weight_ref in enumerate(weight_refs):
        for first in range(0, width, tile):
            total = jnp.dot(x, weight_ref[:, first : first + tile], preferred_element_type=f32)
            columns = slice(i * width + first, i * width + first + tile)
            if add_ref:
                total = total + add_ref[0][..., columns].reshape(total.shape).astype(f32)
            out_ref[..., columns] = total.astype(bf16).reshape(block)


def product(x, weights, tile, pick=None, add=None):
    blocks, pair, tokens, inputs = x.shape
    taken = pair if pick is None else 1
    pick = jnp.zeros((1,), jnp.int32) if pick is None else pick.astype(jnp.int32).reshape(1)
    vmem = pl.BlockSpec(memory_space=pltpu.VMEM)
    operands = [x, *weights] if add is None else [x, *weights, add]
    rows = blocks * taken * tokens
    columns = weights[0].shape[1] * len(weights)
    return pl.pallas_call(
        functools.partial(product_kernel, tile, len(weights)),
        out_shape=jax.ShapeDtypeStruct((blocks, taken, tokens, columns), bf16),
        in_specs=[pl.BlockSpec(memory_space=pltpu.SMEM)] + [vmem] * len(operands),
        out_specs=vmem,
        compiler_params=pltpu.CompilerParams(vmem_limit_bytes=20 * 1024 * 1024),
        cost_estimate=pl.CostEstimate(
            flops=2 * rows * inputs * columns,
            bytes_accessed=2 * (rows * inputs + inputs * columns + rows * columns),
            transcendentals=0,
        ),
    )(pick, *operands)


VMEM = pl.BlockSpec(memory_space=pltpu.VMEM)
SMEM = pl.BlockSpec(memory_space=pltpu.SMEM)


def small_call(kernel, outs, scalars, arrays, moved):
    return pl.pallas_call(
        kernel,
        out_shape=outs,
        in_specs=[SMEM] * len(scalars) + [VMEM] * len(arrays),
        out_specs=jax.tree.map(lambda _: VMEM, outs),
        compiler_params=pltpu.CompilerParams(vmem_limit_bytes=16 * 1024 * 1024),
        cost_estimate=pl.CostEstimate(flops=moved, bytes_accessed=moved, transcendentals=0),
    )(*scalars, *arrays)


def spread_kernel(place_ref, mine_ref, theirs_ref, gate_ref, up_ref, *out_refs):
    y, side = place_ref[0], place_ref[1]
    give_ref, keep_ref, self_ref, right_ref, left_ref, opposite_ref, far_ref = out_refs
    order = [(y + i) % 4 for i in range(4)]
    sides = (side, 1 - side)
    n = mine_ref.shape[2]
    x = jnp.concatenate(
        [mine_ref[i, 1 - side] for i in range(4)]
        + [theirs_ref[i, s] for i in order for s in sides]
        + [mine_ref[i, side] for i in range(4)],
        axis=0,
    )
    step = pl.program_id(0)

    def put(weight_ref):
        total = jnp.dot(x, weight_ref[...], preferred_element_type=f32).astype(bf16)
        for i in range(4):
            give_ref[i] = total[i * n : (i + 1) * n]
            keep_ref[i] = total[(12 + i) * n : (13 + i) * n]
        for first, ref in ((4, self_ref), (6, right_ref), (10, left_ref)):
            for j in range(2):
                ref[j] = total[(first + j) * n : (first + j + 1) * n]
        opposite_ref[...] = total[8 * n : 9 * n]
        far_ref[...] = total[9 * n : 10 * n]

    half = pl.num_programs(0) // 2
    pl.when(step < half)(functools.partial(put, gate_ref))
    pl.when(step >= half)(functools.partial(put, up_ref))


def partial_columns(place, mine, theirs, gate, up):
    tile = 896
    inputs, width = gate.shape
    count = width // tile
    tokens = mine.shape[2]
    whole = pl.BlockSpec(mine.shape, lambda n, p: (0, 0, 0, 0))

    def out(*lead):
        block = pl.BlockSpec((*lead, tokens, tile), lambda n, p: (0,) * (len(lead) + 1) + (n,))
        return jax.ShapeDtypeStruct((*lead, tokens, 2 * width), bf16), block

    shapes, blocks = zip(*[out(4), out(4), out(2), out(2), out(2), out(), out()])
    rows = 16 * tokens
    return pl.pallas_call(
        spread_kernel,
        out_shape=shapes,
        grid_spec=pltpu.PrefetchScalarGridSpec(
            num_scalar_prefetch=1,
            grid=(2 * count,),
            in_specs=[
                whole,
                whole,
                pl.BlockSpec((inputs, tile), lambda n, p: (0, jnp.minimum(n, count - 1))),
                pl.BlockSpec((inputs, tile), lambda n, p: (0, jnp.maximum(n - count, 0))),
            ],
            out_specs=blocks,
        ),
        compiler_params=pltpu.CompilerParams(vmem_limit_bytes=60 * 1024 * 1024),
        cost_estimate=pl.CostEstimate(
            flops=4 * rows * inputs * width,
            bytes_accessed=2 * (rows * inputs + 2 * inputs * width + 2 * rows * width),
            transcendentals=0,
        ),
    )(place, mine, theirs, gate, up)


def add_pieces(*pieces):
    def kernel(*refs):
        refs[-1][...] = sum(r[...].astype(f32) for r in refs[:-1]).astype(bf16)

    first = pieces[0]
    return small_call(kernel, jax.ShapeDtypeStruct(first.shape, bf16), (), pieces, 2 * first.size)


def gated(pieces, factor):
    tokens, width = pieces[0].shape[-2], pieces[0].shape[-1] // 2

    def kernel(*refs):
        scale = refs[-2][...]

        def total(columns):
            parts = [r[..., columns].astype(f32) for r in refs[:-2]]
            return sum(jnp.sum(v, axis=0) if v.ndim == 3 else v for v in parts) * scale

        gate = total(slice(0, width))
        refs[-1][...] = (gate / (1.0 + jnp.exp(-gate)) * total(slice(width, 2 * width))).astype(bf16)

    out = jax.ShapeDtypeStruct((tokens, width), bf16)
    return small_call(kernel, out, (), [*pieces, factor[:, None]], 8 * tokens * width)


def down_kernel(tile, place_ref, *refs):
    y, side = place_ref[0], place_ref[1]
    pieces, weight_ref, add_ref, out_ref = refs[:8], refs[8], refs[9:-1], refs[-1]
    n = pieces[0].shape[0]
    x = jnp.concatenate([p[...] for p in pieces], axis=0)
    total = jnp.dot(x, weight_ref[...], preferred_element_type=f32)
    for i in range(4):
        for j in range(2):
            at = 2 * ((y + i) % 4) + (side if j == 0 else 1 - side)
            part = total[(2 * i + j) * n : (2 * i + j + 1) * n]
            if add_ref:
                part = part + add_ref[0][at].astype(f32)
            out_ref[at] = part.astype(bf16)


def down_product(place, pieces, weight, add=None):
    tile = 256
    tokens, inputs = pieces[0].shape
    width = weight.shape[1]
    piece = pl.BlockSpec((tokens, inputs), lambda n, p: (0, 0))
    by_column = pl.BlockSpec((8, tokens, tile), lambda n, p: (0, 0, n))
    operands = [*pieces, weight] + ([] if add is None else [add])
    specs = [piece] * 8 + [pl.BlockSpec((inputs, tile), lambda n, p: (0, n))]
    specs += [] if add is None else [by_column]
    return pl.pallas_call(
        functools.partial(down_kernel, tile),
        out_shape=jax.ShapeDtypeStruct((8, tokens, width), bf16),
        grid_spec=pltpu.PrefetchScalarGridSpec(
            num_scalar_prefetch=1, grid=(width // tile,), in_specs=specs, out_specs=by_column
        ),
        compiler_params=pltpu.CompilerParams(vmem_limit_bytes=20 * 1024 * 1024),
        cost_estimate=pl.CostEstimate(
            flops=16 * tokens * inputs * width,
            bytes_accessed=2 * (8 * tokens * inputs + inputs * width + 8 * tokens * width),
            transcendentals=0,
        ),
    )(place, *operands)


def to_right(x):
    return lax.ppermute(x, "y", [(i, (i + 1) % 4) for i in range(4)])


def to_left(x):
    return lax.ppermute(x, "y", [(i, (i + 3) % 4) for i in range(4)])


def ring_start(pieces):
    _, right, left, opposite, far = pieces
    return to_right(opposite), to_left(far), to_right(right[1]), to_left(left[0])


def ring_middle(pieces, from_left, from_right):
    return add_pieces(pieces[1][0], from_left), add_pieces(pieces[2][1], from_right)


def ring_end(pieces, arrived, sums):
    third_left, third_right = to_right(sums[0]), to_left(sums[1])
    own = pieces[0]
    return (own[0], arrived[3], third_left), (own[1], arrived[2], third_right)


def gather_start(mine):
    return to_right(mine), to_left(mine)


def gather_middle(got, mine_left):
    return to_right(got), to_left(got), to_right(mine_left)


def gather_end(mine, got, mine_left, mine_right, got_left, got_right, mine_far):
    return mine, got, mine_right, got_right, mine_far, to_left(got_right), mine_left, got_left


def exchange(x, axes):
    return lax.all_to_all(x, axes, split_axis=0, concat_axis=0, tiled=True)


def swap(x, axis="core"):
    return lax.ppermute(x, axis, [(0, 1), (1, 0)])


def spread(x, copies):
    return jnp.broadcast_to(x[None], (copies,) + x.shape)


def take(x, index, axis):
    return lax.dynamic_index_in_dim(x, index, axis, keepdims=False)


def local(
    queries,
    cache_keys,
    cache_values,
    stretch_keys,
    stretch_values,
    block_lists,
    out_weight,
    residual,
    norm_gain,
    gate_weight,
    up_weight,
    down_weight,
):
    core = lax.axis_index("core")
    side = lax.axis_index("xl")
    col = lax.axis_index(COL)
    group = lax.axis_index(ZXH)
    me = lax.axis_index(ROW) * 8 + col
    local_blocks = cache_keys.shape[1] // BLK
    tokens_here = residual.shape[0]

    matched = block_lists // local_blocks == me
    within = jnp.sum(jnp.where(matched, block_lists % local_blocks, 0), axis=2)
    source = (jnp.arange(KV_HEADS, dtype=jnp.int32)[:, None] * local_blocks + within.T).reshape(-1)

    piece = BLK // 4
    flat_keys = cache_keys.reshape(4 * KV_HEADS * local_blocks, piece, HEAD_DIM)
    flat_values = cache_values.reshape(4 * KV_HEADS * local_blocks, piece, HEAD_DIM)

    def pick(flat, first, count):
        index = 4 * source[:, None] + jnp.arange(first, first + count, dtype=jnp.int32)[None, :]
        return flat[index].reshape(64, count * piece, HEAD_DIM)

    def near(stretch):
        part = BLK // 8
        rows = lax.dynamic_slice_in_dim(stretch, group * part, part, 1)
        return jnp.broadcast_to(rows[:, None], (KV_HEADS, 8, part, HEAD_DIM)).reshape(64, part, HEAD_DIM)

    first = [pick(flat_keys, 0, 3), pick(flat_values, 0, 3), near(stretch_keys), near(stretch_values)]
    first = exchange(jnp.concatenate(first, axis=1), CHIP)
    second = [pick(flat_keys, 3, 1), pick(flat_values, 3, 1)]
    second = exchange(jnp.concatenate(second, axis=1), CHIP)
    my_list = block_lists[col, group]
    place = jnp.stack([core, col]).astype(jnp.int32)
    other_queries = swap(queries)
    own, send, order = attend((my_list, place), queries, other_queries, first, (), local_blocks, 5)
    own, send = attend((order,), queries, other_queries, second, (own, send), local_blocks, 16)
    attended = exchange(merge(own, swap(send), 8), COL).reshape(8, 2, tokens_here, -1)

    def row_sum(give, mine, pick, weight):
        both = product(mine, (weight,), 512, pick, add=swap(give))
        return jnp.sum(exchange(both.reshape(8, tokens_here, -1), ZXH).astype(f32), axis=0)

    give = product(attended, (out_weight,), 512, 1 - core)
    stream = residual.astype(f32) + row_sum(give, attended, core, out_weight)
    gain = norm_gain.astype(f32)[None, :]
    own_rows = exchange(spread((stream * gain).astype(bf16), 8), ZXH)
    other_rows = swap(own_rows)

    def squares(x):
        plain = x.astype(f32) / gain[None]
        return jnp.sum(plain * plain, axis=2)

    squares = jnp.stack([squares(own_rows), squares(other_rows)], axis=1)

    by_pair = (4, 2, tokens_here, own_rows.shape[-1])
    where = jnp.stack([lax.axis_index("y"), side]).astype(jnp.int32)
    columns = partial_columns(
        where, own_rows.reshape(by_pair), other_rows.reshape(by_pair), gate_weight, up_weight
    )
    (give, keep, *pieces), squares = lax.optimization_barrier((columns, squares))
    squares = exchange(squares, COL)
    got = swap(give, "xl")
    arrived = ring_start(pieces)
    steps, squares = lax.optimization_barrier((arrived[:2], squares))
    factor = lax.rsqrt(jnp.sum(squares, axis=0).reshape(2, tokens_here) / D + 1e-05)
    here, there = ring_end(pieces, arrived, ring_middle(pieces, *steps))
    other_give = add_pieces(*there)
    got, other_give, here, factor = lax.optimization_barrier((got, other_give, here, factor))
    own_part = exchange((got.astype(f32) + keep.astype(f32)).astype(bf16), "y")
    other_hidden = gated((*here, swap(other_give, "xl")), factor[1])
    other_got = swap(other_hidden, "xl")
    first = gather_start(other_hidden)
    other_all = gather_end(other_hidden, other_got, *first, *gather_middle(other_got, first[0]))
    own_part, other_all = lax.optimization_barrier((own_part, other_all))
    own_hidden = gated((own_part,), factor[0])
    own_got = swap(own_hidden, "xl")
    first = gather_start(own_hidden)
    second = gather_middle(own_got, first[0])
    first, second, other_all = lax.optimization_barrier((first, second, other_all))
    own_all = gather_end(own_hidden, own_got, *first, *second)
    given = down_product(where, other_all, down_weight)
    down = down_product(where, own_all, down_weight, add=swap(given))
    mlp = jnp.sum(exchange(down, ZXH).astype(f32), axis=0)
    return (stream + mlp).astype(bf16)


def solution(mesh):
    mesh = Mesh(mesh.devices.reshape(4, 2, 2, 4, 2), AXES)
    in_specs = (
        P(COL, ROW),
        P(None, ROW + COL, None),
        P(None, ROW + COL, None),
        P(None, COL, None),
        P(None, COL, None),
        P(),
        P(ROW, COL),
        P(ROW, COL),
        P(COL),
        P(COL, ROW),
        P(COL, ROW),
        P(ROW, COL),
    )
    return jax.shard_map(local, mesh=mesh, in_specs=in_specs, out_specs=P(ROW, COL), check_vma=False)
```

```python
import functools
import math

import jax
import jax.numpy as jnp
from jax import lax
from jax.experimental import pallas as pl
from jax.experimental.pallas import tpu as pltpu
from jax.sharding import Mesh, PartitionSpec as P

D = 8192
KV_HEADS = 8
HEAD_DIM = 128
BLK = 128
GROUP = 8
AXES = ("z", "xh", "core", "y", "xl")
ROW = ("z", "xh", "core")
ZXH = ("z", "xh")
COL = ("y", "xl")
CHIP = ("z", "xh", "y", "xl")
NEG = -1e30
bf16 = jnp.bfloat16
f32 = jnp.float32


def nt_dot(a, b):
    return lax.dot_general(a, b, (((1,), (1,)), ((), ())), preferred_element_type=f32)


def tn_dot(a, b):
    return lax.dot_general(a, b, (((0,), (0,)), ((), ())), preferred_element_type=f32)


def attend_kernel(scale, per_step, local_blocks, last, *refs):
    if last:
        order_ref, own_q_ref, other_q_ref, chunk_ref, own_in_ref, send_in_ref = refs[:6]
    else:
        list_ref, place_ref, own_q_ref, other_q_ref, chunk_ref = refs[:5]
        order_ref = refs[7]
    own_ref, send_ref = refs[6:8] if last else refs[5:7]
    q_ref, top_ref, sum_ref, acc_ref = refs[-4:]
    length = order_ref.shape[0] - 1
    part_rows = (chunk_ref.shape[1] - (0 if last else BLK // 4)) // 2
    heads = own_q_ref.shape[1] // HEAD_DIM
    rows = heads * BLK
    for h in range(heads):
        cols = pl.ds(h * HEAD_DIM, HEAD_DIM)
        q_ref[pl.ds(h * BLK, BLK), :] = own_q_ref[:, cols]
        q_ref[pl.ds(rows + h * BLK, BLK), :] = other_q_ref[:, cols]
    if last:
        for half, ref in ((0, own_in_ref), (1, send_in_ref)):
            acc_ref[half] = ref[0:HEAD_DIM, :]
            top_ref[half] = ref[HEAD_DIM : HEAD_DIM + 1, :]
            sum_ref[half] = ref[HEAD_DIM + 1 : HEAD_DIM + 2, :]
        count = order_ref[length]
    else:
        core = place_ref[0]
        block = place_ref[1]
        top_ref[...] = jnp.full_like(top_ref, NEG)
        sum_ref[...] = jnp.zeros_like(sum_ref)
        acc_ref[...] = jnp.zeros_like(acc_ref)

        def collect(i, count):
            device = list_ref[i] // local_blocks
            row = device // 8
            order_ref[count] = (row // 2) * 8 + device % 8
            return count + jnp.where(row % 2 == core, 1, 0)

        count = lax.fori_loop(0, length, collect, jnp.int32(0))
        order_ref[length] = count

    def update(half, keys, values, bias):
        part = pl.ds(half * rows, rows)
        scores = nt_dot(keys, q_ref[part, :]) * scale + bias
        old = top_ref[half]
        new = jnp.maximum(old, jnp.max(scores, axis=0, keepdims=True))
        weights = jnp.exp2(scores - new)
        decay = jnp.exp2(old - new)
        top_ref[half] = new
        sum_ref[half] = sum_ref[half] * decay + jnp.sum(weights, axis=0, keepdims=True)
        acc_ref[half] = acc_ref[half] * decay + tn_dot(values, weights.astype(bf16))

    def far(step, carry):
        slots = [order_ref[jnp.minimum(step * per_step + i, count - 1)] for i in range(per_step)]
        keys = jnp.concatenate([chunk_ref[s, 0:part_rows] for s in slots], axis=0)
        values = jnp.concatenate([chunk_ref[s, part_rows : 2 * part_rows] for s in slots], axis=0)
        bias = jnp.concatenate(
            [
                jnp.full((part_rows, 1), jnp.where(step * per_step + i < count, 0.0, NEG), f32)
                for i in range(per_step)
            ],
            axis=0,
        )
        for half in range(2):
            update(half, keys, values, bias)
        return carry

    lax.fori_loop(0, (count + per_step - 1) // per_step, far, 0)

    def near(j, carry):
        which = core + 2 * j
        shift = (block - which) * BLK
        key_pos = lax.broadcasted_iota(jnp.int32, (BLK, rows), 0)
        token = lax.broadcasted_iota(jnp.int32, (BLK, rows), 1) % BLK
        bias = jnp.where(key_pos <= token + shift, 0.0, NEG)
        at = 2 * part_rows
        eighth = BLK // 8
        keys = jnp.concatenate([chunk_ref[i * 8 + which, at : at + eighth] for i in range(8)], axis=0)
        values = jnp.concatenate([chunk_ref[i * 8 + which, at + eighth :] for i in range(8)], axis=0)
        for half in range(2):
            update(half, keys, values, bias)
        return carry

    if not last:
        lax.fori_loop(0, (block - core + 2) // 2, near, 0)
    for half, ref in ((0, own_ref), (1, send_ref)):
        ref[0:HEAD_DIM, :] = acc_ref[half]
        ref[HEAD_DIM : HEAD_DIM + 1, :] = top_ref[half]
        ref[HEAD_DIM + 1 : HEAD_DIM + 2, :] = sum_ref[half]


def attend(scalars, own_q, other_q, chunk, state, local_blocks, per_step):
    heads = own_q.shape[1] // HEAD_DIM
    rows = heads * BLK
    length = scalars[0].shape[0] - len(state) // 2
    packed = jax.ShapeDtypeStruct((HEAD_DIM + 8, rows), f32)
    smem = pl.BlockSpec(memory_space=pltpu.SMEM)
    vmem = pl.BlockSpec(memory_space=pltpu.VMEM)
    scale = math.log2(math.e) / math.sqrt(HEAD_DIM)
    arrays = [own_q, other_q, chunk, *state]
    outs = [packed, packed]
    if not state:
        outs.append(jax.ShapeDtypeStruct((length + 1,), jnp.int32))
    return pl.pallas_call(
        functools.partial(attend_kernel, scale, per_step, local_blocks, len(state) > 0),
        out_shape=outs,
        in_specs=[smem] * len(scalars) + [vmem] * len(arrays),
        out_specs=[vmem, vmem, smem][: len(outs)],
        scratch_shapes=[
            pltpu.VMEM((2 * rows, HEAD_DIM), bf16),
            pltpu.VMEM((2, 1, rows), f32),
            pltpu.VMEM((2, 1, rows), f32),
            pltpu.VMEM((2, HEAD_DIM, rows), f32),
        ],
        compiler_params=pltpu.CompilerParams(vmem_limit_bytes=24 * 1024 * 1024),
        cost_estimate=pl.CostEstimate(
            flops=2 * rows * 40 * chunk.shape[1] * HEAD_DIM,
            bytes_accessed=2 * chunk.size,
            transcendentals=rows * 40 * chunk.shape[1],
        ),
    )(*scalars, *arrays)


def merge_kernel(own_ref, got_ref, out_ref):
    own_top = own_ref[HEAD_DIM : HEAD_DIM + 1, :]
    got_top = got_ref[HEAD_DIM : HEAD_DIM + 1, :]
    top = jnp.maximum(own_top, got_top)
    own_w = jnp.exp2(own_top - top)
    got_w = jnp.exp2(got_top - top)
    total = own_w * own_ref[HEAD_DIM + 1 : HEAD_DIM + 2, :] + got_w * got_ref[HEAD_DIM + 1 : HEAD_DIM + 2, :]
    mixed = (own_ref[0:HEAD_DIM, :] * own_w + got_ref[0:HEAD_DIM, :] * got_w) / total
    heads = mixed.shape[1] // BLK
    for h in range(heads):
        piece = mixed[:, h * BLK : (h + 1) * BLK].T.astype(bf16)
        for i in range(out_ref.shape[0]):
            out_ref[i, :, pl.ds(h * HEAD_DIM, HEAD_DIM)] = piece


def merge(own, got, copies):
    heads = own.shape[1] // BLK
    vmem = pl.BlockSpec(memory_space=pltpu.VMEM)
    return pl.pallas_call(
        merge_kernel,
        out_shape=jax.ShapeDtypeStruct((copies, BLK, heads * HEAD_DIM), bf16),
        in_specs=[vmem, vmem],
        out_specs=vmem,
        compiler_params=pltpu.CompilerParams(vmem_limit_bytes=12 * 1024 * 1024),
    )(own, got)


def product_kernel(tile, weight_count, pick_ref, x_ref, *refs):
    weight_refs, add_ref, out_ref = refs[:weight_count], refs[weight_count:-1], refs[-1]
    x = x_ref[:, pick_ref[0]] if x_ref.shape[1] > out_ref.shape[1] else x_ref[...]
    x = x.reshape(-1, x.shape[-1])
    width = weight_refs[0].shape[1]
    block = out_ref.shape[:-1] + (tile,)
    for i, weight_ref in enumerate(weight_refs):
        for first in range(0, width, tile):
            total = jnp.dot(x, weight_ref[:, first : first + tile], preferred_element_type=f32)
            columns = slice(i * width + first, i * width + first + tile)
            if add_ref:
                total = total + add_ref[0][..., columns].reshape(total.shape).astype(f32)
            out_ref[..., columns] = total.astype(bf16).reshape(block)


def product(x, weights, tile, pick=None, add=None):
    blocks, pair, tokens, inputs = x.shape
    taken = pair if pick is None else 1
    pick = jnp.zeros((1,), jnp.int32) if pick is None else pick.astype(jnp.int32).reshape(1)
    vmem = pl.BlockSpec(memory_space=pltpu.VMEM)
    operands = [x, *weights] if add is None else [x, *weights, add]
    rows = blocks * taken * tokens
    columns = weights[0].shape[1] * len(weights)
    return pl.pallas_call(
        functools.partial(product_kernel, tile, len(weights)),
        out_shape=jax.ShapeDtypeStruct((blocks, taken, tokens, columns), bf16),
        in_specs=[pl.BlockSpec(memory_space=pltpu.SMEM)] + [vmem] * len(operands),
        out_specs=vmem,
        compiler_params=pltpu.CompilerParams(vmem_limit_bytes=20 * 1024 * 1024),
        cost_estimate=pl.CostEstimate(
            flops=2 * rows * inputs * columns,
            bytes_accessed=2 * (rows * inputs + inputs * columns + rows * columns),
            transcendentals=0,
        ),
    )(pick, *operands)


VMEM = pl.BlockSpec(memory_space=pltpu.VMEM)
SMEM = pl.BlockSpec(memory_space=pltpu.SMEM)


def small_call(kernel, outs, scalars, arrays, moved):
    return pl.pallas_call(
        kernel,
        out_shape=outs,
        in_specs=[SMEM] * len(scalars) + [VMEM] * len(arrays),
        out_specs=jax.tree.map(lambda _: VMEM, outs),
        compiler_params=pltpu.CompilerParams(vmem_limit_bytes=16 * 1024 * 1024),
        cost_estimate=pl.CostEstimate(flops=moved, bytes_accessed=moved, transcendentals=0),
    )(*scalars, *arrays)


def columns_kernel(place_ref, mine_ref, theirs_ref, gate_ref, up_ref, *out_refs):
    y, side = place_ref[0], place_ref[1]
    n = mine_ref.shape[2]
    x = jnp.concatenate(
        [ref[(y + i) % 4, s] for s in (1 - side, side) for i in range(4) for ref in (mine_ref, theirs_ref)],
        axis=0,
    )
    step = pl.program_id(0)

    def put(weight_ref):
        total = jnp.dot(x, weight_ref[...], preferred_element_type=f32).astype(bf16)
        for i, ref in enumerate(out_refs):
            ref[...] = total[i * n : (i + 1) * n]

    half = pl.num_programs(0) // 2
    pl.when(step < half)(functools.partial(put, gate_ref))
    pl.when(step >= half)(functools.partial(put, up_ref))


def partial_columns(place, mine, theirs, gate, up):
    tile = 896
    inputs, width = gate.shape
    count = width // tile
    tokens = mine.shape[2]
    whole = pl.BlockSpec(mine.shape, lambda n, p: (0, 0, 0, 0))
    rows = 16 * tokens
    return pl.pallas_call(
        columns_kernel,
        out_shape=(jax.ShapeDtypeStruct((tokens, 2 * width), bf16),) * 16,
        grid_spec=pltpu.PrefetchScalarGridSpec(
            num_scalar_prefetch=1,
            grid=(2 * count,),
            in_specs=[
                whole,
                whole,
                pl.BlockSpec((inputs, tile), lambda n, p: (0, jnp.minimum(n, count - 1))),
                pl.BlockSpec((inputs, tile), lambda n, p: (0, jnp.maximum(n - count, 0))),
            ],
            out_specs=(pl.BlockSpec((tokens, tile), lambda n, p: (0, n)),) * 16,
        ),
        compiler_params=pltpu.CompilerParams(vmem_limit_bytes=60 * 1024 * 1024),
        cost_estimate=pl.CostEstimate(
            flops=4 * rows * inputs * width,
            bytes_accessed=2 * (rows * inputs + 2 * inputs * width + 2 * rows * width),
            transcendentals=0,
        ),
    )(place, mine, theirs, gate, up)


def add_pieces(*pieces):
    def kernel(*refs):
        refs[-1][...] = sum(r[...].astype(f32) for r in refs[:-1]).astype(bf16)

    first = pieces[0]
    return small_call(kernel, jax.ShapeDtypeStruct(first.shape, bf16), (), pieces, 2 * first.size)


def add_halves(*halves):
    count = len(halves[0])

    def kernel(*refs):
        for i in range(len(halves)):
            mine = refs[i * count : (i + 1) * count]
            refs[-1][i] = sum(r[...].astype(f32) for r in mine).astype(bf16)

    first = halves[0][0]
    out = jax.ShapeDtypeStruct((len(halves), *first.shape), bf16)
    return small_call(kernel, out, (), [p for h in halves for p in h], 8 * first.size)


def gated(halves, got, factor):
    count = len(halves[0])
    tokens, width = halves[0][0].shape[0], halves[0][0].shape[1] // 2

    def kernel(*refs):
        got_ref, factor_ref, out_ref = refs[-3:]
        for i in range(len(halves)):
            rows = pl.ds(i * tokens, tokens)
            mine = refs[i * count : (i + 1) * count]
            scale = factor_ref[rows, :]

            def total(columns):
                parts = sum(r[:, columns].astype(f32) for r in mine)
                return (parts + got_ref[i, :, columns].astype(f32)) * scale

            gate = total(slice(0, width))
            up = total(slice(width, 2 * width))
            out_ref[rows, :] = (gate / (1.0 + jnp.exp(-gate)) * up).astype(bf16)

    out = jax.ShapeDtypeStruct((tokens * len(halves), width), bf16)
    arrays = [p for h in halves for p in h] + [got, factor[:, None]]
    return small_call(kernel, out, (), arrays, 16 * tokens * width)


def down_kernel(tile, place_ref, *refs):
    y, side = place_ref[0], place_ref[1]
    pieces, weight_ref, add_ref, out_ref = refs[:8], refs[8], refs[9:-1], refs[-1]
    n = pieces[0].shape[0]
    x = jnp.concatenate([p[...] for p in pieces], axis=0)
    total = jnp.dot(x, weight_ref[...], preferred_element_type=f32)
    for i in range(4):
        for j in range(2):
            at = 2 * ((y + i) % 4) + (side if j == 0 else 1 - side)
            part = total[(2 * i + j) * n : (2 * i + j + 1) * n]
            if add_ref:
                part = part + add_ref[0][at].astype(f32)
            out_ref[at] = part.astype(bf16)


def down_product(place, pieces, half, weight, add=None):
    tile = 256
    tokens, inputs = pieces[0].shape[0] // 2, pieces[0].shape[1]
    width = weight.shape[1]
    piece = pl.BlockSpec((tokens, inputs), lambda n, p: (half, 0))
    by_column = pl.BlockSpec((8, tokens, tile), lambda n, p: (0, 0, n))
    operands = [*pieces, weight] + ([] if add is None else [add])
    specs = [piece] * 8 + [pl.BlockSpec((inputs, tile), lambda n, p: (0, n))]
    specs += [] if add is None else [by_column]
    return pl.pallas_call(
        functools.partial(down_kernel, tile),
        out_shape=jax.ShapeDtypeStruct((8, tokens, width), bf16),
        grid_spec=pltpu.PrefetchScalarGridSpec(
            num_scalar_prefetch=1, grid=(width // tile,), in_specs=specs, out_specs=by_column
        ),
        compiler_params=pltpu.CompilerParams(vmem_limit_bytes=20 * 1024 * 1024),
        cost_estimate=pl.CostEstimate(
            flops=16 * tokens * inputs * width,
            bytes_accessed=2 * (8 * tokens * inputs + inputs * width + 8 * tokens * width),
            transcendentals=0,
        ),
    )(place, *operands)


def to_right(x):
    return lax.ppermute(x, "y", [(i, (i + 1) % 4) for i in range(4)])


def to_left(x):
    return lax.ppermute(x, "y", [(i, (i + 3) % 4) for i in range(4)])


def ring_start(pieces):
    right, left, opposite = pieces[2:4], pieces[6:8], pieces[4:6]
    return to_right(opposite[0]), to_left(opposite[1]), to_right(right[1]), to_left(left[0])


def ring_middle(pieces, from_left, from_right):
    return add_pieces(pieces[2], from_left), add_pieces(pieces[7], from_right)


def ring_end(pieces, arrived, sums):
    third_left, third_right = to_right(sums[0]), to_left(sums[1])
    return (pieces[0], arrived[3], third_left), (pieces[1], arrived[2], third_right)


def gather_start(mine):
    return to_right(mine), to_left(mine)


def gather_middle(got, mine_left):
    return to_right(got), to_left(got), to_right(mine_left)


def gather_end(mine, got, mine_left, mine_right, got_left, got_right, mine_far):
    return mine, got, mine_right, got_right, mine_far, to_left(got_right), mine_left, got_left


def exchange(x, axes):
    return lax.all_to_all(x, axes, split_axis=0, concat_axis=0, tiled=True)


def swap(x, axis="core"):
    return lax.ppermute(x, axis, [(0, 1), (1, 0)])


def spread(x, copies):
    return jnp.broadcast_to(x[None], (copies,) + x.shape)


def take(x, index, axis):
    return lax.dynamic_index_in_dim(x, index, axis, keepdims=False)


def local(
    queries,
    cache_keys,
    cache_values,
    stretch_keys,
    stretch_values,
    block_lists,
    out_weight,
    residual,
    norm_gain,
    gate_weight,
    up_weight,
    down_weight,
):
    core = lax.axis_index("core")
    side = lax.axis_index("xl")
    col = lax.axis_index(COL)
    group = lax.axis_index(ZXH)
    me = lax.axis_index(ROW) * 8 + col
    local_blocks = cache_keys.shape[1] // BLK
    tokens_here = residual.shape[0]

    matched = block_lists // local_blocks == me
    within = jnp.sum(jnp.where(matched, block_lists % local_blocks, 0), axis=2)
    source = (jnp.arange(KV_HEADS, dtype=jnp.int32)[:, None] * local_blocks + within.T).reshape(-1)

    piece = BLK // 4
    flat_keys = cache_keys.reshape(4 * KV_HEADS * local_blocks, piece, HEAD_DIM)
    flat_values = cache_values.reshape(4 * KV_HEADS * local_blocks, piece, HEAD_DIM)

    def pick(flat, first, count):
        index = 4 * source[:, None] + jnp.arange(first, first + count, dtype=jnp.int32)[None, :]
        return flat[index].reshape(64, count * piece, HEAD_DIM)

    def near(stretch):
        part = BLK // 8
        rows = lax.dynamic_slice_in_dim(stretch, group * part, part, 1)
        return jnp.broadcast_to(rows[:, None], (KV_HEADS, 8, part, HEAD_DIM)).reshape(64, part, HEAD_DIM)

    first = [pick(flat_keys, 0, 3), pick(flat_values, 0, 3), near(stretch_keys), near(stretch_values)]
    first = exchange(jnp.concatenate(first, axis=1), CHIP)
    second = [pick(flat_keys, 3, 1), pick(flat_values, 3, 1)]
    second = exchange(jnp.concatenate(second, axis=1), CHIP)
    my_list = block_lists[col, group]
    place = jnp.stack([core, col]).astype(jnp.int32)
    other_queries = swap(queries)
    own, send, order = attend((my_list, place), queries, other_queries, first, (), local_blocks, 5)
    own, send = attend((order,), queries, other_queries, second, (own, send), local_blocks, 16)
    attended = exchange(merge(own, swap(send), 8), COL).reshape(8, 2, tokens_here, -1)

    def row_sum(give, mine, pick, weight):
        both = product(mine, (weight,), 512, pick, add=swap(give))
        return jnp.sum(exchange(both.reshape(8, tokens_here, -1), ZXH).astype(f32), axis=0)

    give = product(attended, (out_weight,), 512, 1 - core)
    stream = residual.astype(f32) + row_sum(give, attended, core, out_weight)
    gain = norm_gain.astype(f32)[None, :]
    own_rows = exchange(spread((stream * gain).astype(bf16), 8), ZXH)
    other_rows = swap(own_rows)

    def squares(x):
        plain = x.astype(f32) / gain[None]
        return jnp.sum(plain * plain, axis=2)

    squares = jnp.stack([squares(own_rows), squares(other_rows)], axis=1)

    by_pair = (4, 2, tokens_here, own_rows.shape[-1])
    where = jnp.stack([lax.axis_index("y"), side]).astype(jnp.int32)
    columns = partial_columns(
        where, own_rows.reshape(by_pair), other_rows.reshape(by_pair), gate_weight, up_weight
    )
    theirs, mine = columns[:8], columns[8:]
    arrived = ring_start(theirs)
    sums = ring_middle(theirs, *arrived[:2])
    sums, mine, squares = lax.optimization_barrier((sums, mine, squares))
    squares = exchange(squares, COL)
    halves = ring_end(theirs, arrived, sums)
    mine_arrived = ring_start(mine)
    halves, squares = lax.optimization_barrier((halves, squares))
    got = swap(add_halves(*halves), "xl")
    factor = lax.rsqrt(jnp.sum(squares, axis=0).reshape(-1) / D + 1e-05)
    halves = ring_end(mine, mine_arrived, ring_middle(mine, *mine_arrived[:2]))
    hidden = gated(halves, got, factor)
    hidden_got = swap(hidden, "xl")
    first = gather_start(hidden)
    pieces = gather_end(hidden, hidden_got, *first, *gather_middle(hidden_got, first[0]))
    given = down_product(where, pieces, 1, down_weight)
    down = down_product(where, pieces, 0, down_weight, add=swap(given))
    mlp = jnp.sum(exchange(down, ZXH).astype(f32), axis=0)
    return (stream + mlp).astype(bf16)


def solution(mesh):
    mesh = Mesh(mesh.devices.reshape(4, 2, 2, 4, 2), AXES)
    in_specs = (
        P(COL, ROW),
        P(None, ROW + COL, None),
        P(None, ROW + COL, None),
        P(None, COL, None),
        P(None, COL, None),
        P(),
        P(ROW, COL),
        P(ROW, COL),
        P(COL),
        P(COL, ROW),
        P(COL, ROW),
        P(ROW, COL),
    )
    return jax.shard_map(local, mesh=mesh, in_specs=in_specs, out_specs=P(ROW, COL), check_vma=False)
```

```python
import functools
import math

import jax
import jax.numpy as jnp
from jax import lax
from jax.experimental import pallas as pl
from jax.experimental.pallas import tpu as pltpu
from jax.sharding import Mesh, PartitionSpec as P

D = 8192
KV_HEADS = 8
HEAD_DIM = 128
BLK = 128
GROUP = 8
AXES = ("z", "xh", "core", "y", "xl")
ROW = ("z", "xh", "core")
ZXH = ("z", "xh")
COL = ("y", "xl")
CHIP = ("z", "xh", "y", "xl")
NEG = -1e30
bf16 = jnp.bfloat16
f32 = jnp.float32


def nt_dot(a, b):
    return lax.dot_general(a, b, (((1,), (1,)), ((), ())), preferred_element_type=f32)


def tn_dot(a, b):
    return lax.dot_general(a, b, (((0,), (0,)), ((), ())), preferred_element_type=f32)


def attend_kernel(scale, per_step, local_blocks, last, *refs):
    if last:
        order_ref, own_q_ref, other_q_ref, chunk_ref, own_in_ref, send_in_ref = refs[:6]
    else:
        list_ref, place_ref, own_q_ref, other_q_ref, chunk_ref = refs[:5]
        order_ref = refs[7]
    own_ref, send_ref = refs[6:8] if last else refs[5:7]
    q_ref, top_ref, sum_ref, acc_ref = refs[-4:]
    length = order_ref.shape[0] - 1
    part_rows = (chunk_ref.shape[1] - (0 if last else BLK // 4)) // 2
    heads = own_q_ref.shape[1] // HEAD_DIM
    rows = heads * BLK
    for h in range(heads):
        cols = pl.ds(h * HEAD_DIM, HEAD_DIM)
        q_ref[pl.ds(h * BLK, BLK), :] = own_q_ref[:, cols]
        q_ref[pl.ds(rows + h * BLK, BLK), :] = other_q_ref[:, cols]
    if last:
        for half, ref in ((0, own_in_ref), (1, send_in_ref)):
            acc_ref[half] = ref[0:HEAD_DIM, :]
            top_ref[half] = ref[HEAD_DIM : HEAD_DIM + 1, :]
            sum_ref[half] = ref[HEAD_DIM + 1 : HEAD_DIM + 2, :]
        count = order_ref[length]
    else:
        core = place_ref[0]
        block = place_ref[1]
        top_ref[...] = jnp.full_like(top_ref, NEG)
        sum_ref[...] = jnp.zeros_like(sum_ref)
        acc_ref[...] = jnp.zeros_like(acc_ref)

        def collect(i, count):
            device = list_ref[i] // local_blocks
            row = device // 8
            order_ref[count] = (row // 2) * 8 + device % 8
            return count + jnp.where(row % 2 == core, 1, 0)

        count = lax.fori_loop(0, length, collect, jnp.int32(0))
        order_ref[length] = count

    def update(half, keys, values, bias):
        part = pl.ds(half * rows, rows)
        scores = nt_dot(keys, q_ref[part, :]) * scale + bias
        old = top_ref[half]
        new = jnp.maximum(old, jnp.max(scores, axis=0, keepdims=True))
        weights = jnp.exp2(scores - new)
        decay = jnp.exp2(old - new)
        top_ref[half] = new
        sum_ref[half] = sum_ref[half] * decay + jnp.sum(weights, axis=0, keepdims=True)
        acc_ref[half] = acc_ref[half] * decay + tn_dot(values, weights.astype(bf16))

    def far(step, carry):
        slots = [order_ref[jnp.minimum(step * per_step + i, count - 1)] for i in range(per_step)]
        keys = jnp.concatenate([chunk_ref[s, 0:part_rows] for s in slots], axis=0)
        values = jnp.concatenate([chunk_ref[s, part_rows : 2 * part_rows] for s in slots], axis=0)
        bias = jnp.concatenate(
            [
                jnp.full((part_rows, 1), jnp.where(step * per_step + i < count, 0.0, NEG), f32)
                for i in range(per_step)
            ],
            axis=0,
        )
        for half in range(2):
            update(half, keys, values, bias)
        return carry

    lax.fori_loop(0, (count + per_step - 1) // per_step, far, 0)

    def near(j, carry):
        which = core + 2 * j
        shift = (block - which) * BLK
        key_pos = lax.broadcasted_iota(jnp.int32, (BLK, rows), 0)
        token = lax.broadcasted_iota(jnp.int32, (BLK, rows), 1) % BLK
        bias = jnp.where(key_pos <= token + shift, 0.0, NEG)
        at = 2 * part_rows
        eighth = BLK // 8
        keys = jnp.concatenate([chunk_ref[i * 8 + which, at : at + eighth] for i in range(8)], axis=0)
        values = jnp.concatenate([chunk_ref[i * 8 + which, at + eighth :] for i in range(8)], axis=0)
        for half in range(2):
            update(half, keys, values, bias)
        return carry

    if not last:
        lax.fori_loop(0, (block - core + 2) // 2, near, 0)
    for half, ref in ((0, own_ref), (1, send_ref)):
        ref[0:HEAD_DIM, :] = acc_ref[half]
        ref[HEAD_DIM : HEAD_DIM + 1, :] = top_ref[half]
        ref[HEAD_DIM + 1 : HEAD_DIM + 2, :] = sum_ref[half]


def attend(scalars, own_q, other_q, chunk, state, local_blocks, per_step):
    heads = own_q.shape[1] // HEAD_DIM
    rows = heads * BLK
    length = scalars[0].shape[0] - len(state) // 2
    packed = jax.ShapeDtypeStruct((HEAD_DIM + 8, rows), f32)
    smem = pl.BlockSpec(memory_space=pltpu.SMEM)
    vmem = pl.BlockSpec(memory_space=pltpu.VMEM)
    scale = math.log2(math.e) / math.sqrt(HEAD_DIM)
    arrays = [own_q, other_q, chunk, *state]
    outs = [packed, packed]
    if not state:
        outs.append(jax.ShapeDtypeStruct((length + 1,), jnp.int32))
    return pl.pallas_call(
        functools.partial(attend_kernel, scale, per_step, local_blocks, len(state) > 0),
        out_shape=outs,
        in_specs=[smem] * len(scalars) + [vmem] * len(arrays),
        out_specs=[vmem, vmem, smem][: len(outs)],
        scratch_shapes=[
            pltpu.VMEM((2 * rows, HEAD_DIM), bf16),
            pltpu.VMEM((2, 1, rows), f32),
            pltpu.VMEM((2, 1, rows), f32),
            pltpu.VMEM((2, HEAD_DIM, rows), f32),
        ],
        compiler_params=pltpu.CompilerParams(vmem_limit_bytes=24 * 1024 * 1024),
        cost_estimate=pl.CostEstimate(
            flops=2 * rows * 40 * chunk.shape[1] * HEAD_DIM,
            bytes_accessed=2 * chunk.size,
            transcendentals=rows * 40 * chunk.shape[1],
        ),
    )(*scalars, *arrays)


def merge_kernel(own_ref, got_ref, out_ref):
    own_top = own_ref[HEAD_DIM : HEAD_DIM + 1, :]
    got_top = got_ref[HEAD_DIM : HEAD_DIM + 1, :]
    top = jnp.maximum(own_top, got_top)
    own_w = jnp.exp2(own_top - top)
    got_w = jnp.exp2(got_top - top)
    total = own_w * own_ref[HEAD_DIM + 1 : HEAD_DIM + 2, :] + got_w * got_ref[HEAD_DIM + 1 : HEAD_DIM + 2, :]
    mixed = (own_ref[0:HEAD_DIM, :] * own_w + got_ref[0:HEAD_DIM, :] * got_w) / total
    heads = mixed.shape[1] // BLK
    for h in range(heads):
        piece = mixed[:, h * BLK : (h + 1) * BLK].T.astype(bf16)
        for i in range(out_ref.shape[0]):
            out_ref[i, :, pl.ds(h * HEAD_DIM, HEAD_DIM)] = piece


def merge(own, got, copies):
    heads = own.shape[1] // BLK
    vmem = pl.BlockSpec(memory_space=pltpu.VMEM)
    return pl.pallas_call(
        merge_kernel,
        out_shape=jax.ShapeDtypeStruct((copies, BLK, heads * HEAD_DIM), bf16),
        in_specs=[vmem, vmem],
        out_specs=vmem,
        compiler_params=pltpu.CompilerParams(vmem_limit_bytes=12 * 1024 * 1024),
    )(own, got)


def product_kernel(tile, weight_count, pick_ref, x_ref, *refs):
    weight_refs, add_ref, out_ref = refs[:weight_count], refs[weight_count:-1], refs[-1]
    x = x_ref[:, pick_ref[0]] if x_ref.shape[1] > out_ref.shape[1] else x_ref[...]
    x = x.reshape(-1, x.shape[-1])
    width = weight_refs[0].shape[1]
    block = out_ref.shape[:-1] + (tile,)
    for i, weight_ref in enumerate(weight_refs):
        for first in range(0, width, tile):
            total = jnp.dot(x, weight_ref[:, first : first + tile], preferred_element_type=f32)
            columns = slice(i * width + first, i * width + first + tile)
            if add_ref:
                total = total + add_ref[0][..., columns].reshape(total.shape).astype(f32)
            out_ref[..., columns] = total.astype(bf16).reshape(block)


def product(x, weights, tile, pick=None, add=None):
    blocks, pair, tokens, inputs = x.shape
    taken = pair if pick is None else 1
    pick = jnp.zeros((1,), jnp.int32) if pick is None else pick.astype(jnp.int32).reshape(1)
    vmem = pl.BlockSpec(memory_space=pltpu.VMEM)
    operands = [x, *weights] if add is None else [x, *weights, add]
    rows = blocks * taken * tokens
    columns = weights[0].shape[1] * len(weights)
    return pl.pallas_call(
        functools.partial(product_kernel, tile, len(weights)),
        out_shape=jax.ShapeDtypeStruct((blocks, taken, tokens, columns), bf16),
        in_specs=[pl.BlockSpec(memory_space=pltpu.SMEM)] + [vmem] * len(operands),
        out_specs=vmem,
        compiler_params=pltpu.CompilerParams(vmem_limit_bytes=20 * 1024 * 1024),
        cost_estimate=pl.CostEstimate(
            flops=2 * rows * inputs * columns,
            bytes_accessed=2 * (rows * inputs + inputs * columns + rows * columns),
            transcendentals=0,
        ),
    )(pick, *operands)


VMEM = pl.BlockSpec(memory_space=pltpu.VMEM)
SMEM = pl.BlockSpec(memory_space=pltpu.SMEM)


def small_call(kernel, outs, scalars, arrays, moved):
    return pl.pallas_call(
        kernel,
        out_shape=outs,
        in_specs=[SMEM] * len(scalars) + [VMEM] * len(arrays),
        out_specs=jax.tree.map(lambda _: VMEM, outs),
        compiler_params=pltpu.CompilerParams(vmem_limit_bytes=16 * 1024 * 1024),
        cost_estimate=pl.CostEstimate(flops=moved, bytes_accessed=moved, transcendentals=0),
    )(*scalars, *arrays)


def columns_kernel(place_ref, mine_ref, theirs_ref, gate_ref, up_ref, *out_refs):
    y, side = place_ref[0], place_ref[1]
    n = mine_ref.shape[2]
    x = jnp.concatenate(
        [ref[(y + i) % 4, s] for s in (1 - side, side) for i in range(4) for ref in (mine_ref, theirs_ref)],
        axis=0,
    )
    step = pl.program_id(0)

    def put(weight_ref):
        total = jnp.dot(x, weight_ref[...], preferred_element_type=f32).astype(bf16)
        for i, ref in enumerate(out_refs):
            ref[...] = total[i * n : (i + 1) * n]

    half = pl.num_programs(0) // 2
    pl.when(step < half)(functools.partial(put, gate_ref))
    pl.when(step >= half)(functools.partial(put, up_ref))


def partial_columns(place, mine, theirs, gate, up):
    tile = 896
    inputs, width = gate.shape
    count = width // tile
    tokens = mine.shape[2]
    whole = pl.BlockSpec(mine.shape, lambda n, p: (0, 0, 0, 0))
    rows = 16 * tokens
    return pl.pallas_call(
        columns_kernel,
        out_shape=(jax.ShapeDtypeStruct((tokens, 2 * width), bf16),) * 16,
        grid_spec=pltpu.PrefetchScalarGridSpec(
            num_scalar_prefetch=1,
            grid=(2 * count,),
            in_specs=[
                whole,
                whole,
                pl.BlockSpec((inputs, tile), lambda n, p: (0, jnp.minimum(n, count - 1))),
                pl.BlockSpec((inputs, tile), lambda n, p: (0, jnp.maximum(n - count, 0))),
            ],
            out_specs=(pl.BlockSpec((tokens, tile), lambda n, p: (0, n)),) * 16,
        ),
        compiler_params=pltpu.CompilerParams(vmem_limit_bytes=60 * 1024 * 1024),
        cost_estimate=pl.CostEstimate(
            flops=4 * rows * inputs * width,
            bytes_accessed=2 * (rows * inputs + 2 * inputs * width + 2 * rows * width),
            transcendentals=0,
        ),
    )(place, mine, theirs, gate, up)


def add_pieces(*pieces):
    def kernel(*refs):
        refs[-1][...] = sum(r[...].astype(f32) for r in refs[:-1]).astype(bf16)

    first = pieces[0]
    return small_call(kernel, jax.ShapeDtypeStruct(first.shape, bf16), (), pieces, 2 * first.size)


def add_halves(*halves):
    count = len(halves[0])

    def kernel(*refs):
        for i in range(len(halves)):
            mine = refs[i * count : (i + 1) * count]
            refs[-1][i] = sum(r[...].astype(f32) for r in mine).astype(bf16)

    first = halves[0][0]
    out = jax.ShapeDtypeStruct((len(halves), *first.shape), bf16)
    return small_call(kernel, out, (), [p for h in halves for p in h], 8 * first.size)


def gated(halves, got, factor):
    count = len(halves[0])
    tokens, width = halves[0][0].shape[0], halves[0][0].shape[1] // 2

    def kernel(*refs):
        got_ref, factor_ref, out_ref = refs[-3:]
        for i in range(len(halves)):
            rows = pl.ds(i * tokens, tokens)
            mine = refs[i * count : (i + 1) * count]
            scale = factor_ref[rows, :]

            def total(columns):
                parts = sum(r[:, columns].astype(f32) for r in mine)
                return (parts + got_ref[i, :, columns].astype(f32)) * scale

            gate = total(slice(0, width))
            up = total(slice(width, 2 * width))
            out_ref[rows, :] = (gate / (1.0 + jnp.exp(-gate)) * up).astype(bf16)

    out = jax.ShapeDtypeStruct((tokens * len(halves), width), bf16)
    arrays = [p for h in halves for p in h] + [got, factor[:, None]]
    return small_call(kernel, out, (), arrays, 16 * tokens * width)


def down_product(pieces, weight):
    tile = 512
    count, tokens, inputs = len(pieces), pieces[0].shape[0] // 2, pieces[0].shape[1]
    width = weight.shape[1]

    def kernel(*refs):
        weight_ref, keep_ref, give_ref = refs[count:]
        x = jnp.concatenate([p[...] for p in refs[:count]], axis=0)
        total = jnp.dot(x, weight_ref[...], preferred_element_type=f32)
        for i in range(count):
            at = 2 * i * tokens
            keep_ref[i] = total[at : at + tokens]
            give_ref[i] = total[at + tokens : at + 2 * tokens].astype(bf16)

    by_column = pl.BlockSpec((count, tokens, tile), lambda n: (0, 0, n))
    specs = [pl.BlockSpec((2 * tokens, inputs), lambda n: (0, 0))] * count
    return pl.pallas_call(
        kernel,
        grid=(width // tile,),
        out_shape=(
            jax.ShapeDtypeStruct((count, tokens, width), f32),
            jax.ShapeDtypeStruct((count, tokens, width), bf16),
        ),
        in_specs=specs + [pl.BlockSpec((inputs, tile), lambda n: (0, n))],
        out_specs=(by_column, by_column),
        compiler_params=pltpu.CompilerParams(vmem_limit_bytes=24 * 1024 * 1024),
        cost_estimate=pl.CostEstimate(
            flops=4 * count * tokens * inputs * width,
            bytes_accessed=2 * (2 * count * tokens * inputs + inputs * width + 3 * count * tokens * width),
            transcendentals=0,
        ),
    )(*pieces, weight)


def join_blocks(place, near, far):
    def kernel(place_ref, near_ref, near_got_ref, far_ref, far_got_ref, out_ref):
        y, side = place_ref[0], place_ref[1]
        for i, (kept_ref, got_ref, first) in enumerate(
            (
                (near_ref, near_got_ref, 0),
                (near_ref, near_got_ref, 2),
                (far_ref, far_got_ref, 0),
                (near_ref, near_got_ref, 4),
            )
        ):
            for j in range(2):
                at = 2 * ((y + i) % 4) + (side if j == 0 else 1 - side)
                out_ref[at] = (kept_ref[first + j] + got_ref[first + j].astype(f32)).astype(bf16)

    out = jax.ShapeDtypeStruct((8, *near[0].shape[1:]), bf16)
    return small_call(kernel, out, (place,), (*near, *far), 4 * near[0].size)


def to_right(x):
    return lax.ppermute(x, "y", [(i, (i + 1) % 4) for i in range(4)])


def to_left(x):
    return lax.ppermute(x, "y", [(i, (i + 3) % 4) for i in range(4)])


def ring_start(pieces):
    right, left, opposite = pieces[2:4], pieces[6:8], pieces[4:6]
    return to_right(opposite[0]), to_left(opposite[1]), to_right(right[1]), to_left(left[0])


def ring_middle(pieces, from_left, from_right):
    return add_pieces(pieces[2], from_left), add_pieces(pieces[7], from_right)


def ring_end(pieces, arrived, sums):
    third_left, third_right = to_right(sums[0]), to_left(sums[1])
    return (pieces[0], arrived[3], third_left), (pieces[1], arrived[2], third_right)


def gather_start(mine):
    return to_right(mine), to_left(mine)


def pack_kernel(within_ref, group_ref, keys_ref, values_ref, near_keys_ref, near_values_ref, out_ref):
    eighth = BLK // 8
    rows = (out_ref.shape[1] - 2 * eighth) // 2
    goal = pl.program_id(0)
    near = pl.ds(pl.multiple_of(group_ref[0] * eighth, eighth), eighth)
    for i in range(out_ref.shape[0]):
        at = within_ref[goal, i]
        out_ref[i, 0:rows] = keys_ref[at, 0:rows]
        out_ref[i, rows : 2 * rows] = values_ref[at, 0:rows]
        out_ref[i, 2 * rows : 2 * rows + eighth] = near_keys_ref[0, near]
        out_ref[i, 2 * rows + eighth :] = near_values_ref[0, near]


def pack(within, group, keys, values, near_keys, near_values, rows):
    def of_group(x):
        return pl.BlockSpec((x.shape[0] // KV_HEADS, *x.shape[1:]), lambda n, s, g: (n, 0, 0))

    arrays = (keys, values, near_keys, near_values)
    height = 2 * rows + BLK // 4
    return pl.pallas_call(
        pack_kernel,
        out_shape=jax.ShapeDtypeStruct((64, height, HEAD_DIM), bf16),
        grid_spec=pltpu.PrefetchScalarGridSpec(
            num_scalar_prefetch=2,
            grid=(8,),
            in_specs=[of_group(x) for x in arrays],
            out_specs=pl.BlockSpec((8, height, HEAD_DIM), lambda n, s, g: (n, 0, 0)),
        ),
        compiler_params=pltpu.CompilerParams(vmem_limit_bytes=60 * 1024 * 1024),
        cost_estimate=pl.CostEstimate(flops=0, bytes_accessed=64 * height * 512, transcendentals=0),
    )(within, group.astype(jnp.int32).reshape(1), *arrays)


def exchange(x, axes):
    return lax.all_to_all(x, axes, split_axis=0, concat_axis=0, tiled=True)


def swap(x, axis="core"):
    return lax.ppermute(x, axis, [(0, 1), (1, 0)])


def spread(x, copies):
    return jnp.broadcast_to(x[None], (copies,) + x.shape)


def take(x, index, axis):
    return lax.dynamic_index_in_dim(x, index, axis, keepdims=False)


def local(
    queries,
    cache_keys,
    cache_values,
    stretch_keys,
    stretch_values,
    block_lists,
    out_weight,
    residual,
    norm_gain,
    gate_weight,
    up_weight,
    down_weight,
):
    core = lax.axis_index("core")
    side = lax.axis_index("xl")
    col = lax.axis_index(COL)
    group = lax.axis_index(ZXH)
    me = lax.axis_index(ROW) * 8 + col
    local_blocks = cache_keys.shape[1] // BLK
    tokens_here = residual.shape[0]

    matched = block_lists // local_blocks == me
    within = jnp.sum(jnp.where(matched, block_lists % local_blocks, 0), axis=2)
    source = (jnp.arange(KV_HEADS, dtype=jnp.int32)[:, None] * local_blocks + within.T).reshape(-1)

    piece = BLK // 4
    flat_keys = cache_keys.reshape(4 * KV_HEADS * local_blocks, piece, HEAD_DIM)
    flat_values = cache_values.reshape(4 * KV_HEADS * local_blocks, piece, HEAD_DIM)

    def pick(flat, first, count):
        index = 4 * source[:, None] + jnp.arange(first, first + count, dtype=jnp.int32)[None, :]
        return flat[index].reshape(64, count * piece, HEAD_DIM)

    blocked = (KV_HEADS * local_blocks, BLK, HEAD_DIM)
    first = pack(
        within.T, group, cache_keys.reshape(blocked), cache_values.reshape(blocked),
        stretch_keys, stretch_values, 3 * piece,
    )
    first = exchange(first, CHIP)
    second = [pick(flat_keys, 3, 1), pick(flat_values, 3, 1)]
    second = exchange(jnp.concatenate(second, axis=1), CHIP)
    my_list = block_lists[col, group]
    place = jnp.stack([core, col]).astype(jnp.int32)
    other_queries = swap(queries)
    own, send, order = attend((my_list, place), queries, other_queries, first, (), local_blocks, 5)
    own, send = attend((order,), queries, other_queries, second, (own, send), local_blocks, 16)
    attended = exchange(merge(own, swap(send), 8), COL).reshape(8, 2, tokens_here, -1)

    def row_sum(give, mine, pick, weight):
        both = product(mine, (weight,), 512, pick, add=swap(give))
        return jnp.sum(exchange(both.reshape(8, tokens_here, -1), ZXH).astype(f32), axis=0)

    give = product(attended, (out_weight,), 512, 1 - core)
    stream = residual.astype(f32) + row_sum(give, attended, core, out_weight)
    gain = norm_gain.astype(f32)[None, :]
    own_rows = exchange(spread((stream * gain).astype(bf16), 8), ZXH)
    other_rows = swap(own_rows)

    def squares(x):
        plain = x.astype(f32) / gain[None]
        return jnp.sum(plain * plain, axis=2)

    squares = jnp.stack([squares(own_rows), squares(other_rows)], axis=1)

    by_pair = (4, 2, tokens_here, own_rows.shape[-1])
    where = jnp.stack([lax.axis_index("y"), side]).astype(jnp.int32)
    columns = partial_columns(
        where, own_rows.reshape(by_pair), other_rows.reshape(by_pair), gate_weight, up_weight
    )
    theirs, mine = columns[:8], columns[8:]
    arrived = ring_start(theirs)
    sums = ring_middle(theirs, *arrived[:2])
    sums, mine, squares = lax.optimization_barrier((sums, mine, squares))
    squares = exchange(squares, COL)
    halves = ring_end(theirs, arrived, sums)
    mine_arrived = ring_start(mine)
    halves, squares = lax.optimization_barrier((halves, squares))
    got = swap(add_halves(*halves), "xl")
    factor = lax.rsqrt(jnp.sum(squares, axis=0).reshape(-1) / D + 1e-05)
    halves = ring_end(mine, mine_arrived, ring_middle(mine, *mine_arrived[:2]))
    hidden = gated(halves, got, factor)
    first, hidden_got = lax.optimization_barrier((gather_start(hidden), swap(hidden, "xl")))
    got_left, got_right = to_right(hidden_got), to_left(hidden_got)
    mine_far = to_right(first[0])
    got_left, got_right, mine_far = lax.optimization_barrier((got_left, got_right, mine_far))
    got_far = to_left(got_right)
    near = (hidden, hidden_got, first[1], got_right, first[0], got_left)
    kept, give = down_product(near, down_weight)
    far_kept, far_give = down_product((mine_far, got_far), down_weight)
    down = join_blocks(where, (kept, swap(give)), (far_kept, swap(far_give)))
    mlp = jnp.sum(exchange(down, ZXH).astype(f32), axis=0)
    return (stream + mlp).astype(bf16)


def solution(mesh):
    mesh = Mesh(mesh.devices.reshape(4, 2, 2, 4, 2), AXES)
    in_specs = (
        P(COL, ROW),
        P(None, ROW + COL, None),
        P(None, ROW + COL, None),
        P(None, COL, None),
        P(None, COL, None),
        P(),
        P(ROW, COL),
        P(ROW, COL),
        P(COL),
        P(COL, ROW),
        P(COL, ROW),
        P(ROW, COL),
    )
    return jax.shard_map(local, mesh=mesh, in_specs=in_specs, out_specs=P(ROW, COL), check_vma=False)
```

```python
import functools
import math

import jax
import jax.numpy as jnp
from jax import lax
from jax.experimental import pallas as pl
from jax.experimental.pallas import tpu as pltpu
from jax.sharding import Mesh, PartitionSpec as P

D = 8192
KV_HEADS = 8
HEAD_DIM = 128
BLK = 128
GROUP = 8
AXES = ("z", "xh", "core", "y", "xl")
ROW = ("z", "xh", "core")
ZXH = ("z", "xh")
COL = ("y", "xl")
CHIP = ("z", "xh", "y", "xl")
NEG = -1e30
bf16 = jnp.bfloat16
f32 = jnp.float32


def nt_dot(a, b):
    return lax.dot_general(a, b, (((1,), (1,)), ((), ())), preferred_element_type=f32)


def tn_dot(a, b):
    return lax.dot_general(a, b, (((0,), (0,)), ((), ())), preferred_element_type=f32)


def attend_kernel(scale, per_step, local_blocks, last, *refs):
    if last:
        order_ref, own_q_ref, other_q_ref, chunk_ref, own_in_ref, send_in_ref = refs[:6]
    else:
        list_ref, place_ref, own_q_ref, other_q_ref, chunk_ref = refs[:5]
        order_ref = refs[7]
    own_ref, send_ref = refs[6:8] if last else refs[5:7]
    q_ref, top_ref, sum_ref, acc_ref = refs[-4:]
    length = order_ref.shape[0] - 1
    part_rows = (chunk_ref.shape[1] - (0 if last else BLK // 4)) // 2
    heads = own_q_ref.shape[1] // HEAD_DIM
    rows = heads * BLK
    for h in range(heads):
        cols = pl.ds(h * HEAD_DIM, HEAD_DIM)
        q_ref[pl.ds(h * BLK, BLK), :] = own_q_ref[:, cols]
        q_ref[pl.ds(rows + h * BLK, BLK), :] = other_q_ref[:, cols]
    if last:
        for half, ref in ((0, own_in_ref), (1, send_in_ref)):
            acc_ref[half] = ref[0:HEAD_DIM, :]
            top_ref[half] = ref[HEAD_DIM : HEAD_DIM + 1, :]
            sum_ref[half] = ref[HEAD_DIM + 1 : HEAD_DIM + 2, :]
        count = order_ref[length]
    else:
        core = place_ref[0]
        block = place_ref[1]
        top_ref[...] = jnp.full_like(top_ref, NEG)
        sum_ref[...] = jnp.zeros_like(sum_ref)
        acc_ref[...] = jnp.zeros_like(acc_ref)

        def collect(i, count):
            device = list_ref[i] // local_blocks
            row = device // 8
            order_ref[count] = (row // 2) * 8 + device % 8
            return count + jnp.where(row % 2 == core, 1, 0)

        count = lax.fori_loop(0, length, collect, jnp.int32(0))
        order_ref[length] = count

    def update(half, keys, values, bias):
        part = pl.ds(half * rows, rows)
        scores = nt_dot(keys, q_ref[part, :]) * scale + bias
        old = top_ref[half]
        new = jnp.maximum(old, jnp.max(scores, axis=0, keepdims=True))
        weights = jnp.exp2(scores - new)
        decay = jnp.exp2(old - new)
        top_ref[half] = new
        sum_ref[half] = sum_ref[half] * decay + jnp.sum(weights, axis=0, keepdims=True)
        acc_ref[half] = acc_ref[half] * decay + tn_dot(values, weights.astype(bf16))

    def far(step, carry):
        slots = [order_ref[jnp.minimum(step * per_step + i, count - 1)] for i in range(per_step)]
        keys = jnp.concatenate([chunk_ref[s, 0:part_rows] for s in slots], axis=0)
        values = jnp.concatenate([chunk_ref[s, part_rows : 2 * part_rows] for s in slots], axis=0)
        bias = jnp.concatenate(
            [
                jnp.full((part_rows, 1), jnp.where(step * per_step + i < count, 0.0, NEG), f32)
                for i in range(per_step)
            ],
            axis=0,
        )
        for half in range(2):
            update(half, keys, values, bias)
        return carry

    lax.fori_loop(0, (count + per_step - 1) // per_step, far, 0)

    def near(j, carry):
        which = core + 2 * j
        shift = (block - which) * BLK
        key_pos = lax.broadcasted_iota(jnp.int32, (BLK, rows), 0)
        token = lax.broadcasted_iota(jnp.int32, (BLK, rows), 1) % BLK
        bias = jnp.where(key_pos <= token + shift, 0.0, NEG)
        at = 2 * part_rows
        eighth = BLK // 8
        keys = jnp.concatenate([chunk_ref[i * 8 + which, at : at + eighth] for i in range(8)], axis=0)
        values = jnp.concatenate([chunk_ref[i * 8 + which, at + eighth :] for i in range(8)], axis=0)
        for half in range(2):
            update(half, keys, values, bias)
        return carry

    if not last:
        lax.fori_loop(0, (block - core + 2) // 2, near, 0)
    for half, ref in ((0, own_ref), (1, send_ref)):
        ref[0:HEAD_DIM, :] = acc_ref[half]
        ref[HEAD_DIM : HEAD_DIM + 1, :] = top_ref[half]
        ref[HEAD_DIM + 1 : HEAD_DIM + 2, :] = sum_ref[half]


def attend(scalars, own_q, other_q, chunk, state, local_blocks, per_step):
    heads = own_q.shape[1] // HEAD_DIM
    rows = heads * BLK
    length = scalars[0].shape[0] - len(state) // 2
    packed = jax.ShapeDtypeStruct((HEAD_DIM + 8, rows), f32)
    smem = pl.BlockSpec(memory_space=pltpu.SMEM)
    vmem = pl.BlockSpec(memory_space=pltpu.VMEM)
    scale = math.log2(math.e) / math.sqrt(HEAD_DIM)
    arrays = [own_q, other_q, chunk, *state]
    outs = [packed, packed]
    if not state:
        outs.append(jax.ShapeDtypeStruct((length + 1,), jnp.int32))
    return pl.pallas_call(
        functools.partial(attend_kernel, scale, per_step, local_blocks, len(state) > 0),
        out_shape=outs,
        in_specs=[smem] * len(scalars) + [vmem] * len(arrays),
        out_specs=[vmem, vmem, smem][: len(outs)],
        scratch_shapes=[
            pltpu.VMEM((2 * rows, HEAD_DIM), bf16),
            pltpu.VMEM((2, 1, rows), f32),
            pltpu.VMEM((2, 1, rows), f32),
            pltpu.VMEM((2, HEAD_DIM, rows), f32),
        ],
        compiler_params=pltpu.CompilerParams(vmem_limit_bytes=24 * 1024 * 1024),
        cost_estimate=pl.CostEstimate(
            flops=2 * rows * 40 * chunk.shape[1] * HEAD_DIM,
            bytes_accessed=2 * chunk.size,
            transcendentals=rows * 40 * chunk.shape[1],
        ),
    )(*scalars, *arrays)


def merge_kernel(own_ref, got_ref, out_ref):
    own_top = own_ref[HEAD_DIM : HEAD_DIM + 1, :]
    got_top = got_ref[HEAD_DIM : HEAD_DIM + 1, :]
    top = jnp.maximum(own_top, got_top)
    own_w = jnp.exp2(own_top - top)
    got_w = jnp.exp2(got_top - top)
    total = own_w * own_ref[HEAD_DIM + 1 : HEAD_DIM + 2, :] + got_w * got_ref[HEAD_DIM + 1 : HEAD_DIM + 2, :]
    mixed = (own_ref[0:HEAD_DIM, :] * own_w + got_ref[0:HEAD_DIM, :] * got_w) / total
    heads = mixed.shape[1] // BLK
    for h in range(heads):
        piece = mixed[:, h * BLK : (h + 1) * BLK].T.astype(bf16)
        for i in range(out_ref.shape[0]):
            out_ref[i, :, pl.ds(h * HEAD_DIM, HEAD_DIM)] = piece


def merge(own, got, copies):
    heads = own.shape[1] // BLK
    vmem = pl.BlockSpec(memory_space=pltpu.VMEM)
    return pl.pallas_call(
        merge_kernel,
        out_shape=jax.ShapeDtypeStruct((copies, BLK, heads * HEAD_DIM), bf16),
        in_specs=[vmem, vmem],
        out_specs=vmem,
        compiler_params=pltpu.CompilerParams(vmem_limit_bytes=12 * 1024 * 1024),
    )(own, got)


def product_kernel(tile, weight_count, pick_ref, x_ref, *refs):
    weight_refs, add_ref, out_ref = refs[:weight_count], refs[weight_count:-1], refs[-1]
    x = x_ref[:, pick_ref[0]] if x_ref.shape[1] > out_ref.shape[1] else x_ref[...]
    x = x.reshape(-1, x.shape[-1])
    width = weight_refs[0].shape[1]
    block = out_ref.shape[:-1] + (tile,)
    for i, weight_ref in enumerate(weight_refs):
        for first in range(0, width, tile):
            total = jnp.dot(x, weight_ref[:, first : first + tile], preferred_element_type=f32)
            columns = slice(i * width + first, i * width + first + tile)
            if add_ref:
                total = total + add_ref[0][..., columns].reshape(total.shape).astype(f32)
            out_ref[..., columns] = total.astype(bf16).reshape(block)


def product(x, weights, tile, pick=None, add=None):
    blocks, pair, tokens, inputs = x.shape
    taken = pair if pick is None else 1
    pick = jnp.zeros((1,), jnp.int32) if pick is None else pick.astype(jnp.int32).reshape(1)
    vmem = pl.BlockSpec(memory_space=pltpu.VMEM)
    operands = [x, *weights] if add is None else [x, *weights, add]
    rows = blocks * taken * tokens
    columns = weights[0].shape[1] * len(weights)
    return pl.pallas_call(
        functools.partial(product_kernel, tile, len(weights)),
        out_shape=jax.ShapeDtypeStruct((blocks, taken, tokens, columns), bf16),
        in_specs=[pl.BlockSpec(memory_space=pltpu.SMEM)] + [vmem] * len(operands),
        out_specs=vmem,
        compiler_params=pltpu.CompilerParams(vmem_limit_bytes=20 * 1024 * 1024),
        cost_estimate=pl.CostEstimate(
            flops=2 * rows * inputs * columns,
            bytes_accessed=2 * (rows * inputs + inputs * columns + rows * columns),
            transcendentals=0,
        ),
    )(pick, *operands)


VMEM = pl.BlockSpec(memory_space=pltpu.VMEM)
SMEM = pl.BlockSpec(memory_space=pltpu.SMEM)


def small_call(kernel, outs, scalars, arrays, moved):
    return pl.pallas_call(
        kernel,
        out_shape=outs,
        in_specs=[SMEM] * len(scalars) + [VMEM] * len(arrays),
        out_specs=jax.tree.map(lambda _: VMEM, outs),
        compiler_params=pltpu.CompilerParams(vmem_limit_bytes=16 * 1024 * 1024),
        cost_estimate=pl.CostEstimate(flops=moved, bytes_accessed=moved, transcendentals=0),
    )(*scalars, *arrays)


def columns_kernel(place_ref, mine_ref, theirs_ref, gate_ref, up_ref, *out_refs):
    y, side = place_ref[0], place_ref[1]
    n = mine_ref.shape[2]
    x = jnp.concatenate(
        [ref[(y + i) % 4, s] for s in (1 - side, side) for i in range(4) for ref in (mine_ref, theirs_ref)],
        axis=0,
    )
    step = pl.program_id(0)

    def put(weight_ref):
        total = jnp.dot(x, weight_ref[...], preferred_element_type=f32).astype(bf16)
        for i, ref in enumerate(out_refs[:12]):
            at = (0, 1, 2, 3, 4, 5, 6, 7, 8, 9, 10, 15)[i]
            ref[...] = total[at * n : (at + 1) * n]
        for ref, pair in ((out_refs[12], (12, 11)), (out_refs[13], (13, 14))):
            for j, at in enumerate(pair):
                ref[j] = total[at * n : (at + 1) * n]

    half = pl.num_programs(0) // 2
    pl.when(step < half)(functools.partial(put, gate_ref))
    pl.when(step >= half)(functools.partial(put, up_ref))


def partial_columns(place, mine, theirs, gate, up):
    tile = 896
    inputs, width = gate.shape
    count = width // tile
    tokens = mine.shape[2]
    whole = pl.BlockSpec(mine.shape, lambda n, p: (0, 0, 0, 0))
    rows = 16 * tokens
    return pl.pallas_call(
        columns_kernel,
        out_shape=(jax.ShapeDtypeStruct((tokens, 2 * width), bf16),) * 12
        + (jax.ShapeDtypeStruct((2, tokens, 2 * width), bf16),) * 2,
        grid_spec=pltpu.PrefetchScalarGridSpec(
            num_scalar_prefetch=1,
            grid=(2 * count,),
            in_specs=[
                whole,
                whole,
                pl.BlockSpec((inputs, tile), lambda n, p: (0, jnp.minimum(n, count - 1))),
                pl.BlockSpec((inputs, tile), lambda n, p: (0, jnp.maximum(n - count, 0))),
            ],
            out_specs=(pl.BlockSpec((tokens, tile), lambda n, p: (0, n)),) * 12
            + (pl.BlockSpec((2, tokens, tile), lambda n, p: (0, 0, n)),) * 2,
        ),
        compiler_params=pltpu.CompilerParams(vmem_limit_bytes=60 * 1024 * 1024),
        cost_estimate=pl.CostEstimate(
            flops=4 * rows * inputs * width,
            bytes_accessed=2 * (rows * inputs + 2 * inputs * width + 2 * rows * width),
            transcendentals=0,
        ),
    )(place, mine, theirs, gate, up)


def add_pieces(piece, other):
    def kernel(a_ref, b_ref, out_ref):
        b = b_ref[...] if other.ndim == 2 else b_ref[0]
        out_ref[...] = (a_ref[...].astype(f32) + b.astype(f32)).astype(bf16)

    out = jax.ShapeDtypeStruct(piece.shape, bf16)
    return small_call(kernel, out, (), (piece, other), 2 * piece.size)


def add_halves(*halves):
    count = len(halves[0])

    def kernel(*refs):
        for i in range(len(halves)):
            mine = refs[i * count : (i + 1) * count]
            refs[-1][i] = sum(r[...].astype(f32) for r in mine).astype(bf16)

    first = halves[0][0]
    out = jax.ShapeDtypeStruct((len(halves), *first.shape), bf16)
    return small_call(kernel, out, (), [p for h in halves for p in h], 8 * first.size)


def gated(halves, got, factor):
    count = len(halves[0])
    tokens, width = halves[0][0].shape[0], halves[0][0].shape[1] // 2

    def kernel(*refs):
        got_ref, factor_ref, out_ref = refs[-3:]
        for i in range(len(halves)):
            rows = pl.ds(i * tokens, tokens)
            mine = refs[i * count : (i + 1) * count]
            scale = factor_ref[rows, :]

            def total(columns):
                parts = sum((r[:, columns] if len(r.shape) == 2 else r[1, :, columns]).astype(f32) for r in mine)
                return (parts + got_ref[i, :, columns].astype(f32)) * scale

            gate = total(slice(0, width))
            up = total(slice(width, 2 * width))
            out_ref[rows, :] = (gate / (1.0 + jnp.exp(-gate)) * up).astype(bf16)

    out = jax.ShapeDtypeStruct((tokens * len(halves), width), bf16)
    arrays = [p for h in halves for p in h] + [got, factor[:, None]]
    return small_call(kernel, out, (), arrays, 16 * tokens * width)


def down_product(pieces, weight):
    tile = 512
    count, tokens, inputs = len(pieces), pieces[0].shape[0] // 2, pieces[0].shape[1]
    width = weight.shape[1]

    def kernel(*refs):
        weight_ref, keep_ref, give_ref = refs[count:]
        x = jnp.concatenate([p[...] for p in refs[:count]], axis=0)
        total = jnp.dot(x, weight_ref[...], preferred_element_type=f32)
        for i in range(count):
            at = 2 * i * tokens
            keep_ref[i] = total[at : at + tokens]
            give_ref[i] = total[at + tokens : at + 2 * tokens].astype(bf16)

    by_column = pl.BlockSpec((count, tokens, tile), lambda n: (0, 0, n))
    specs = [pl.BlockSpec((2 * tokens, inputs), lambda n: (0, 0))] * count
    return pl.pallas_call(
        kernel,
        grid=(width // tile,),
        out_shape=(
            jax.ShapeDtypeStruct((count, tokens, width), f32),
            jax.ShapeDtypeStruct((count, tokens, width), bf16),
        ),
        in_specs=specs + [pl.BlockSpec((inputs, tile), lambda n: (0, n))],
        out_specs=(by_column, by_column),
        compiler_params=pltpu.CompilerParams(vmem_limit_bytes=24 * 1024 * 1024),
        cost_estimate=pl.CostEstimate(
            flops=4 * count * tokens * inputs * width,
            bytes_accessed=2 * (2 * count * tokens * inputs + inputs * width + 3 * count * tokens * width),
            transcendentals=0,
        ),
    )(*pieces, weight)


def join_blocks(place, near, far):
    def kernel(place_ref, near_ref, near_got_ref, far_ref, far_got_ref, out_ref):
        y, side = place_ref[0], place_ref[1]
        for i, (kept_ref, got_ref, first) in enumerate(
            (
                (near_ref, near_got_ref, 0),
                (near_ref, near_got_ref, 2),
                (far_ref, far_got_ref, 0),
                (near_ref, near_got_ref, 4),
            )
        ):
            for j in range(2):
                at = 2 * ((y + i) % 4) + (side if j == 0 else 1 - side)
                out_ref[at] = (kept_ref[first + j] + got_ref[first + j].astype(f32)).astype(bf16)

    out = jax.ShapeDtypeStruct((8, *near[0].shape[1:]), bf16)
    return small_call(kernel, out, (place,), (*near, *far), 4 * near[0].size)


def to_right(x):
    return lax.ppermute(x, "y", [(i, (i + 1) % 4) for i in range(4)])


def to_left(x):
    return lax.ppermute(x, "y", [(i, (i + 3) % 4) for i in range(4)])


def ring_start(pieces):
    right, left, opposite = pieces[2:4], pieces[6:8], pieces[4:6]
    return to_right(opposite[0]), to_left(opposite[1]), to_right(right[1]), to_left(left[0])


def ring_middle(pieces, from_left, from_right):
    return add_pieces(pieces[2], from_left), add_pieces(pieces[7], from_right)


def ring_end(pieces, arrived, sums):
    third_left, third_right = to_right(sums[0]), to_left(sums[1])
    return (pieces[0], arrived[3], third_left), (pieces[1], arrived[2], third_right)


def gather_start(mine):
    return to_right(mine), to_left(mine)


def pack_kernel(within_ref, group_ref, keys_ref, values_ref, near_keys_ref, near_values_ref, out_ref):
    eighth = BLK // 8
    rows = (out_ref.shape[1] - 2 * eighth) // 2
    goal = pl.program_id(0)
    near = pl.ds(pl.multiple_of(group_ref[0] * eighth, eighth), eighth)
    for i in range(out_ref.shape[0]):
        at = within_ref[goal, i]
        out_ref[i, 0:rows] = keys_ref[at, 0:rows]
        out_ref[i, rows : 2 * rows] = values_ref[at, 0:rows]
        out_ref[i, 2 * rows : 2 * rows + eighth] = near_keys_ref[0, near]
        out_ref[i, 2 * rows + eighth :] = near_values_ref[0, near]


def pack(within, group, keys, values, near_keys, near_values, rows):
    def of_group(x, height):
        return pl.BlockSpec((x.shape[0] // KV_HEADS, height, HEAD_DIM), lambda n, s, g: (n, 0, 0))

    arrays = ((keys, rows), (values, rows), (near_keys, BLK), (near_values, BLK))
    height = 2 * rows + BLK // 4
    return pl.pallas_call(
        pack_kernel,
        out_shape=jax.ShapeDtypeStruct((64, height, HEAD_DIM), bf16),
        grid_spec=pltpu.PrefetchScalarGridSpec(
            num_scalar_prefetch=2,
            grid=(8,),
            in_specs=[of_group(*x) for x in arrays],
            out_specs=pl.BlockSpec((8, height, HEAD_DIM), lambda n, s, g: (n, 0, 0)),
        ),
        compiler_params=pltpu.CompilerParams(vmem_limit_bytes=60 * 1024 * 1024),
        cost_estimate=pl.CostEstimate(flops=0, bytes_accessed=64 * height * 512, transcendentals=0),
    )(within, group.astype(jnp.int32).reshape(1), *[x for x, _ in arrays])


def exchange(x, axes):
    return lax.all_to_all(x, axes, split_axis=0, concat_axis=0, tiled=True)


def swap(x, axis="core"):
    return lax.ppermute(x, axis, [(0, 1), (1, 0)])


def spread(x, copies):
    return jnp.broadcast_to(x[None], (copies,) + x.shape)


def take(x, index, axis):
    return lax.dynamic_index_in_dim(x, index, axis, keepdims=False)


def local(
    queries,
    cache_keys,
    cache_values,
    stretch_keys,
    stretch_values,
    block_lists,
    out_weight,
    residual,
    norm_gain,
    gate_weight,
    up_weight,
    down_weight,
):
    core = lax.axis_index("core")
    side = lax.axis_index("xl")
    col = lax.axis_index(COL)
    group = lax.axis_index(ZXH)
    me = lax.axis_index(ROW) * 8 + col
    local_blocks = cache_keys.shape[1] // BLK
    tokens_here = residual.shape[0]

    matched = block_lists // local_blocks == me
    within = jnp.sum(jnp.where(matched, block_lists % local_blocks, 0), axis=2)
    source = (jnp.arange(KV_HEADS, dtype=jnp.int32)[:, None] * local_blocks + within.T).reshape(-1)

    piece = BLK // 4
    flat_keys = cache_keys.reshape(4 * KV_HEADS * local_blocks, piece, HEAD_DIM)
    flat_values = cache_values.reshape(4 * KV_HEADS * local_blocks, piece, HEAD_DIM)

    def pick(flat, first, count):
        index = 4 * source[:, None] + jnp.arange(first, first + count, dtype=jnp.int32)[None, :]
        return flat[index].reshape(64, count * piece, HEAD_DIM)

    blocked = (KV_HEADS * local_blocks, BLK, HEAD_DIM)
    first = pack(
        within.T, group, cache_keys.reshape(blocked), cache_values.reshape(blocked),
        stretch_keys, stretch_values, 3 * piece,
    )
    first = exchange(first, CHIP)
    second = [pick(flat_keys, 3, 1), pick(flat_values, 3, 1)]
    second = exchange(jnp.concatenate(second, axis=1), CHIP)
    my_list = block_lists[col, group]
    place = jnp.stack([core, col]).astype(jnp.int32)
    other_queries = swap(queries)
    own, send, order = attend((my_list, place), queries, other_queries, first, (), local_blocks, 5)
    own, send = attend((order,), queries, other_queries, second, (own, send), local_blocks, 16)
    attended = exchange(merge(own, swap(send), 8), COL).reshape(8, 2, tokens_here, -1)

    def row_sum(give, mine, pick, weight):
        both = product(mine, (weight,), 512, pick, add=swap(give))
        return jnp.sum(exchange(both.reshape(8, tokens_here, -1), ZXH).astype(f32), axis=0)

    give = product(attended, (out_weight,), 512, 1 - core)
    stream = residual.astype(f32) + row_sum(give, attended, core, out_weight)
    gain = norm_gain.astype(f32)[None, :]
    own_rows = exchange(spread((stream * gain).astype(bf16), 8), ZXH)
    other_rows = swap(own_rows)

    def squares(x):
        plain = x.astype(f32) / gain[None]
        return jnp.sum(plain * plain, axis=2)

    squares = jnp.stack([squares(own_rows), squares(other_rows)], axis=1)

    by_pair = (4, 2, tokens_here, own_rows.shape[-1])
    where = jnp.stack([lax.axis_index("y"), side]).astype(jnp.int32)
    columns = partial_columns(
        where, own_rows.reshape(by_pair), other_rows.reshape(by_pair), gate_weight, up_weight
    )
    theirs, mine = columns[:8], columns[8:]
    arrived = ring_start(theirs)
    sums = ring_middle(theirs, *arrived[:2])
    sums, mine, squares = lax.optimization_barrier((sums, mine, squares))
    squares = exchange(squares, COL)
    halves = ring_end(theirs, arrived, sums)
    own_first, own_second, right, left, go_right, go_left = mine
    from_left, from_right = to_right(go_right), to_left(go_left)
    halves, squares = lax.optimization_barrier((halves, squares))
    got = swap(add_halves(*halves), "xl")
    factor = lax.rsqrt(jnp.sum(squares, axis=0).reshape(-1) / D + 1e-05)
    third_left, third_right = to_right(add_pieces(right, from_left)), to_left(add_pieces(left, from_right))
    halves = (own_first, third_left, from_right), (own_second, third_right, from_left)
    hidden = gated(halves, got, factor)
    first, hidden_got = lax.optimization_barrier((gather_start(hidden), swap(hidden, "xl")))
    got_left, got_right = to_right(hidden_got), to_left(hidden_got)
    mine_far = to_right(first[0])
    got_far = to_left(got_right)
    near = (hidden, hidden_got, first[1], got_right, first[0], got_left)
    kept, give = down_product(near, down_weight)
    far_kept, far_give = down_product((mine_far, got_far), down_weight)
    down = join_blocks(where, (kept, swap(give)), (far_kept, swap(far_give)))
    mlp = jnp.sum(exchange(down, ZXH).astype(f32), axis=0)
    return (stream + mlp).astype(bf16)


def solution(mesh):
    mesh = Mesh(mesh.devices.reshape(4, 2, 2, 4, 2), AXES)
    in_specs = (
        P(COL, ROW),
        P(None, ROW + COL, None),
        P(None, ROW + COL, None),
        P(None, COL, None),
        P(None, COL, None),
        P(),
        P(ROW, COL),
        P(ROW, COL),
        P(COL),
        P(COL, ROW),
        P(COL, ROW),
        P(ROW, COL),
    )
    return jax.shard_map(local, mesh=mesh, in_specs=in_specs, out_specs=P(ROW, COL), check_vma=False)
```

```python
import functools
import math

import jax
import jax.numpy as jnp
from jax import lax
from jax.experimental import pallas as pl
from jax.experimental.pallas import tpu as pltpu
from jax.sharding import Mesh, PartitionSpec as P

D = 8192
KV_HEADS = 8
HEAD_DIM = 128
BLK = 128
GROUP = 8
AXES = ("z", "xh", "core", "y", "xl")
ROW = ("z", "xh", "core")
ZXH = ("z", "xh")
COL = ("y", "xl")
CHIP = ("z", "xh", "y", "xl")
NEG = -1e30
bf16 = jnp.bfloat16
f32 = jnp.float32


def nt_dot(a, b):
    return lax.dot_general(a, b, (((1,), (1,)), ((), ())), preferred_element_type=f32)


def tn_dot(a, b):
    return lax.dot_general(a, b, (((0,), (0,)), ((), ())), preferred_element_type=f32)


def attend_kernel(scale, per_step, local_blocks, last, *refs):
    if last:
        order_ref, own_q_ref, other_q_ref, chunk_ref, own_in_ref, send_in_ref = refs[:6]
    else:
        list_ref, place_ref, own_q_ref, other_q_ref, chunk_ref = refs[:5]
        order_ref = refs[7]
    own_ref, send_ref = refs[6:8] if last else refs[5:7]
    q_ref, top_ref, sum_ref, acc_ref = refs[-4:]
    length = order_ref.shape[0] - 1
    part_rows = (chunk_ref.shape[1] - (0 if last else BLK // 8)) // 2
    heads = own_q_ref.shape[1] // HEAD_DIM
    rows = heads * BLK
    for h in range(heads):
        cols = pl.ds(h * HEAD_DIM, HEAD_DIM)
        q_ref[pl.ds(h * BLK, BLK), :] = own_q_ref[:, cols]
        q_ref[pl.ds(rows + h * BLK, BLK), :] = other_q_ref[:, cols]
    if last:
        for half, ref in ((0, own_in_ref), (1, send_in_ref)):
            acc_ref[half] = ref[0:HEAD_DIM, :]
            top_ref[half] = ref[HEAD_DIM : HEAD_DIM + 1, :]
            sum_ref[half] = ref[HEAD_DIM + 1 : HEAD_DIM + 2, :]
        count = order_ref[length]
    else:
        core = place_ref[0]
        block = place_ref[1]
        top_ref[...] = jnp.full_like(top_ref, NEG)
        sum_ref[...] = jnp.zeros_like(sum_ref)
        acc_ref[...] = jnp.zeros_like(acc_ref)

        def collect(i, count):
            device = list_ref[i] // local_blocks
            row = device // 8
            order_ref[count] = (row // 2) * 8 + device % 8
            return count + jnp.where(row % 2 == core, 1, 0)

        count = lax.fori_loop(0, length, collect, jnp.int32(0))
        order_ref[length] = count

    def update(half, keys, values, bias):
        part = pl.ds(half * rows, rows)
        scores = nt_dot(keys, q_ref[part, :]) * scale + bias
        old = top_ref[half]
        new = jnp.maximum(old, jnp.max(scores, axis=0, keepdims=True))
        weights = jnp.exp2(scores - new)
        decay = jnp.exp2(old - new)
        top_ref[half] = new
        sum_ref[half] = sum_ref[half] * decay + jnp.sum(weights, axis=0, keepdims=True)
        acc_ref[half] = acc_ref[half] * decay + tn_dot(values, weights.astype(bf16))

    def far(step, carry):
        slots = [order_ref[jnp.minimum(step * per_step + i, count - 1)] for i in range(per_step)]
        keys = jnp.concatenate([chunk_ref[s, 0:part_rows] for s in slots], axis=0)
        values = jnp.concatenate([chunk_ref[s, part_rows : 2 * part_rows] for s in slots], axis=0)
        bias = jnp.concatenate(
            [
                jnp.full((part_rows, 1), jnp.where(step * per_step + i < count, 0.0, NEG), f32)
                for i in range(per_step)
            ],
            axis=0,
        )
        for half in range(2):
            update(half, keys, values, bias)
        return carry

    lax.fori_loop(0, (count + per_step - 1) // per_step, far, 0)

    def near(which, carry):
        part = BLK // 16
        index = lax.broadcasted_iota(jnp.int32, (BLK // 2, rows), 0)
        key_pos = index // part * (2 * part) + core * part + index % part
        token = lax.broadcasted_iota(jnp.int32, (BLK // 2, rows), 1) % BLK
        bias = jnp.where(key_pos <= token + (block - which) * BLK, 0.0, NEG)
        at = 2 * part_rows
        keys = jnp.concatenate([chunk_ref[i * 8 + which, at : at + part] for i in range(8)], axis=0)
        values = jnp.concatenate([chunk_ref[i * 8 + which, at + part :] for i in range(8)], axis=0)
        for half in range(2):
            update(half, keys, values, bias)
        return carry

    if not last:
        lax.fori_loop(0, block + 1, near, 0)
    for half, ref in ((0, own_ref), (1, send_ref)):
        ref[0:HEAD_DIM, :] = acc_ref[half]
        ref[HEAD_DIM : HEAD_DIM + 1, :] = top_ref[half]
        ref[HEAD_DIM + 1 : HEAD_DIM + 2, :] = sum_ref[half]


def attend(scalars, own_q, other_q, chunk, state, local_blocks, per_step):
    heads = own_q.shape[1] // HEAD_DIM
    rows = heads * BLK
    length = scalars[0].shape[0] - len(state) // 2
    packed = jax.ShapeDtypeStruct((HEAD_DIM + 8, rows), f32)
    smem = pl.BlockSpec(memory_space=pltpu.SMEM)
    vmem = pl.BlockSpec(memory_space=pltpu.VMEM)
    scale = math.log2(math.e) / math.sqrt(HEAD_DIM)
    arrays = [own_q, other_q, chunk, *state]
    outs = [packed, packed]
    if not state:
        outs.append(jax.ShapeDtypeStruct((length + 1,), jnp.int32))
    return pl.pallas_call(
        functools.partial(attend_kernel, scale, per_step, local_blocks, len(state) > 0),
        out_shape=outs,
        in_specs=[smem] * len(scalars) + [vmem] * len(arrays),
        out_specs=[vmem, vmem, smem][: len(outs)],
        scratch_shapes=[
            pltpu.VMEM((2 * rows, HEAD_DIM), bf16),
            pltpu.VMEM((2, 1, rows), f32),
            pltpu.VMEM((2, 1, rows), f32),
            pltpu.VMEM((2, HEAD_DIM, rows), f32),
        ],
        compiler_params=pltpu.CompilerParams(vmem_limit_bytes=24 * 1024 * 1024),
        cost_estimate=pl.CostEstimate(
            flops=2 * rows * 40 * chunk.shape[1] * HEAD_DIM,
            bytes_accessed=2 * chunk.size,
            transcendentals=rows * 40 * chunk.shape[1],
        ),
    )(*scalars, *arrays)


def merge_kernel(own_ref, got_ref, out_ref):
    own_top = own_ref[HEAD_DIM : HEAD_DIM + 1, :]
    got_top = got_ref[HEAD_DIM : HEAD_DIM + 1, :]
    top = jnp.maximum(own_top, got_top)
    own_w = jnp.exp2(own_top - top)
    got_w = jnp.exp2(got_top - top)
    total = own_w * own_ref[HEAD_DIM + 1 : HEAD_DIM + 2, :] + got_w * got_ref[HEAD_DIM + 1 : HEAD_DIM + 2, :]
    mixed = (own_ref[0:HEAD_DIM, :] * own_w + got_ref[0:HEAD_DIM, :] * got_w) / total
    heads = mixed.shape[1] // BLK
    for h in range(heads):
        piece = mixed[:, h * BLK : (h + 1) * BLK].T.astype(bf16)
        for i in range(out_ref.shape[0]):
            out_ref[i, :, pl.ds(h * HEAD_DIM, HEAD_DIM)] = piece


def merge(own, got, copies):
    heads = own.shape[1] // BLK
    vmem = pl.BlockSpec(memory_space=pltpu.VMEM)
    return pl.pallas_call(
        merge_kernel,
        out_shape=jax.ShapeDtypeStruct((copies, BLK, heads * HEAD_DIM), bf16),
        in_specs=[vmem, vmem],
        out_specs=vmem,
        compiler_params=pltpu.CompilerParams(vmem_limit_bytes=12 * 1024 * 1024),
    )(own, got)


def product_kernel(tile, weight_count, pick_ref, x_ref, *refs):
    weight_refs, add_ref, out_ref = refs[:weight_count], refs[weight_count:-1], refs[-1]
    x = x_ref[:, pick_ref[0]] if x_ref.shape[1] > out_ref.shape[1] else x_ref[...]
    x = x.reshape(-1, x.shape[-1])
    width = weight_refs[0].shape[1]
    block = out_ref.shape[:-1] + (tile,)
    for i, weight_ref in enumerate(weight_refs):
        for first in range(0, width, tile):
            total = jnp.dot(x, weight_ref[:, first : first + tile], preferred_element_type=f32)
            columns = slice(i * width + first, i * width + first + tile)
            if add_ref:
                total = total + add_ref[0][..., columns].reshape(total.shape).astype(f32)
            out_ref[..., columns] = total.astype(bf16).reshape(block)


def product(x, weights, tile, pick=None, add=None):
    blocks, pair, tokens, inputs = x.shape
    taken = pair if pick is None else 1
    pick = jnp.zeros((1,), jnp.int32) if pick is None else pick.astype(jnp.int32).reshape(1)
    vmem = pl.BlockSpec(memory_space=pltpu.VMEM)
    operands = [x, *weights] if add is None else [x, *weights, add]
    rows = blocks * taken * tokens
    columns = weights[0].shape[1] * len(weights)
    return pl.pallas_call(
        functools.partial(product_kernel, tile, len(weights)),
        out_shape=jax.ShapeDtypeStruct((blocks, taken, tokens, columns), bf16),
        in_specs=[pl.BlockSpec(memory_space=pltpu.SMEM)] + [vmem] * len(operands),
        out_specs=vmem,
        compiler_params=pltpu.CompilerParams(vmem_limit_bytes=20 * 1024 * 1024),
        cost_estimate=pl.CostEstimate(
            flops=2 * rows * inputs * columns,
            bytes_accessed=2 * (rows * inputs + inputs * columns + rows * columns),
            transcendentals=0,
        ),
    )(pick, *operands)


VMEM = pl.BlockSpec(memory_space=pltpu.VMEM)
SMEM = pl.BlockSpec(memory_space=pltpu.SMEM)


def small_call(kernel, outs, scalars, arrays, moved):
    return pl.pallas_call(
        kernel,
        out_shape=outs,
        in_specs=[SMEM] * len(scalars) + [VMEM] * len(arrays),
        out_specs=jax.tree.map(lambda _: VMEM, outs),
        compiler_params=pltpu.CompilerParams(vmem_limit_bytes=16 * 1024 * 1024),
        cost_estimate=pl.CostEstimate(flops=moved, bytes_accessed=moved, transcendentals=0),
    )(*scalars, *arrays)


def columns_kernel(place_ref, mine_ref, theirs_ref, gate_ref, up_ref, *out_refs):
    y, side = place_ref[0], place_ref[1]
    n = mine_ref.shape[2]
    x = jnp.concatenate(
        [ref[(y + i) % 4, s] for s in (1 - side, side) for i in range(4) for ref in (mine_ref, theirs_ref)],
        axis=0,
    )
    step = pl.program_id(0)

    def put(weight_ref):
        total = jnp.dot(x, weight_ref[...], preferred_element_type=f32).astype(bf16)
        for i, ref in enumerate(out_refs[:12]):
            at = (0, 1, 2, 3, 4, 5, 6, 7, 8, 9, 10, 15)[i]
            ref[...] = total[at * n : (at + 1) * n]
        for ref, pair in ((out_refs[12], (12, 11)), (out_refs[13], (13, 14))):
            for j, at in enumerate(pair):
                ref[j] = total[at * n : (at + 1) * n]

    half = pl.num_programs(0) // 2
    pl.when(step < half)(functools.partial(put, gate_ref))
    pl.when(step >= half)(functools.partial(put, up_ref))


def partial_columns(place, mine, theirs, gate, up):
    tile = 896
    inputs, width = gate.shape
    count = width // tile
    tokens = mine.shape[2]
    whole = pl.BlockSpec(mine.shape, lambda n, p: (0, 0, 0, 0))
    rows = 16 * tokens
    return pl.pallas_call(
        columns_kernel,
        out_shape=(jax.ShapeDtypeStruct((tokens, 2 * width), bf16),) * 12
        + (jax.ShapeDtypeStruct((2, tokens, 2 * width), bf16),) * 2,
        grid_spec=pltpu.PrefetchScalarGridSpec(
            num_scalar_prefetch=1,
            grid=(2 * count,),
            in_specs=[
                whole,
                whole,
                pl.BlockSpec((inputs, tile), lambda n, p: (0, jnp.minimum(n, count - 1))),
                pl.BlockSpec((inputs, tile), lambda n, p: (0, jnp.maximum(n - count, 0))),
            ],
            out_specs=(pl.BlockSpec((tokens, tile), lambda n, p: (0, n)),) * 12
            + (pl.BlockSpec((2, tokens, tile), lambda n, p: (0, 0, n)),) * 2,
        ),
        compiler_params=pltpu.CompilerParams(vmem_limit_bytes=60 * 1024 * 1024),
        cost_estimate=pl.CostEstimate(
            flops=4 * rows * inputs * width,
            bytes_accessed=2 * (rows * inputs + 2 * inputs * width + 2 * rows * width),
            transcendentals=0,
        ),
    )(place, mine, theirs, gate, up)


def add_pieces(piece, other):
    def kernel(a_ref, b_ref, out_ref):
        b = b_ref[...] if other.ndim == 2 else b_ref[0]
        out_ref[...] = (a_ref[...].astype(f32) + b.astype(f32)).astype(bf16)

    out = jax.ShapeDtypeStruct(piece.shape, bf16)
    return small_call(kernel, out, (), (piece, other), 2 * piece.size)


def add_halves(*halves):
    count = len(halves[0])

    def kernel(*refs):
        for i in range(len(halves)):
            mine = refs[i * count : (i + 1) * count]
            refs[-1][i] = sum(r[...].astype(f32) for r in mine).astype(bf16)

    first = halves[0][0]
    out = jax.ShapeDtypeStruct((len(halves), *first.shape), bf16)
    return small_call(kernel, out, (), [p for h in halves for p in h], 8 * first.size)


def gated(halves, got, factor):
    count = len(halves[0])
    tokens, width = halves[0][0].shape[0], halves[0][0].shape[1] // 2

    def kernel(*refs):
        got_ref, factor_ref, out_ref = refs[-3:]
        for i in range(len(halves)):
            rows = pl.ds(i * tokens, tokens)
            mine = refs[i * count : (i + 1) * count]
            scale = factor_ref[rows, :]

            def total(columns):
                parts = sum((r[:, columns] if len(r.shape) == 2 else r[1, :, columns]).astype(f32) for r in mine)
                return (parts + got_ref[i, :, columns].astype(f32)) * scale

            gate = total(slice(0, width))
            up = total(slice(width, 2 * width))
            out_ref[rows, :] = (gate / (1.0 + jnp.exp(-gate)) * up).astype(bf16)

    out = jax.ShapeDtypeStruct((tokens * len(halves), width), bf16)
    arrays = [p for h in halves for p in h] + [got, factor[:, None]]
    return small_call(kernel, out, (), arrays, 16 * tokens * width)


def down_product(pieces, weight):
    tile = 512
    count, tokens, inputs = len(pieces), pieces[0].shape[0] // 2, pieces[0].shape[1]
    width = weight.shape[1]

    def kernel(*refs):
        weight_ref, keep_ref, give_ref = refs[count:]
        x = jnp.concatenate([p[...] for p in refs[:count]], axis=0)
        total = jnp.dot(x, weight_ref[...], preferred_element_type=f32)
        for i in range(count):
            at = 2 * i * tokens
            keep_ref[i] = total[at : at + tokens]
            give_ref[i] = total[at + tokens : at + 2 * tokens].astype(bf16)

    by_column = pl.BlockSpec((count, tokens, tile), lambda n: (0, 0, n))
    specs = [pl.BlockSpec((2 * tokens, inputs), lambda n: (0, 0))] * count
    return pl.pallas_call(
        kernel,
        grid=(width // tile,),
        out_shape=(
            jax.ShapeDtypeStruct((count, tokens, width), f32),
            jax.ShapeDtypeStruct((count, tokens, width), bf16),
        ),
        in_specs=specs + [pl.BlockSpec((inputs, tile), lambda n: (0, n))],
        out_specs=(by_column, by_column),
        compiler_params=pltpu.CompilerParams(vmem_limit_bytes=24 * 1024 * 1024),
        cost_estimate=pl.CostEstimate(
            flops=4 * count * tokens * inputs * width,
            bytes_accessed=2 * (2 * count * tokens * inputs + inputs * width + 3 * count * tokens * width),
            transcendentals=0,
        ),
    )(*pieces, weight)


def join_blocks(place, near, far):
    def kernel(place_ref, near_ref, near_got_ref, far_ref, far_got_ref, out_ref):
        y, side = place_ref[0], place_ref[1]
        for i, (kept_ref, got_ref, first) in enumerate(
            (
                (near_ref, near_got_ref, 0),
                (near_ref, near_got_ref, 2),
                (far_ref, far_got_ref, 0),
                (near_ref, near_got_ref, 4),
            )
        ):
            for j in range(2):
                at = 2 * ((y + i) % 4) + (side if j == 0 else 1 - side)
                out_ref[at] = (kept_ref[first + j] + got_ref[first + j].astype(f32)).astype(bf16)

    out = jax.ShapeDtypeStruct((8, *near[0].shape[1:]), bf16)
    return small_call(kernel, out, (place,), (*near, *far), 4 * near[0].size)


def to_right(x):
    return lax.ppermute(x, "y", [(i, (i + 1) % 4) for i in range(4)])


def to_left(x):
    return lax.ppermute(x, "y", [(i, (i + 3) % 4) for i in range(4)])


def ring_start(pieces):
    right, left, opposite = pieces[2:4], pieces[6:8], pieces[4:6]
    return to_right(opposite[0]), to_left(opposite[1]), to_right(right[1]), to_left(left[0])


def ring_middle(pieces, from_left, from_right):
    return add_pieces(pieces[2], from_left), add_pieces(pieces[7], from_right)


def ring_end(pieces, arrived, sums):
    third_left, third_right = to_right(sums[0]), to_left(sums[1])
    return (pieces[0], arrived[3], third_left), (pieces[1], arrived[2], third_right)


def gather_start(mine):
    return to_right(mine), to_left(mine)


def pack_kernel(within_ref, first_ref, keys_ref, values_ref, near_keys_ref, near_values_ref, out_ref):
    part = BLK // 16
    rows = (out_ref.shape[1] - 2 * part) // 2
    near = pl.ds(pl.multiple_of(first_ref[0], part), part)
    for i in range(out_ref.shape[0]):
        at = within_ref[pl.program_id(0), i]
        out_ref[i, 0:rows] = keys_ref[at, 0:rows]
        out_ref[i, rows : 2 * rows] = values_ref[at, 0:rows]
        out_ref[i, 2 * rows : 2 * rows + part] = near_keys_ref[0, near]
        out_ref[i, 2 * rows + part :] = near_values_ref[0, near]


def pack(within, place, keys, values, near_keys, near_values, rows):
    def of_group(x, height):
        return pl.BlockSpec((x.shape[0] // KV_HEADS, height, HEAD_DIM), lambda n, s, g: (n, 0, 0))

    arrays = ((keys, rows), (values, rows), (near_keys, BLK), (near_values, BLK))
    height = 2 * rows + BLK // 8
    return pl.pallas_call(
        pack_kernel,
        out_shape=jax.ShapeDtypeStruct((64, height, HEAD_DIM), bf16),
        grid_spec=pltpu.PrefetchScalarGridSpec(
            num_scalar_prefetch=2,
            grid=(8,),
            in_specs=[of_group(*x) for x in arrays],
            out_specs=pl.BlockSpec((8, height, HEAD_DIM), lambda n, s, g: (n, 0, 0)),
        ),
        compiler_params=pltpu.CompilerParams(vmem_limit_bytes=60 * 1024 * 1024),
        cost_estimate=pl.CostEstimate(flops=0, bytes_accessed=64 * height * 512, transcendentals=0),
    )(within, (place * (BLK // 16)).astype(jnp.int32).reshape(1), *[x for x, _ in arrays])


def exchange(x, axes):
    return lax.all_to_all(x, axes, split_axis=0, concat_axis=0, tiled=True)


def swap(x, axis="core"):
    return lax.ppermute(x, axis, [(0, 1), (1, 0)])


def spread(x, copies):
    return jnp.broadcast_to(x[None], (copies,) + x.shape)


def take(x, index, axis):
    return lax.dynamic_index_in_dim(x, index, axis, keepdims=False)


def local(
    queries,
    cache_keys,
    cache_values,
    stretch_keys,
    stretch_values,
    block_lists,
    out_weight,
    residual,
    norm_gain,
    gate_weight,
    up_weight,
    down_weight,
):
    core = lax.axis_index("core")
    side = lax.axis_index("xl")
    col = lax.axis_index(COL)
    group = lax.axis_index(ZXH)
    me = lax.axis_index(ROW) * 8 + col
    local_blocks = cache_keys.shape[1] // BLK
    tokens_here = residual.shape[0]

    matched = block_lists // local_blocks == me
    within = jnp.sum(jnp.where(matched, block_lists % local_blocks, 0), axis=2)
    source = (jnp.arange(KV_HEADS, dtype=jnp.int32)[:, None] * local_blocks + within.T).reshape(-1)

    piece = BLK // 4
    flat_keys = cache_keys.reshape(4 * KV_HEADS * local_blocks, piece, HEAD_DIM)
    flat_values = cache_values.reshape(4 * KV_HEADS * local_blocks, piece, HEAD_DIM)

    def pick(flat, first, count):
        index = 4 * source[:, None] + jnp.arange(first, first + count, dtype=jnp.int32)[None, :]
        return flat[index].reshape(64, count * piece, HEAD_DIM)

    blocked = (KV_HEADS * local_blocks, BLK, HEAD_DIM)
    first = pack(
        within.T, 2 * group + core, cache_keys.reshape(blocked), cache_values.reshape(blocked),
        stretch_keys, stretch_values, 3 * piece,
    )
    first = exchange(first, CHIP)
    second = [pick(flat_keys, 3, 1), pick(flat_values, 3, 1)]
    second = exchange(jnp.concatenate(second, axis=1), CHIP)
    my_list = block_lists[col, group]
    place = jnp.stack([core, col]).astype(jnp.int32)
    other_queries = swap(queries)
    own, send, order = attend((my_list, place), queries, other_queries, first, (), local_blocks, 5)
    own, send = attend((order,), queries, other_queries, second, (own, send), local_blocks, 16)
    attended = exchange(merge(own, swap(send), 8), COL).reshape(8, 2, tokens_here, -1)

    def row_sum(give, mine, pick, weight):
        both = product(mine, (weight,), 512, pick, add=swap(give))
        return jnp.sum(exchange(both.reshape(8, tokens_here, -1), ZXH).astype(f32), axis=0)

    give = product(attended, (out_weight,), 512, 1 - core)
    stream = residual.astype(f32) + row_sum(give, attended, core, out_weight)
    gain = norm_gain.astype(f32)[None, :]
    own_rows = exchange(spread((stream * gain).astype(bf16), 8), ZXH)
    other_rows = swap(own_rows)

    def squares(x):
        plain = x.astype(f32) / gain[None]
        return jnp.sum(plain * plain, axis=2)

    squares = jnp.stack([squares(own_rows), squares(other_rows)], axis=1)

    by_pair = (4, 2, tokens_here, own_rows.shape[-1])
    where = jnp.stack([lax.axis_index("y"), side]).astype(jnp.int32)
    columns = partial_columns(
        where, own_rows.reshape(by_pair), other_rows.reshape(by_pair), gate_weight, up_weight
    )
    columns, squares = lax.optimization_barrier((columns, squares))
    theirs, mine = columns[:8], columns[8:]
    squares = exchange(squares, COL)
    arrived = ring_start(theirs)
    steps, squares = lax.optimization_barrier((arrived[:2], squares))
    sums = ring_middle(theirs, *steps)
    sums, mine = lax.optimization_barrier((sums, mine))
    halves = ring_end(theirs, arrived, sums)
    own_first, own_second, right, left, go_right, go_left = mine
    from_left, from_right = to_right(go_right), to_left(go_left)
    got = swap(add_halves(*halves), "xl")
    factor = lax.rsqrt(jnp.sum(squares, axis=0).reshape(-1) / D + 1e-05)
    third_left, third_right = to_right(add_pieces(right, from_left)), to_left(add_pieces(left, from_right))
    halves = (own_first, third_left, from_right), (own_second, third_right, from_left)
    hidden = gated(halves, got, factor)
    first, hidden_got = lax.optimization_barrier((gather_start(hidden), swap(hidden, "xl")))
    got_left, got_right = to_right(hidden_got), to_left(hidden_got)
    mine_far = to_right(first[0])
    got_far = to_left(got_right)
    near = (hidden, hidden_got, first[1], got_right, first[0], got_left)
    kept, give = down_product(near, down_weight)
    far_kept, far_give = down_product((mine_far, got_far), down_weight)
    down = join_blocks(where, (kept, swap(give)), (far_kept, swap(far_give)))
    mlp = jnp.sum(exchange(down, ZXH).astype(f32), axis=0)
    return (stream + mlp).astype(bf16)


def solution(mesh):
    mesh = Mesh(mesh.devices.reshape(4, 2, 2, 4, 2), AXES)
    in_specs = (
        P(COL, ROW),
        P(None, ROW + COL, None),
        P(None, ROW + COL, None),
        P(None, COL, None),
        P(None, COL, None),
        P(),
        P(ROW, COL),
        P(ROW, COL),
        P(COL),
        P(COL, ROW),
        P(COL, ROW),
        P(ROW, COL),
    )
    return jax.shard_map(local, mesh=mesh, in_specs=in_specs, out_specs=P(ROW, COL), check_vma=False)
```

```python
import functools
import math

import jax
import jax.numpy as jnp
from jax import lax
from jax.experimental import pallas as pl
from jax.experimental.pallas import tpu as pltpu
from jax.sharding import Mesh, PartitionSpec as P

D = 8192
KV_HEADS = 8
HEAD_DIM = 128
BLK = 128
GROUP = 8
AXES = ("z", "xh", "core", "y", "xl")
ROW = ("z", "xh", "core")
ZXH = ("z", "xh")
COL = ("y", "xl")
CHIP = ("z", "xh", "y", "xl")
NEG = -1e30
bf16 = jnp.bfloat16
f32 = jnp.float32


def nt_dot(a, b):
    return lax.dot_general(a, b, (((1,), (1,)), ((), ())), preferred_element_type=f32)


def tn_dot(a, b):
    return lax.dot_general(a, b, (((0,), (0,)), ((), ())), preferred_element_type=f32)


def attend_kernel(scale, per_step, local_blocks, last, *refs):
    if last:
        order_ref, own_q_ref, other_q_ref, chunk_ref, own_in_ref, send_in_ref = refs[:6]
    else:
        list_ref, place_ref, own_q_ref, other_q_ref, chunk_ref = refs[:5]
        order_ref = refs[7]
    own_ref, send_ref = refs[6:8] if last else refs[5:7]
    q_ref, top_ref, sum_ref, acc_ref = refs[-4:]
    length = order_ref.shape[0] - 1
    part_rows = (chunk_ref.shape[1] - (0 if last else BLK // 4)) // 2
    heads = own_q_ref.shape[1] // HEAD_DIM
    rows = heads * BLK
    for h in range(heads):
        cols = pl.ds(h * HEAD_DIM, HEAD_DIM)
        q_ref[pl.ds(h * BLK, BLK), :] = own_q_ref[:, cols]
        q_ref[pl.ds(rows + h * BLK, BLK), :] = other_q_ref[:, cols]
    if last:
        for half, ref in ((0, own_in_ref), (1, send_in_ref)):
            acc_ref[half] = ref[0:HEAD_DIM, :]
            top_ref[half] = ref[HEAD_DIM : HEAD_DIM + 1, :]
            sum_ref[half] = ref[HEAD_DIM + 1 : HEAD_DIM + 2, :]
        count = order_ref[length]
    else:
        core = place_ref[0]
        block = place_ref[1]
        top_ref[...] = jnp.full_like(top_ref, NEG)
        sum_ref[...] = jnp.zeros_like(sum_ref)
        acc_ref[...] = jnp.zeros_like(acc_ref)

        def collect(i, count):
            device = list_ref[i] // local_blocks
            row = device // 8
            order_ref[count] = (row // 2) * 8 + device % 8
            return count + jnp.where(row % 2 == core, 1, 0)

        count = lax.fori_loop(0, length, collect, jnp.int32(0))
        order_ref[length] = count

    def update(half, keys, values, bias):
        part = pl.ds(half * rows, rows)
        scores = nt_dot(keys, q_ref[part, :]) * scale + bias
        old = top_ref[half]
        new = jnp.maximum(old, jnp.max(scores, axis=0, keepdims=True))
        weights = jnp.exp2(scores - new)
        decay = jnp.exp2(old - new)
        top_ref[half] = new
        sum_ref[half] = sum_ref[half] * decay + jnp.sum(weights, axis=0, keepdims=True)
        acc_ref[half] = acc_ref[half] * decay + tn_dot(values, weights.astype(bf16))

    def far(step, carry):
        slots = [order_ref[jnp.minimum(step * per_step + i, count - 1)] for i in range(per_step)]
        keys = jnp.concatenate([chunk_ref[s, 0:part_rows] for s in slots], axis=0)
        values = jnp.concatenate([chunk_ref[s, part_rows : 2 * part_rows] for s in slots], axis=0)
        bias = jnp.concatenate(
            [
                jnp.full((part_rows, 1), jnp.where(step * per_step + i < count, 0.0, NEG), f32)
                for i in range(per_step)
            ],
            axis=0,
        )
        for half in range(2):
            update(half, keys, values, bias)
        return carry

    lax.fori_loop(0, (count + per_step - 1) // per_step, far, 0)

    def near(j, carry):
        which = core + 2 * j
        shift = (block - which) * BLK
        key_pos = lax.broadcasted_iota(jnp.int32, (BLK, rows), 0)
        token = lax.broadcasted_iota(jnp.int32, (BLK, rows), 1) % BLK
        bias = jnp.where(key_pos <= token + shift, 0.0, NEG)
        at = 2 * part_rows
        eighth = BLK // 8
        keys = jnp.concatenate([chunk_ref[i * 8 + which, at : at + eighth] for i in range(8)], axis=0)
        values = jnp.concatenate([chunk_ref[i * 8 + which, at + eighth :] for i in range(8)], axis=0)
        for half in range(2):
            update(half, keys, values, bias)
        return carry

    if not last:
        lax.fori_loop(0, (block - core + 2) // 2, near, 0)
    for half, ref in ((0, own_ref), (1, send_ref)):
        ref[0:HEAD_DIM, :] = acc_ref[half]
        ref[HEAD_DIM : HEAD_DIM + 1, :] = top_ref[half]
        ref[HEAD_DIM + 1 : HEAD_DIM + 2, :] = sum_ref[half]


def attend(scalars, own_q, other_q, chunk, state, local_blocks, per_step):
    heads = own_q.shape[1] // HEAD_DIM
    rows = heads * BLK
    length = scalars[0].shape[0] - len(state) // 2
    packed = jax.ShapeDtypeStruct((HEAD_DIM + 8, rows), f32)
    smem = pl.BlockSpec(memory_space=pltpu.SMEM)
    vmem = pl.BlockSpec(memory_space=pltpu.VMEM)
    scale = math.log2(math.e) / math.sqrt(HEAD_DIM)
    arrays = [own_q, other_q, chunk, *state]
    outs = [packed, packed]
    if not state:
        outs.append(jax.ShapeDtypeStruct((length + 1,), jnp.int32))
    return pl.pallas_call(
        functools.partial(attend_kernel, scale, per_step, local_blocks, len(state) > 0),
        out_shape=outs,
        in_specs=[smem] * len(scalars) + [vmem] * len(arrays),
        out_specs=[vmem, vmem, smem][: len(outs)],
        scratch_shapes=[
            pltpu.VMEM((2 * rows, HEAD_DIM), bf16),
            pltpu.VMEM((2, 1, rows), f32),
            pltpu.VMEM((2, 1, rows), f32),
            pltpu.VMEM((2, HEAD_DIM, rows), f32),
        ],
        compiler_params=pltpu.CompilerParams(vmem_limit_bytes=24 * 1024 * 1024),
        cost_estimate=pl.CostEstimate(
            flops=2 * rows * 40 * chunk.shape[1] * HEAD_DIM,
            bytes_accessed=2 * chunk.size,
            transcendentals=rows * 40 * chunk.shape[1],
        ),
    )(*scalars, *arrays)


def merge_kernel(own_ref, got_ref, out_ref):
    own_top = own_ref[HEAD_DIM : HEAD_DIM + 1, :]
    got_top = got_ref[HEAD_DIM : HEAD_DIM + 1, :]
    top = jnp.maximum(own_top, got_top)
    own_w = jnp.exp2(own_top - top)
    got_w = jnp.exp2(got_top - top)
    total = own_w * own_ref[HEAD_DIM + 1 : HEAD_DIM + 2, :] + got_w * got_ref[HEAD_DIM + 1 : HEAD_DIM + 2, :]
    mixed = (own_ref[0:HEAD_DIM, :] * own_w + got_ref[0:HEAD_DIM, :] * got_w) / total
    heads = mixed.shape[1] // BLK
    for h in range(heads):
        piece = mixed[:, h * BLK : (h + 1) * BLK].T.astype(bf16)
        for i in range(out_ref.shape[0]):
            out_ref[i, :, pl.ds(h * HEAD_DIM, HEAD_DIM)] = piece


def merge(own, got, copies):
    heads = own.shape[1] // BLK
    vmem = pl.BlockSpec(memory_space=pltpu.VMEM)
    return pl.pallas_call(
        merge_kernel,
        out_shape=jax.ShapeDtypeStruct((copies, BLK, heads * HEAD_DIM), bf16),
        in_specs=[vmem, vmem],
        out_specs=vmem,
        compiler_params=pltpu.CompilerParams(vmem_limit_bytes=12 * 1024 * 1024),
    )(own, got)


def product_kernel(tile, weight_count, pick_ref, x_ref, *refs):
    weight_refs, add_ref, out_ref = refs[:weight_count], refs[weight_count:-1], refs[-1]
    x = x_ref[:, pick_ref[0]] if x_ref.shape[1] > out_ref.shape[1] else x_ref[...]
    x = x.reshape(-1, x.shape[-1])
    width = weight_refs[0].shape[1]
    block = out_ref.shape[:-1] + (tile,)
    for i, weight_ref in enumerate(weight_refs):
        for first in range(0, width, tile):
            total = jnp.dot(x, weight_ref[:, first : first + tile], preferred_element_type=f32)
            columns = slice(i * width + first, i * width + first + tile)
            if add_ref:
                total = total + add_ref[0][..., columns].reshape(total.shape).astype(f32)
            out_ref[..., columns] = total.astype(bf16).reshape(block)


def product(x, weights, tile, pick=None, add=None):
    blocks, pair, tokens, inputs = x.shape
    taken = pair if pick is None else 1
    pick = jnp.zeros((1,), jnp.int32) if pick is None else pick.astype(jnp.int32).reshape(1)
    vmem = pl.BlockSpec(memory_space=pltpu.VMEM)
    operands = [x, *weights] if add is None else [x, *weights, add]
    rows = blocks * taken * tokens
    columns = weights[0].shape[1] * len(weights)
    return pl.pallas_call(
        functools.partial(product_kernel, tile, len(weights)),
        out_shape=jax.ShapeDtypeStruct((blocks, taken, tokens, columns), bf16),
        in_specs=[pl.BlockSpec(memory_space=pltpu.SMEM)] + [vmem] * len(operands),
        out_specs=vmem,
        compiler_params=pltpu.CompilerParams(vmem_limit_bytes=20 * 1024 * 1024),
        cost_estimate=pl.CostEstimate(
            flops=2 * rows * inputs * columns,
            bytes_accessed=2 * (rows * inputs + inputs * columns + rows * columns),
            transcendentals=0,
        ),
    )(pick, *operands)


VMEM = pl.BlockSpec(memory_space=pltpu.VMEM)
SMEM = pl.BlockSpec(memory_space=pltpu.SMEM)


def small_call(kernel, outs, scalars, arrays, moved):
    return pl.pallas_call(
        kernel,
        out_shape=outs,
        in_specs=[SMEM] * len(scalars) + [VMEM] * len(arrays),
        out_specs=jax.tree.map(lambda _: VMEM, outs),
        compiler_params=pltpu.CompilerParams(vmem_limit_bytes=16 * 1024 * 1024),
        cost_estimate=pl.CostEstimate(flops=moved, bytes_accessed=moved, transcendentals=0),
    )(*scalars, *arrays)


def columns_kernel(place_ref, mine_ref, theirs_ref, gate_ref, up_ref, *out_refs):
    y, side = place_ref[0], place_ref[1]
    n = mine_ref.shape[2]
    x = jnp.concatenate(
        [ref[(y + i) % 4, s] for s in (1 - side, side) for i in range(4) for ref in (mine_ref, theirs_ref)],
        axis=0,
    )
    step = pl.program_id(0)

    def put(weight_ref):
        total = jnp.dot(x, weight_ref[...], preferred_element_type=f32).astype(bf16)
        for i, ref in enumerate(out_refs):
            ref[...] = total[i * n : (i + 1) * n]

    half = pl.num_programs(0) // 2
    pl.when(step < half)(functools.partial(put, gate_ref))
    pl.when(step >= half)(functools.partial(put, up_ref))


def partial_columns(place, mine, theirs, gate, up):
    tile = 896
    inputs, width = gate.shape
    count = width // tile
    tokens = mine.shape[2]
    whole = pl.BlockSpec(mine.shape, lambda n, p: (0, 0, 0, 0))
    rows = 16 * tokens
    return pl.pallas_call(
        columns_kernel,
        out_shape=(jax.ShapeDtypeStruct((tokens, 2 * width), bf16),) * 16,
        grid_spec=pltpu.PrefetchScalarGridSpec(
            num_scalar_prefetch=1,
            grid=(2 * count,),
            in_specs=[
                whole,
                whole,
                pl.BlockSpec((inputs, tile), lambda n, p: (0, jnp.minimum(n, count - 1))),
                pl.BlockSpec((inputs, tile), lambda n, p: (0, jnp.maximum(n - count, 0))),
            ],
            out_specs=(pl.BlockSpec((tokens, tile), lambda n, p: (0, n)),) * 16,
        ),
        compiler_params=pltpu.CompilerParams(vmem_limit_bytes=60 * 1024 * 1024),
        cost_estimate=pl.CostEstimate(
            flops=4 * rows * inputs * width,
            bytes_accessed=2 * (rows * inputs + 2 * inputs * width + 2 * rows * width),
            transcendentals=0,
        ),
    )(place, mine, theirs, gate, up)


def add_pieces(*pieces):
    def kernel(*refs):
        refs[-1][...] = sum(r[...].astype(f32) for r in refs[:-1]).astype(bf16)

    first = pieces[0]
    return small_call(kernel, jax.ShapeDtypeStruct(first.shape, bf16), (), pieces, 2 * first.size)


def add_halves(*halves):
    count = len(halves[0])

    def kernel(*refs):
        for i in range(len(halves)):
            mine = refs[i * count : (i + 1) * count]
            refs[-1][i] = sum(r[...].astype(f32) for r in mine).astype(bf16)

    first = halves[0][0]
    out = jax.ShapeDtypeStruct((len(halves), *first.shape), bf16)
    return small_call(kernel, out, (), [p for h in halves for p in h], 8 * first.size)


def gated(halves, got, factor):
    count = len(halves[0])
    tokens, width = halves[0][0].shape[0], halves[0][0].shape[1] // 2

    def kernel(*refs):
        got_ref, factor_ref, out_ref = refs[-3:]
        for i in range(len(halves)):
            rows = pl.ds(i * tokens, tokens)
            mine = refs[i * count : (i + 1) * count]
            scale = factor_ref[rows, :]

            def total(columns):
                parts = sum(r[:, columns].astype(f32) for r in mine)
                return (parts + got_ref[i, :, columns].astype(f32)) * scale

            gate = total(slice(0, width))
            up = total(slice(width, 2 * width))
            out_ref[rows, :] = (gate / (1.0 + jnp.exp(-gate)) * up).astype(bf16)

    out = jax.ShapeDtypeStruct((tokens * len(halves), width), bf16)
    arrays = [p for h in halves for p in h] + [got, factor[:, None]]
    return small_call(kernel, out, (), arrays, 16 * tokens * width)


def down_product(pieces, weight):
    tile = 512
    count, tokens, inputs = len(pieces), pieces[0].shape[0] // 2, pieces[0].shape[1]
    width = weight.shape[1]

    def kernel(*refs):
        weight_ref, keep_ref, give_ref = refs[count:]
        x = jnp.concatenate([p[...] for p in refs[:count]], axis=0)
        total = jnp.dot(x, weight_ref[...], preferred_element_type=f32)
        for i in range(count):
            at = 2 * i * tokens
            keep_ref[i] = total[at : at + tokens]
            give_ref[i] = total[at + tokens : at + 2 * tokens].astype(bf16)

    by_column = pl.BlockSpec((count, tokens, tile), lambda n: (0, 0, n))
    specs = [pl.BlockSpec((2 * tokens, inputs), lambda n: (0, 0))] * count
    return pl.pallas_call(
        kernel,
        grid=(width // tile,),
        out_shape=(
            jax.ShapeDtypeStruct((count, tokens, width), f32),
            jax.ShapeDtypeStruct((count, tokens, width), bf16),
        ),
        in_specs=specs + [pl.BlockSpec((inputs, tile), lambda n: (0, n))],
        out_specs=(by_column, by_column),
        compiler_params=pltpu.CompilerParams(vmem_limit_bytes=24 * 1024 * 1024),
        cost_estimate=pl.CostEstimate(
            flops=4 * count * tokens * inputs * width,
            bytes_accessed=2 * (2 * count * tokens * inputs + inputs * width + 3 * count * tokens * width),
            transcendentals=0,
        ),
    )(*pieces, weight)


def join_blocks(place, near, far):
    def kernel(place_ref, near_ref, near_got_ref, far_ref, far_got_ref, out_ref):
        y, side = place_ref[0], place_ref[1]
        for i, (kept_ref, got_ref, first) in enumerate(
            (
                (near_ref, near_got_ref, 0),
                (near_ref, near_got_ref, 2),
                (far_ref, far_got_ref, 0),
                (near_ref, near_got_ref, 4),
            )
        ):
            for j in range(2):
                at = 2 * ((y + i) % 4) + (side if j == 0 else 1 - side)
                out_ref[at] = (kept_ref[first + j] + got_ref[first + j].astype(f32)).astype(bf16)

    out = jax.ShapeDtypeStruct((8, *near[0].shape[1:]), bf16)
    return small_call(kernel, out, (place,), (*near, *far), 4 * near[0].size)


def to_right(x):
    return lax.ppermute(x, "y", [(i, (i + 1) % 4) for i in range(4)])


def to_left(x):
    return lax.ppermute(x, "y", [(i, (i + 3) % 4) for i in range(4)])


def ring_start(pieces):
    right, left, opposite = pieces[2:4], pieces[6:8], pieces[4:6]
    return to_right(opposite[0]), to_left(opposite[1]), to_right(right[1]), to_left(left[0])


def ring_middle(pieces, from_left, from_right):
    return add_pieces(pieces[2], from_left), add_pieces(pieces[7], from_right)


def ring_end(pieces, arrived, sums):
    third_left, third_right = to_right(sums[0]), to_left(sums[1])
    return (pieces[0], arrived[3], third_left), (pieces[1], arrived[2], third_right)


def gather_start(mine):
    return to_right(mine), to_left(mine)


def pack_kernel(within_ref, group_ref, keys_ref, values_ref, near_keys_ref, near_values_ref, out_ref):
    eighth = BLK // 8
    rows = (out_ref.shape[1] - 2 * eighth) // 2
    goal = pl.program_id(0)
    near = pl.ds(pl.multiple_of(group_ref[0] * eighth, eighth), eighth)
    for i in range(out_ref.shape[0]):
        at = within_ref[goal, i]
        out_ref[i, 0:rows] = keys_ref[at, 0:rows]
        out_ref[i, rows : 2 * rows] = values_ref[at, 0:rows]
        out_ref[i, 2 * rows : 2 * rows + eighth] = near_keys_ref[0, near]
        out_ref[i, 2 * rows + eighth :] = near_values_ref[0, near]


def pack(within, group, keys, values, near_keys, near_values, rows):
    def of_group(x, height):
        return pl.BlockSpec((x.shape[0] // KV_HEADS, height, HEAD_DIM), lambda n, s, g: (n, 0, 0))

    arrays = ((keys, rows), (values, rows), (near_keys, BLK), (near_values, BLK))
    height = 2 * rows + BLK // 4
    return pl.pallas_call(
        pack_kernel,
        out_shape=jax.ShapeDtypeStruct((64, height, HEAD_DIM), bf16),
        grid_spec=pltpu.PrefetchScalarGridSpec(
            num_scalar_prefetch=2,
            grid=(8,),
            in_specs=[of_group(*x) for x in arrays],
            out_specs=pl.BlockSpec((8, height, HEAD_DIM), lambda n, s, g: (n, 0, 0)),
        ),
        compiler_params=pltpu.CompilerParams(vmem_limit_bytes=60 * 1024 * 1024),
        cost_estimate=pl.CostEstimate(flops=0, bytes_accessed=64 * height * 512, transcendentals=0),
    )(within, group.astype(jnp.int32).reshape(1), *[x for x, _ in arrays])


def exchange(x, axes):
    return lax.all_to_all(x, axes, split_axis=0, concat_axis=0, tiled=True)


def swap(x, axis="core"):
    return lax.ppermute(x, axis, [(0, 1), (1, 0)])


def spread(x, copies):
    return jnp.broadcast_to(x[None], (copies,) + x.shape)


def take(x, index, axis):
    return lax.dynamic_index_in_dim(x, index, axis, keepdims=False)


def local(
    queries,
    cache_keys,
    cache_values,
    stretch_keys,
    stretch_values,
    block_lists,
    out_weight,
    residual,
    norm_gain,
    gate_weight,
    up_weight,
    down_weight,
):
    core = lax.axis_index("core")
    side = lax.axis_index("xl")
    col = lax.axis_index(COL)
    group = lax.axis_index(ZXH)
    me = lax.axis_index(ROW) * 8 + col
    local_blocks = cache_keys.shape[1] // BLK
    tokens_here = residual.shape[0]

    matched = block_lists // local_blocks == me
    within = jnp.sum(jnp.where(matched, block_lists % local_blocks, 0), axis=2)
    source = (jnp.arange(KV_HEADS, dtype=jnp.int32)[:, None] * local_blocks + within.T).reshape(-1)

    piece = BLK // 4
    flat_keys = cache_keys.reshape(4 * KV_HEADS * local_blocks, piece, HEAD_DIM)
    flat_values = cache_values.reshape(4 * KV_HEADS * local_blocks, piece, HEAD_DIM)

    def pick(flat, first, count):
        index = 4 * source[:, None] + jnp.arange(first, first + count, dtype=jnp.int32)[None, :]
        return flat[index].reshape(64, count * piece, HEAD_DIM)

    blocked = (KV_HEADS * local_blocks, BLK, HEAD_DIM)
    first = pack(
        within.T, group, cache_keys.reshape(blocked), cache_values.reshape(blocked),
        stretch_keys, stretch_values, 3 * piece,
    )
    first = exchange(first, CHIP)
    second = [pick(flat_keys, 3, 1), pick(flat_values, 3, 1)]
    second = exchange(jnp.concatenate(second, axis=1), CHIP)
    my_list = block_lists[col, group]
    place = jnp.stack([core, col]).astype(jnp.int32)
    other_queries = swap(queries)
    own, send, order = attend((my_list, place), queries, other_queries, first, (), local_blocks, 5)
    own, send = attend((order,), queries, other_queries, second, (own, send), local_blocks, 16)
    attended = exchange(merge(own, swap(send), 8), COL).reshape(8, 2, tokens_here, -1)

    def row_sum(give, mine, pick, weight):
        both = product(mine, (weight,), 512, pick, add=swap(give))
        return jnp.sum(exchange(both.reshape(8, tokens_here, -1), ZXH).astype(f32), axis=0)

    give = product(attended, (out_weight,), 512, 1 - core)
    stream = residual.astype(f32) + row_sum(give, attended, core, out_weight)
    gain = norm_gain.astype(f32)[None, :]
    own_rows = exchange(spread((stream * gain).astype(bf16), 8), ZXH)
    other_rows = swap(own_rows)

    def squares(x):
        plain = x.astype(f32) / gain[None]
        return jnp.sum(plain * plain, axis=2)

    squares = jnp.stack([squares(own_rows), squares(other_rows)], axis=1)

    by_pair = (4, 2, tokens_here, own_rows.shape[-1])
    where = jnp.stack([lax.axis_index("y"), side]).astype(jnp.int32)
    columns = partial_columns(
        where, own_rows.reshape(by_pair), other_rows.reshape(by_pair), gate_weight, up_weight
    )
    theirs, mine = columns[:8], columns[8:]
    arrived = ring_start(theirs)
    sums = ring_middle(theirs, *arrived[:2])
    sums, mine, squares = lax.optimization_barrier((sums, mine, squares))
    squares = exchange(squares, COL)
    halves = ring_end(theirs, arrived, sums)
    mine_arrived = ring_start(mine)
    halves, squares = lax.optimization_barrier((halves, squares))
    got = swap(add_halves(*halves), "xl")
    factor = lax.rsqrt(jnp.sum(squares, axis=0).reshape(-1) / D + 1e-05)
    halves = ring_end(mine, mine_arrived, ring_middle(mine, *mine_arrived[:2]))
    hidden = gated(halves, got, factor)
    first, hidden_got = lax.optimization_barrier((gather_start(hidden), swap(hidden, "xl")))
    got_left, got_right = to_right(hidden_got), to_left(hidden_got)
    mine_far = to_right(first[0])
    got_far = to_left(got_right)
    near = (hidden, hidden_got, first[1], got_right, first[0], got_left)
    kept, give = down_product(near, down_weight)
    far_kept, far_give = down_product((mine_far, got_far), down_weight)
    down = join_blocks(where, (kept, swap(give)), (far_kept, swap(far_give)))
    mlp = jnp.sum(exchange(down, ZXH).astype(f32), axis=0)
    return (stream + mlp).astype(bf16)


def solution(mesh):
    mesh = Mesh(mesh.devices.reshape(4, 2, 2, 4, 2), AXES)
    in_specs = (
        P(COL, ROW),
        P(None, ROW + COL, None),
        P(None, ROW + COL, None),
        P(None, COL, None),
        P(None, COL, None),
        P(),
        P(ROW, COL),
        P(ROW, COL),
        P(COL),
        P(COL, ROW),
        P(COL, ROW),
        P(ROW, COL),
    )
    return jax.shard_map(local, mesh=mesh, in_specs=in_specs, out_specs=P(ROW, COL), check_vma=False)
```

```python
import functools
import math

import jax
import jax.numpy as jnp
from jax import lax
from jax.experimental import pallas as pl
from jax.experimental.pallas import tpu as pltpu
from jax.sharding import Mesh, PartitionSpec as P

D = 8192
KV_HEADS = 8
HEAD_DIM = 128
BLK = 128
GROUP = 8
AXES = ("z", "xh", "core", "y", "xl")
ROW = ("z", "xh", "core")
ZXH = ("z", "xh")
COL = ("y", "xl")
CHIP = ("z", "xh", "y", "xl")
NEG = -1e30
bf16 = jnp.bfloat16
f32 = jnp.float32


def nt_dot(a, b):
    return lax.dot_general(a, b, (((1,), (1,)), ((), ())), preferred_element_type=f32)


def tn_dot(a, b):
    return lax.dot_general(a, b, (((0,), (0,)), ((), ())), preferred_element_type=f32)


def attend_kernel(scale, per_step, local_blocks, last, *refs):
    if last:
        order_ref, own_q_ref, other_q_ref, chunk_ref, own_in_ref, send_in_ref = refs[:6]
    else:
        list_ref, place_ref, own_q_ref, other_q_ref, chunk_ref = refs[:5]
        order_ref = refs[7]
    own_ref, send_ref = refs[6:8] if last else refs[5:7]
    q_ref, top_ref, sum_ref, acc_ref = refs[-4:]
    length = order_ref.shape[0] - 1
    part_rows = (chunk_ref.shape[1] - (0 if last else BLK // 4)) // 2
    heads = own_q_ref.shape[1] // HEAD_DIM
    rows = heads * BLK
    for h in range(heads):
        cols = pl.ds(h * HEAD_DIM, HEAD_DIM)
        q_ref[pl.ds(h * BLK, BLK), :] = own_q_ref[:, cols]
        q_ref[pl.ds(rows + h * BLK, BLK), :] = other_q_ref[:, cols]
    if last:
        for half, ref in ((0, own_in_ref), (1, send_in_ref)):
            acc_ref[half] = ref[0:HEAD_DIM, :]
            top_ref[half] = ref[HEAD_DIM : HEAD_DIM + 1, :]
            sum_ref[half] = ref[HEAD_DIM + 1 : HEAD_DIM + 2, :]
        count = order_ref[length]
    else:
        core = place_ref[0]
        block = place_ref[1]
        top_ref[...] = jnp.full_like(top_ref, NEG)
        sum_ref[...] = jnp.zeros_like(sum_ref)
        acc_ref[...] = jnp.zeros_like(acc_ref)

        def collect(i, count):
            device = list_ref[i] // local_blocks
            row = device // 8
            order_ref[count] = (row // 2) * 8 + device % 8
            return count + jnp.where(row % 2 == core, 1, 0)

        count = lax.fori_loop(0, length, collect, jnp.int32(0))
        order_ref[length] = count

    def update(half, keys, values, bias):
        part = pl.ds(half * rows, rows)
        scores = nt_dot(keys, q_ref[part, :]) * scale + bias
        old = top_ref[half]
        new = jnp.maximum(old, jnp.max(scores, axis=0, keepdims=True))
        weights = jnp.exp2(scores - new)
        decay = jnp.exp2(old - new)
        top_ref[half] = new
        sum_ref[half] = sum_ref[half] * decay + jnp.sum(weights, axis=0, keepdims=True)
        acc_ref[half] = acc_ref[half] * decay + tn_dot(values, weights.astype(bf16))

    def far(step, carry):
        slots = [order_ref[jnp.minimum(step * per_step + i, count - 1)] for i in range(per_step)]
        keys = jnp.concatenate([chunk_ref[s, 0:part_rows] for s in slots], axis=0)
        values = jnp.concatenate([chunk_ref[s, part_rows : 2 * part_rows] for s in slots], axis=0)
        bias = jnp.concatenate(
            [
                jnp.full((part_rows, 1), jnp.where(step * per_step + i < count, 0.0, NEG), f32)
                for i in range(per_step)
            ],
            axis=0,
        )
        for half in range(2):
            update(half, keys, values, bias)
        return carry

    lax.fori_loop(0, (count + per_step - 1) // per_step, far, 0)

    def near(j, carry):
        which = core + 2 * j
        shift = (block - which) * BLK
        key_pos = lax.broadcasted_iota(jnp.int32, (BLK, rows), 0)
        token = lax.broadcasted_iota(jnp.int32, (BLK, rows), 1) % BLK
        bias = jnp.where(key_pos <= token + shift, 0.0, NEG)
        at = 2 * part_rows
        eighth = BLK // 8
        keys = jnp.concatenate([chunk_ref[i * 8 + which, at : at + eighth] for i in range(8)], axis=0)
        values = jnp.concatenate([chunk_ref[i * 8 + which, at + eighth :] for i in range(8)], axis=0)
        for half in range(2):
            update(half, keys, values, bias)
        return carry

    if not last:
        lax.fori_loop(0, (block - core + 2) // 2, near, 0)
    for half, ref in ((0, own_ref), (1, send_ref)):
        ref[0:HEAD_DIM, :] = acc_ref[half]
        ref[HEAD_DIM : HEAD_DIM + 1, :] = top_ref[half]
        ref[HEAD_DIM + 1 : HEAD_DIM + 2, :] = sum_ref[half]


def attend(scalars, own_q, other_q, chunk, state, local_blocks, per_step):
    heads = own_q.shape[1] // HEAD_DIM
    rows = heads * BLK
    length = scalars[0].shape[0] - len(state) // 2
    packed = jax.ShapeDtypeStruct((HEAD_DIM + 8, rows), f32)
    smem = pl.BlockSpec(memory_space=pltpu.SMEM)
    vmem = pl.BlockSpec(memory_space=pltpu.VMEM)
    scale = math.log2(math.e) / math.sqrt(HEAD_DIM)
    arrays = [own_q, other_q, chunk, *state]
    outs = [packed, packed]
    if not state:
        outs.append(jax.ShapeDtypeStruct((length + 1,), jnp.int32))
    return pl.pallas_call(
        functools.partial(attend_kernel, scale, per_step, local_blocks, len(state) > 0),
        out_shape=outs,
        in_specs=[smem] * len(scalars) + [vmem] * len(arrays),
        out_specs=[vmem, vmem, smem][: len(outs)],
        scratch_shapes=[
            pltpu.VMEM((2 * rows, HEAD_DIM), bf16),
            pltpu.VMEM((2, 1, rows), f32),
            pltpu.VMEM((2, 1, rows), f32),
            pltpu.VMEM((2, HEAD_DIM, rows), f32),
        ],
        compiler_params=pltpu.CompilerParams(vmem_limit_bytes=24 * 1024 * 1024),
        cost_estimate=pl.CostEstimate(
            flops=2 * rows * 40 * chunk.shape[1] * HEAD_DIM,
            bytes_accessed=2 * chunk.size,
            transcendentals=rows * 40 * chunk.shape[1],
        ),
    )(*scalars, *arrays)


def merge_kernel(own_ref, got_ref, out_ref):
    own_top = own_ref[HEAD_DIM : HEAD_DIM + 1, :]
    got_top = got_ref[HEAD_DIM : HEAD_DIM + 1, :]
    top = jnp.maximum(own_top, got_top)
    own_w = jnp.exp2(own_top - top)
    got_w = jnp.exp2(got_top - top)
    total = own_w * own_ref[HEAD_DIM + 1 : HEAD_DIM + 2, :] + got_w * got_ref[HEAD_DIM + 1 : HEAD_DIM + 2, :]
    mixed = (own_ref[0:HEAD_DIM, :] * own_w + got_ref[0:HEAD_DIM, :] * got_w) / total
    heads = mixed.shape[1] // BLK
    for h in range(heads):
        piece = mixed[:, h * BLK : (h + 1) * BLK].T.astype(bf16)
        for i in range(out_ref.shape[0]):
            out_ref[i, :, pl.ds(h * HEAD_DIM, HEAD_DIM)] = piece


def merge(own, got, copies):
    heads = own.shape[1] // BLK
    vmem = pl.BlockSpec(memory_space=pltpu.VMEM)
    return pl.pallas_call(
        merge_kernel,
        out_shape=jax.ShapeDtypeStruct((copies, BLK, heads * HEAD_DIM), bf16),
        in_specs=[vmem, vmem],
        out_specs=vmem,
        compiler_params=pltpu.CompilerParams(vmem_limit_bytes=12 * 1024 * 1024),
    )(own, got)


def product_kernel(tile, weight_count, pick_ref, x_ref, *refs):
    weight_refs, add_ref, out_ref = refs[:weight_count], refs[weight_count:-1], refs[-1]
    x = x_ref[:, pick_ref[0]] if x_ref.shape[1] > out_ref.shape[1] else x_ref[...]
    x = x.reshape(-1, x.shape[-1])
    width = weight_refs[0].shape[1]
    block = out_ref.shape[:-1] + (tile,)
    for i, weight_ref in enumerate(weight_refs):
        for first in range(0, width, tile):
            total = jnp.dot(x, weight_ref[:, first : first + tile], preferred_element_type=f32)
            columns = slice(i * width + first, i * width + first + tile)
            if add_ref:
                total = total + add_ref[0][..., columns].reshape(total.shape).astype(f32)
            out_ref[..., columns] = total.astype(bf16).reshape(block)


def product(x, weights, tile, pick=None, add=None):
    blocks, pair, tokens, inputs = x.shape
    taken = pair if pick is None else 1
    pick = jnp.zeros((1,), jnp.int32) if pick is None else pick.astype(jnp.int32).reshape(1)
    vmem = pl.BlockSpec(memory_space=pltpu.VMEM)
    operands = [x, *weights] if add is None else [x, *weights, add]
    rows = blocks * taken * tokens
    columns = weights[0].shape[1] * len(weights)
    return pl.pallas_call(
        functools.partial(product_kernel, tile, len(weights)),
        out_shape=jax.ShapeDtypeStruct((blocks, taken, tokens, columns), bf16),
        in_specs=[pl.BlockSpec(memory_space=pltpu.SMEM)] + [vmem] * len(operands),
        out_specs=vmem,
        compiler_params=pltpu.CompilerParams(vmem_limit_bytes=20 * 1024 * 1024),
        cost_estimate=pl.CostEstimate(
            flops=2 * rows * inputs * columns,
            bytes_accessed=2 * (rows * inputs + inputs * columns + rows * columns),
            transcendentals=0,
        ),
    )(pick, *operands)


VMEM = pl.BlockSpec(memory_space=pltpu.VMEM)
SMEM = pl.BlockSpec(memory_space=pltpu.SMEM)


def small_call(kernel, outs, scalars, arrays, moved):
    return pl.pallas_call(
        kernel,
        out_shape=outs,
        in_specs=[SMEM] * len(scalars) + [VMEM] * len(arrays),
        out_specs=jax.tree.map(lambda _: VMEM, outs),
        compiler_params=pltpu.CompilerParams(vmem_limit_bytes=16 * 1024 * 1024),
        cost_estimate=pl.CostEstimate(flops=moved, bytes_accessed=moved, transcendentals=0),
    )(*scalars, *arrays)


def columns_kernel(place_ref, mine_ref, theirs_ref, gate_ref, up_ref, *out_refs):
    y, side = place_ref[0], place_ref[1]
    n = mine_ref.shape[2]
    x = jnp.concatenate(
        [ref[(y + i) % 4, s] for s in (1 - side, side) for i in range(4) for ref in (mine_ref, theirs_ref)],
        axis=0,
    )
    step = pl.program_id(0)

    def put(weight_ref):
        total = jnp.dot(x, weight_ref[...], preferred_element_type=f32).astype(bf16)
        for i, ref in enumerate(out_refs):
            ref[...] = total[i * n : (i + 1) * n]

    half = pl.num_programs(0) // 2
    pl.when(step < half)(functools.partial(put, gate_ref))
    pl.when(step >= half)(functools.partial(put, up_ref))


def partial_columns(place, mine, theirs, gate, up):
    tile = 896
    inputs, width = gate.shape
    count = width // tile
    tokens = mine.shape[2]
    whole = pl.BlockSpec(mine.shape, lambda n, p: (0, 0, 0, 0))
    rows = 16 * tokens
    return pl.pallas_call(
        columns_kernel,
        out_shape=(jax.ShapeDtypeStruct((tokens, 2 * width), bf16),) * 16,
        grid_spec=pltpu.PrefetchScalarGridSpec(
            num_scalar_prefetch=1,
            grid=(2 * count,),
            in_specs=[
                whole,
                whole,
                pl.BlockSpec((inputs, tile), lambda n, p: (0, jnp.minimum(n, count - 1))),
                pl.BlockSpec((inputs, tile), lambda n, p: (0, jnp.maximum(n - count, 0))),
            ],
            out_specs=(pl.BlockSpec((tokens, tile), lambda n, p: (0, n)),) * 16,
        ),
        compiler_params=pltpu.CompilerParams(vmem_limit_bytes=60 * 1024 * 1024),
        cost_estimate=pl.CostEstimate(
            flops=4 * rows * inputs * width,
            bytes_accessed=2 * (rows * inputs + 2 * inputs * width + 2 * rows * width),
            transcendentals=0,
        ),
    )(place, mine, theirs, gate, up)


def add_pieces(*pieces):
    def kernel(*refs):
        refs[-1][...] = sum(r[...].astype(f32) for r in refs[:-1]).astype(bf16)

    first = pieces[0]
    return small_call(kernel, jax.ShapeDtypeStruct(first.shape, bf16), (), pieces, 2 * first.size)


def add_halves(*halves):
    count = len(halves[0])

    def kernel(*refs):
        for i in range(len(halves)):
            mine = refs[i * count : (i + 1) * count]
            refs[-1][i] = sum(r[...].astype(f32) for r in mine).astype(bf16)

    first = halves[0][0]
    out = jax.ShapeDtypeStruct((len(halves), *first.shape), bf16)
    return small_call(kernel, out, (), [p for h in halves for p in h], 8 * first.size)


def gated(halves, got, factor):
    count = len(halves[0])
    tokens, width = halves[0][0].shape[0], halves[0][0].shape[1] // 2

    def kernel(*refs):
        got_ref, factor_ref, out_ref = refs[-3:]
        for i in range(len(halves)):
            rows = pl.ds(i * tokens, tokens)
            mine = refs[i * count : (i + 1) * count]
            scale = factor_ref[rows, :]

            def total(columns):
                parts = sum(r[:, columns].astype(f32) for r in mine)
                return (parts + got_ref[i, :, columns].astype(f32)) * scale

            gate = total(slice(0, width))
            up = total(slice(width, 2 * width))
            out_ref[rows, :] = (gate / (1.0 + jnp.exp(-gate)) * up).astype(bf16)

    out = jax.ShapeDtypeStruct((tokens * len(halves), width), bf16)
    arrays = [p for h in halves for p in h] + [got, factor[:, None]]
    return small_call(kernel, out, (), arrays, 16 * tokens * width)


def down_product(pieces, weight):
    tile = 512
    count, tokens, inputs = len(pieces), pieces[0].shape[0] // 2, pieces[0].shape[1]
    width = weight.shape[1]

    def kernel(*refs):
        weight_ref, keep_ref, give_ref = refs[count:]
        x = jnp.concatenate([p[...] for p in refs[:count]], axis=0)
        total = jnp.dot(x, weight_ref[...], preferred_element_type=f32)
        for i in range(count):
            at = 2 * i * tokens
            keep_ref[i] = total[at : at + tokens]
            give_ref[i] = total[at + tokens : at + 2 * tokens].astype(bf16)

    by_column = pl.BlockSpec((count, tokens, tile), lambda n: (0, 0, n))
    specs = [pl.BlockSpec((2 * tokens, inputs), lambda n: (0, 0))] * count
    return pl.pallas_call(
        kernel,
        grid=(width // tile,),
        out_shape=(
            jax.ShapeDtypeStruct((count, tokens, width), f32),
            jax.ShapeDtypeStruct((count, tokens, width), bf16),
        ),
        in_specs=specs + [pl.BlockSpec((inputs, tile), lambda n: (0, n))],
        out_specs=(by_column, by_column),
        compiler_params=pltpu.CompilerParams(vmem_limit_bytes=24 * 1024 * 1024),
        cost_estimate=pl.CostEstimate(
            flops=4 * count * tokens * inputs * width,
            bytes_accessed=2 * (2 * count * tokens * inputs + inputs * width + 3 * count * tokens * width),
            transcendentals=0,
        ),
    )(*pieces, weight)


def join_blocks(place, near, far):
    def kernel(place_ref, near_ref, near_got_ref, far_ref, far_got_ref, out_ref):
        y, side = place_ref[0], place_ref[1]
        for i, (kept_ref, got_ref, first) in enumerate(
            (
                (near_ref, near_got_ref, 0),
                (near_ref, near_got_ref, 2),
                (far_ref, far_got_ref, 0),
                (near_ref, near_got_ref, 4),
            )
        ):
            for j in range(2):
                at = 2 * ((y + i) % 4) + (side if j == 0 else 1 - side)
                out_ref[at] = (kept_ref[first + j] + got_ref[first + j].astype(f32)).astype(bf16)

    out = jax.ShapeDtypeStruct((8, *near[0].shape[1:]), bf16)
    return small_call(kernel, out, (place,), (*near, *far), 4 * near[0].size)


def to_right(x):
    return lax.ppermute(x, "y", [(i, (i + 1) % 4) for i in range(4)])


def to_left(x):
    return lax.ppermute(x, "y", [(i, (i + 3) % 4) for i in range(4)])


def ring_start(pieces):
    right, left, opposite = pieces[2:4], pieces[6:8], pieces[4:6]
    return to_right(opposite[0]), to_left(opposite[1]), to_right(right[1]), to_left(left[0])


def ring_middle(pieces, from_left, from_right):
    return add_pieces(pieces[2], from_left), add_pieces(pieces[7], from_right)


def ring_end(pieces, arrived, sums):
    third_left, third_right = to_right(sums[0]), to_left(sums[1])
    return (pieces[0], arrived[3], third_left), (pieces[1], arrived[2], third_right)


def gather_start(mine):
    return to_right(mine), to_left(mine)


def pack_kernel(within_ref, group_ref, keys_ref, values_ref, near_keys_ref, near_values_ref, out_ref):
    eighth = BLK // 8
    rows = (out_ref.shape[1] - 2 * eighth) // 2
    goal = pl.program_id(0)
    near = pl.ds(pl.multiple_of(group_ref[0] * eighth, eighth), eighth)
    for i in range(out_ref.shape[0]):
        at = within_ref[goal, i]
        out_ref[i, 0:rows] = keys_ref[at, 0:rows]
        out_ref[i, rows : 2 * rows] = values_ref[at, 0:rows]
        out_ref[i, 2 * rows : 2 * rows + eighth] = near_keys_ref[0, near]
        out_ref[i, 2 * rows + eighth :] = near_values_ref[0, near]


def pack(within, group, keys, values, near_keys, near_values, rows):
    def of_group(x, height):
        return pl.BlockSpec((x.shape[0] // KV_HEADS, height, HEAD_DIM), lambda n, s, g: (n, 0, 0))

    arrays = ((keys, rows), (values, rows), (near_keys, BLK), (near_values, BLK))
    height = 2 * rows + BLK // 4
    return pl.pallas_call(
        pack_kernel,
        out_shape=jax.ShapeDtypeStruct((64, height, HEAD_DIM), bf16),
        grid_spec=pltpu.PrefetchScalarGridSpec(
            num_scalar_prefetch=2,
            grid=(8,),
            in_specs=[of_group(*x) for x in arrays],
            out_specs=pl.BlockSpec((8, height, HEAD_DIM), lambda n, s, g: (n, 0, 0)),
        ),
        compiler_params=pltpu.CompilerParams(vmem_limit_bytes=60 * 1024 * 1024),
        cost_estimate=pl.CostEstimate(flops=0, bytes_accessed=64 * height * 512, transcendentals=0),
    )(within, group.astype(jnp.int32).reshape(1), *[x for x, _ in arrays])


def exchange(x, axes):
    return lax.all_to_all(x, axes, split_axis=0, concat_axis=0, tiled=True)


def swap(x, axis="core"):
    return lax.ppermute(x, axis, [(0, 1), (1, 0)])


def spread(x, copies):
    return jnp.broadcast_to(x[None], (copies,) + x.shape)


def take(x, index, axis):
    return lax.dynamic_index_in_dim(x, index, axis, keepdims=False)


def local(
    queries,
    cache_keys,
    cache_values,
    stretch_keys,
    stretch_values,
    block_lists,
    out_weight,
    residual,
    norm_gain,
    gate_weight,
    up_weight,
    down_weight,
):
    core = lax.axis_index("core")
    side = lax.axis_index("xl")
    col = lax.axis_index(COL)
    group = lax.axis_index(ZXH)
    me = lax.axis_index(ROW) * 8 + col
    local_blocks = cache_keys.shape[1] // BLK
    tokens_here = residual.shape[0]

    matched = block_lists // local_blocks == me
    within = jnp.sum(jnp.where(matched, block_lists % local_blocks, 0), axis=2)
    source = (jnp.arange(KV_HEADS, dtype=jnp.int32)[:, None] * local_blocks + within.T).reshape(-1)

    piece = BLK // 4
    flat_keys = cache_keys.reshape(4 * KV_HEADS * local_blocks, piece, HEAD_DIM)
    flat_values = cache_values.reshape(4 * KV_HEADS * local_blocks, piece, HEAD_DIM)

    def pick(flat, first, count):
        index = 4 * source[:, None] + jnp.arange(first, first + count, dtype=jnp.int32)[None, :]
        return flat[index].reshape(64, count * piece, HEAD_DIM)

    blocked = (KV_HEADS * local_blocks, BLK, HEAD_DIM)
    first = pack(
        within.T, group, cache_keys.reshape(blocked), cache_values.reshape(blocked),
        stretch_keys, stretch_values, 3 * piece,
    )
    first = exchange(first, CHIP)
    second = [pick(flat_keys, 3, 1), pick(flat_values, 3, 1)]
    second = exchange(jnp.concatenate(second, axis=1), CHIP)
    my_list = block_lists[col, group]
    place = jnp.stack([core, col]).astype(jnp.int32)
    other_queries = swap(queries)
    own, send, order = attend((my_list, place), queries, other_queries, first, (), local_blocks, 5)
    own, send = attend((order,), queries, other_queries, second, (own, send), local_blocks, 16)
    attended = exchange(merge(own, swap(send), 8), COL).reshape(8, 2, tokens_here, -1)

    def row_sum(give, mine, pick, weight):
        both = product(mine, (weight,), 512, pick, add=swap(give))
        return jnp.sum(exchange(both.reshape(8, tokens_here, -1), ZXH).astype(f32), axis=0)

    give = product(attended, (out_weight,), 512, 1 - core)
    stream = residual.astype(f32) + row_sum(give, attended, core, out_weight)
    gain = norm_gain.astype(f32)[None, :]
    own_rows = exchange(spread((stream * gain).astype(bf16), 8), ZXH)
    other_rows = swap(own_rows)

    def squares(x):
        plain = x.astype(f32) / gain[None]
        return jnp.sum(plain * plain, axis=2)

    squares = jnp.stack([squares(own_rows), squares(other_rows)], axis=1)

    by_pair = (4, 2, tokens_here, own_rows.shape[-1])
    where = jnp.stack([lax.axis_index("y"), side]).astype(jnp.int32)
    columns = partial_columns(
        where, own_rows.reshape(by_pair), other_rows.reshape(by_pair), gate_weight, up_weight
    )
    theirs, mine = columns[:8], columns[8:]
    arrived = ring_start(theirs)
    sums = ring_middle(theirs, *arrived[:2])
    sums, mine, squares = lax.optimization_barrier((sums, mine, squares))
    squares = exchange(squares, COL)
    halves = ring_end(theirs, arrived, sums)
    mine_arrived = ring_start(mine)
    got = swap(add_halves(*halves), "xl")
    steps, squares = lax.optimization_barrier((mine_arrived[:2], squares))
    halves = ring_end(mine, mine_arrived, ring_middle(mine, *steps))
    factor = lax.rsqrt(jnp.sum(squares, axis=0).reshape(-1) / D + 1e-05)
    hidden = gated(halves, got, factor)
    first, hidden_got = lax.optimization_barrier((gather_start(hidden), swap(hidden, "xl")))
    got_left, got_right = to_right(hidden_got), to_left(hidden_got)
    mine_far = to_right(first[0])
    got_far = to_left(got_right)
    near = (hidden, hidden_got, first[1], got_right, first[0], got_left)
    kept, give = down_product(near, down_weight)
    far_kept, far_give = down_product((mine_far, got_far), down_weight)
    down = join_blocks(where, (kept, swap(give)), (far_kept, swap(far_give)))
    mlp = jnp.sum(exchange(down, ZXH).astype(f32), axis=0)
    return (stream + mlp).astype(bf16)


def solution(mesh):
    mesh = Mesh(mesh.devices.reshape(4, 2, 2, 4, 2), AXES)
    in_specs = (
        P(COL, ROW),
        P(None, ROW + COL, None),
        P(None, ROW + COL, None),
        P(None, COL, None),
        P(None, COL, None),
        P(),
        P(ROW, COL),
        P(ROW, COL),
        P(COL),
        P(COL, ROW),
        P(COL, ROW),
        P(ROW, COL),
    )
    return jax.shard_map(local, mesh=mesh, in_specs=in_specs, out_specs=P(ROW, COL), check_vma=False)
```

```python
import functools
import math

import jax
import jax.numpy as jnp
from jax import lax
from jax.experimental import pallas as pl
from jax.experimental.pallas import tpu as pltpu
from jax.sharding import Mesh, PartitionSpec as P

D = 8192
KV_HEADS = 8
HEAD_DIM = 128
BLK = 128
GROUP = 8
AXES = ("z", "xh", "core", "y", "xl")
ROW = ("z", "xh", "core")
ZXH = ("z", "xh")
COL = ("y", "xl")
CHIP = ("z", "xh", "y", "xl")
NEG = -1e30
bf16 = jnp.bfloat16
f32 = jnp.float32


def nt_dot(a, b):
    return lax.dot_general(a, b, (((1,), (1,)), ((), ())), preferred_element_type=f32)


def tn_dot(a, b):
    return lax.dot_general(a, b, (((0,), (0,)), ((), ())), preferred_element_type=f32)


def attend_kernel(scale, per_step, local_blocks, last, *refs):
    if last:
        order_ref, own_q_ref, other_q_ref, chunk_ref, own_in_ref, send_in_ref = refs[:6]
    else:
        list_ref, place_ref, own_q_ref, other_q_ref, chunk_ref = refs[:5]
        order_ref = refs[7]
    own_ref, send_ref = refs[6:8] if last else refs[5:7]
    q_ref, top_ref, sum_ref, acc_ref = refs[-4:]
    length = order_ref.shape[0] - 1
    part_rows = (chunk_ref.shape[1] - (0 if last else BLK // 4)) // 2
    heads = own_q_ref.shape[1] // HEAD_DIM
    rows = heads * BLK
    for h in range(heads):
        cols = pl.ds(h * HEAD_DIM, HEAD_DIM)
        q_ref[pl.ds(h * BLK, BLK), :] = own_q_ref[:, cols]
        q_ref[pl.ds(rows + h * BLK, BLK), :] = other_q_ref[:, cols]
    if last:
        for half, ref in ((0, own_in_ref), (1, send_in_ref)):
            acc_ref[half] = ref[0:HEAD_DIM, :]
            top_ref[half] = ref[HEAD_DIM : HEAD_DIM + 1, :]
            sum_ref[half] = ref[HEAD_DIM + 1 : HEAD_DIM + 2, :]
        count = order_ref[length]
    else:
        core = place_ref[0]
        block = place_ref[1]
        top_ref[...] = jnp.full_like(top_ref, NEG)
        sum_ref[...] = jnp.zeros_like(sum_ref)
        acc_ref[...] = jnp.zeros_like(acc_ref)

        def collect(i, count):
            device = list_ref[i] // local_blocks
            row = device // 8
            order_ref[count] = (row // 2) * 8 + device % 8
            return count + jnp.where(row % 2 == core, 1, 0)

        count = lax.fori_loop(0, length, collect, jnp.int32(0))
        order_ref[length] = count

    def update(half, keys, values, bias):
        part = pl.ds(half * rows, rows)
        scores = nt_dot(keys, q_ref[part, :]) * scale + bias
        old = top_ref[half]
        new = jnp.maximum(old, jnp.max(scores, axis=0, keepdims=True))
        weights = jnp.exp2(scores - new)
        decay = jnp.exp2(old - new)
        top_ref[half] = new
        sum_ref[half] = sum_ref[half] * decay + jnp.sum(weights, axis=0, keepdims=True)
        acc_ref[half] = acc_ref[half] * decay + tn_dot(values, weights.astype(bf16))

    def far(step, carry):
        slots = [order_ref[jnp.minimum(step * per_step + i, count - 1)] for i in range(per_step)]
        keys = jnp.concatenate([chunk_ref[s, 0:part_rows] for s in slots], axis=0)
        values = jnp.concatenate([chunk_ref[s, part_rows : 2 * part_rows] for s in slots], axis=0)
        bias = jnp.concatenate(
            [
                jnp.full((part_rows, 1), jnp.where(step * per_step + i < count, 0.0, NEG), f32)
                for i in range(per_step)
            ],
            axis=0,
        )
        for half in range(2):
            update(half, keys, values, bias)
        return carry

    lax.fori_loop(0, (count + per_step - 1) // per_step, far, 0)

    def near(j, carry):
        which = core + 2 * j
        shift = (block - which) * BLK
        key_pos = lax.broadcasted_iota(jnp.int32, (BLK, rows), 0)
        token = lax.broadcasted_iota(jnp.int32, (BLK, rows), 1) % BLK
        bias = jnp.where(key_pos <= token + shift, 0.0, NEG)
        at = 2 * part_rows
        eighth = BLK // 8
        keys = jnp.concatenate([chunk_ref[i * 8 + which, at : at + eighth] for i in range(8)], axis=0)
        values = jnp.concatenate([chunk_ref[i * 8 + which, at + eighth :] for i in range(8)], axis=0)
        for half in range(2):
            update(half, keys, values, bias)
        return carry

    if not last:
        lax.fori_loop(0, (block - core + 2) // 2, near, 0)
    for half, ref in ((0, own_ref), (1, send_ref)):
        ref[0:HEAD_DIM, :] = acc_ref[half]
        ref[HEAD_DIM : HEAD_DIM + 1, :] = top_ref[half]
        ref[HEAD_DIM + 1 : HEAD_DIM + 2, :] = sum_ref[half]


def attend(scalars, own_q, other_q, chunk, state, local_blocks, per_step):
    heads = own_q.shape[1] // HEAD_DIM
    rows = heads * BLK
    length = scalars[0].shape[0] - len(state) // 2
    packed = jax.ShapeDtypeStruct((HEAD_DIM + 8, rows), f32)
    smem = pl.BlockSpec(memory_space=pltpu.SMEM)
    vmem = pl.BlockSpec(memory_space=pltpu.VMEM)
    scale = math.log2(math.e) / math.sqrt(HEAD_DIM)
    arrays = [own_q, other_q, chunk, *state]
    outs = [packed, packed]
    if not state:
        outs.append(jax.ShapeDtypeStruct((length + 1,), jnp.int32))
    return pl.pallas_call(
        functools.partial(attend_kernel, scale, per_step, local_blocks, len(state) > 0),
        out_shape=outs,
        in_specs=[smem] * len(scalars) + [vmem] * len(arrays),
        out_specs=[vmem, vmem, smem][: len(outs)],
        scratch_shapes=[
            pltpu.VMEM((2 * rows, HEAD_DIM), bf16),
            pltpu.VMEM((2, 1, rows), f32),
            pltpu.VMEM((2, 1, rows), f32),
            pltpu.VMEM((2, HEAD_DIM, rows), f32),
        ],
        compiler_params=pltpu.CompilerParams(vmem_limit_bytes=24 * 1024 * 1024),
        cost_estimate=pl.CostEstimate(
            flops=2 * rows * 40 * chunk.shape[1] * HEAD_DIM,
            bytes_accessed=2 * chunk.size,
            transcendentals=rows * 40 * chunk.shape[1],
        ),
    )(*scalars, *arrays)


def merge_kernel(own_ref, got_ref, out_ref):
    own_top = own_ref[HEAD_DIM : HEAD_DIM + 1, :]
    got_top = got_ref[HEAD_DIM : HEAD_DIM + 1, :]
    top = jnp.maximum(own_top, got_top)
    own_w = jnp.exp2(own_top - top)
    got_w = jnp.exp2(got_top - top)
    total = own_w * own_ref[HEAD_DIM + 1 : HEAD_DIM + 2, :] + got_w * got_ref[HEAD_DIM + 1 : HEAD_DIM + 2, :]
    mixed = (own_ref[0:HEAD_DIM, :] * own_w + got_ref[0:HEAD_DIM, :] * got_w) / total
    heads = mixed.shape[1] // BLK
    for h in range(heads):
        piece = mixed[:, h * BLK : (h + 1) * BLK].T.astype(bf16)
        for i in range(out_ref.shape[0]):
            out_ref[i, :, pl.ds(h * HEAD_DIM, HEAD_DIM)] = piece


def merge(own, got, copies):
    heads = own.shape[1] // BLK
    vmem = pl.BlockSpec(memory_space=pltpu.VMEM)
    return pl.pallas_call(
        merge_kernel,
        out_shape=jax.ShapeDtypeStruct((copies, BLK, heads * HEAD_DIM), bf16),
        in_specs=[vmem, vmem],
        out_specs=vmem,
        compiler_params=pltpu.CompilerParams(vmem_limit_bytes=12 * 1024 * 1024),
    )(own, got)


def product_kernel(tile, weight_count, pick_ref, x_ref, *refs):
    weight_refs, add_ref, out_ref = refs[:weight_count], refs[weight_count:-1], refs[-1]
    x = x_ref[:, pick_ref[0]] if x_ref.shape[1] > out_ref.shape[1] else x_ref[...]
    x = x.reshape(-1, x.shape[-1])
    width = weight_refs[0].shape[1]
    block = out_ref.shape[:-1] + (tile,)
    for i, weight_ref in enumerate(weight_refs):
        for first in range(0, width, tile):
            total = jnp.dot(x, weight_ref[:, first : first + tile], preferred_element_type=f32)
            columns = slice(i * width + first, i * width + first + tile)
            if add_ref:
                total = total + add_ref[0][..., columns].reshape(total.shape).astype(f32)
            out_ref[..., columns] = total.astype(bf16).reshape(block)


def product(x, weights, tile, pick=None, add=None):
    blocks, pair, tokens, inputs = x.shape
    taken = pair if pick is None else 1
    pick = jnp.zeros((1,), jnp.int32) if pick is None else pick.astype(jnp.int32).reshape(1)
    vmem = pl.BlockSpec(memory_space=pltpu.VMEM)
    operands = [x, *weights] if add is None else [x, *weights, add]
    rows = blocks * taken * tokens
    columns = weights[0].shape[1] * len(weights)
    return pl.pallas_call(
        functools.partial(product_kernel, tile, len(weights)),
        out_shape=jax.ShapeDtypeStruct((blocks, taken, tokens, columns), bf16),
        in_specs=[pl.BlockSpec(memory_space=pltpu.SMEM)] + [vmem] * len(operands),
        out_specs=vmem,
        compiler_params=pltpu.CompilerParams(vmem_limit_bytes=20 * 1024 * 1024),
        cost_estimate=pl.CostEstimate(
            flops=2 * rows * inputs * columns,
            bytes_accessed=2 * (rows * inputs + inputs * columns + rows * columns),
            transcendentals=0,
        ),
    )(pick, *operands)


VMEM = pl.BlockSpec(memory_space=pltpu.VMEM)
SMEM = pl.BlockSpec(memory_space=pltpu.SMEM)


def small_call(kernel, outs, scalars, arrays, moved):
    return pl.pallas_call(
        kernel,
        out_shape=outs,
        in_specs=[SMEM] * len(scalars) + [VMEM] * len(arrays),
        out_specs=jax.tree.map(lambda _: VMEM, outs),
        compiler_params=pltpu.CompilerParams(vmem_limit_bytes=16 * 1024 * 1024),
        cost_estimate=pl.CostEstimate(flops=moved, bytes_accessed=moved, transcendentals=0),
    )(*scalars, *arrays)


def columns_kernel(place_ref, mine_ref, theirs_ref, gate_ref, up_ref, *out_refs):
    y, side = place_ref[0], place_ref[1]
    n = mine_ref.shape[2]
    x = jnp.concatenate(
        [ref[(y + i) % 4, s] for s in (1 - side, side) for i in range(4) for ref in (mine_ref, theirs_ref)],
        axis=0,
    )
    step = pl.program_id(0)

    def put(weight_ref):
        total = jnp.dot(x, weight_ref[...], preferred_element_type=f32).astype(bf16)
        for i, ref in enumerate(out_refs[:12]):
            at = (0, 1, 2, 3, 4, 5, 6, 7, 8, 9, 10, 15)[i]
            ref[...] = total[at * n : (at + 1) * n]
        for ref, pair in ((out_refs[12], (12, 11)), (out_refs[13], (13, 14))):
            for j, at in enumerate(pair):
                ref[j] = total[at * n : (at + 1) * n]

    half = pl.num_programs(0) // 2
    pl.when(step < half)(functools.partial(put, gate_ref))
    pl.when(step >= half)(functools.partial(put, up_ref))


def partial_columns(place, mine, theirs, gate, up):
    tile = 896
    inputs, width = gate.shape
    count = width // tile
    tokens = mine.shape[2]
    whole = pl.BlockSpec(mine.shape, lambda n, p: (0, 0, 0, 0))
    rows = 16 * tokens
    return pl.pallas_call(
        columns_kernel,
        out_shape=(jax.ShapeDtypeStruct((tokens, 2 * width), bf16),) * 12
        + (jax.ShapeDtypeStruct((2, tokens, 2 * width), bf16),) * 2,
        grid_spec=pltpu.PrefetchScalarGridSpec(
            num_scalar_prefetch=1,
            grid=(2 * count,),
            in_specs=[
                whole,
                whole,
                pl.BlockSpec((inputs, tile), lambda n, p: (0, jnp.minimum(n, count - 1))),
                pl.BlockSpec((inputs, tile), lambda n, p: (0, jnp.maximum(n - count, 0))),
            ],
            out_specs=(pl.BlockSpec((tokens, tile), lambda n, p: (0, n)),) * 12
            + (pl.BlockSpec((2, tokens, tile), lambda n, p: (0, 0, n)),) * 2,
        ),
        compiler_params=pltpu.CompilerParams(vmem_limit_bytes=60 * 1024 * 1024),
        cost_estimate=pl.CostEstimate(
            flops=4 * rows * inputs * width,
            bytes_accessed=2 * (rows * inputs + 2 * inputs * width + 2 * rows * width),
            transcendentals=0,
        ),
    )(place, mine, theirs, gate, up)


def add_pieces(piece, other):
    def kernel(a_ref, b_ref, out_ref):
        b = b_ref[...] if other.ndim == 2 else b_ref[0]
        out_ref[...] = (a_ref[...].astype(f32) + b.astype(f32)).astype(bf16)

    out = jax.ShapeDtypeStruct(piece.shape, bf16)
    return small_call(kernel, out, (), (piece, other), 2 * piece.size)


def add_halves(*halves):
    count = len(halves[0])

    def kernel(*refs):
        for i in range(len(halves)):
            mine = refs[i * count : (i + 1) * count]
            refs[-1][i] = sum(r[...].astype(f32) for r in mine).astype(bf16)

    first = halves[0][0]
    out = jax.ShapeDtypeStruct((len(halves), *first.shape), bf16)
    return small_call(kernel, out, (), [p for h in halves for p in h], 8 * first.size)


def gated(halves, got, factor):
    count = len(halves[0])
    tokens, width = halves[0][0].shape[0], halves[0][0].shape[1] // 2

    def kernel(*refs):
        got_ref, factor_ref, out_ref = refs[-3:]
        for i in range(len(halves)):
            rows = pl.ds(i * tokens, tokens)
            mine = refs[i * count : (i + 1) * count]
            scale = factor_ref[rows, :]

            def total(columns):
                parts = sum((r[:, columns] if len(r.shape) == 2 else r[1, :, columns]).astype(f32) for r in mine)
                return (parts + got_ref[i, :, columns].astype(f32)) * scale

            gate = total(slice(0, width))
            up = total(slice(width, 2 * width))
            out_ref[rows, :] = (gate / (1.0 + jnp.exp(-gate)) * up).astype(bf16)

    out = jax.ShapeDtypeStruct((tokens * len(halves), width), bf16)
    arrays = [p for h in halves for p in h] + [got, factor[:, None]]
    return small_call(kernel, out, (), arrays, 16 * tokens * width)


def down_product(pieces, weight):
    tile = 512
    count, tokens, inputs = len(pieces), pieces[0].shape[0] // 2, pieces[0].shape[1]
    width = weight.shape[1]

    def kernel(*refs):
        weight_ref, keep_ref, give_ref = refs[count:]
        x = jnp.concatenate([p[...] for p in refs[:count]], axis=0)
        total = jnp.dot(x, weight_ref[...], preferred_element_type=f32)
        for i in range(count):
            at = 2 * i * tokens
            keep_ref[i] = total[at : at + tokens]
            give_ref[i] = total[at + tokens : at + 2 * tokens].astype(bf16)

    by_column = pl.BlockSpec((count, tokens, tile), lambda n: (0, 0, n))
    specs = [pl.BlockSpec((2 * tokens, inputs), lambda n: (0, 0))] * count
    return pl.pallas_call(
        kernel,
        grid=(width // tile,),
        out_shape=(
            jax.ShapeDtypeStruct((count, tokens, width), f32),
            jax.ShapeDtypeStruct((count, tokens, width), bf16),
        ),
        in_specs=specs + [pl.BlockSpec((inputs, tile), lambda n: (0, n))],
        out_specs=(by_column, by_column),
        compiler_params=pltpu.CompilerParams(vmem_limit_bytes=24 * 1024 * 1024),
        cost_estimate=pl.CostEstimate(
            flops=4 * count * tokens * inputs * width,
            bytes_accessed=2 * (2 * count * tokens * inputs + inputs * width + 3 * count * tokens * width),
            transcendentals=0,
        ),
    )(*pieces, weight)


def join_blocks(place, near, far):
    def kernel(place_ref, near_ref, near_got_ref, far_ref, far_got_ref, out_ref):
        y, side = place_ref[0], place_ref[1]
        for i, (kept_ref, got_ref, first) in enumerate(
            (
                (near_ref, near_got_ref, 0),
                (near_ref, near_got_ref, 2),
                (far_ref, far_got_ref, 0),
                (near_ref, near_got_ref, 4),
            )
        ):
            for j in range(2):
                at = 2 * ((y + i) % 4) + (side if j == 0 else 1 - side)
                out_ref[at] = (kept_ref[first + j] + got_ref[first + j].astype(f32)).astype(bf16)

    out = jax.ShapeDtypeStruct((8, *near[0].shape[1:]), bf16)
    return small_call(kernel, out, (place,), (*near, *far), 4 * near[0].size)


def to_right(x):
    return lax.ppermute(x, "y", [(i, (i + 1) % 4) for i in range(4)])


def to_left(x):
    return lax.ppermute(x, "y", [(i, (i + 3) % 4) for i in range(4)])


def ring_start(pieces):
    right, left, opposite = pieces[2:4], pieces[6:8], pieces[4:6]
    return to_right(opposite[0]), to_left(opposite[1]), to_right(right[1]), to_left(left[0])


def ring_middle(pieces, from_left, from_right):
    return add_pieces(pieces[2], from_left), add_pieces(pieces[7], from_right)


def ring_end(pieces, arrived, sums):
    third_left, third_right = to_right(sums[0]), to_left(sums[1])
    return (pieces[0], arrived[3], third_left), (pieces[1], arrived[2], third_right)


def gather_start(mine):
    return to_right(mine), to_left(mine)


def pack_kernel(within_ref, group_ref, keys_ref, values_ref, near_keys_ref, near_values_ref, out_ref):
    eighth = BLK // 8
    rows = (out_ref.shape[1] - 2 * eighth) // 2
    goal = pl.program_id(0)
    near = pl.ds(pl.multiple_of(group_ref[0] * eighth, eighth), eighth)
    for i in range(out_ref.shape[0]):
        at = within_ref[goal, i]
        out_ref[i, 0:rows] = keys_ref[at, 0:rows]
        out_ref[i, rows : 2 * rows] = values_ref[at, 0:rows]
        out_ref[i, 2 * rows : 2 * rows + eighth] = near_keys_ref[0, near]
        out_ref[i, 2 * rows + eighth :] = near_values_ref[0, near]


def pack(within, group, keys, values, near_keys, near_values, rows):
    def of_group(x, height):
        return pl.BlockSpec((x.shape[0] // KV_HEADS, height, HEAD_DIM), lambda n, s, g: (n, 0, 0))

    arrays = ((keys, rows), (values, rows), (near_keys, BLK), (near_values, BLK))
    height = 2 * rows + BLK // 4
    return pl.pallas_call(
        pack_kernel,
        out_shape=jax.ShapeDtypeStruct((64, height, HEAD_DIM), bf16),
        grid_spec=pltpu.PrefetchScalarGridSpec(
            num_scalar_prefetch=2,
            grid=(8,),
            in_specs=[of_group(*x) for x in arrays],
            out_specs=pl.BlockSpec((8, height, HEAD_DIM), lambda n, s, g: (n, 0, 0)),
        ),
        compiler_params=pltpu.CompilerParams(vmem_limit_bytes=60 * 1024 * 1024),
        cost_estimate=pl.CostEstimate(flops=0, bytes_accessed=64 * height * 512, transcendentals=0),
    )(within, group.astype(jnp.int32).reshape(1), *[x for x, _ in arrays])


def exchange(x, axes):
    return lax.all_to_all(x, axes, split_axis=0, concat_axis=0, tiled=True)


def swap(x, axis="core"):
    return lax.ppermute(x, axis, [(0, 1), (1, 0)])


def spread(x, copies):
    return jnp.broadcast_to(x[None], (copies,) + x.shape)


def take(x, index, axis):
    return lax.dynamic_index_in_dim(x, index, axis, keepdims=False)


def local(
    queries,
    cache_keys,
    cache_values,
    stretch_keys,
    stretch_values,
    block_lists,
    out_weight,
    residual,
    norm_gain,
    gate_weight,
    up_weight,
    down_weight,
):
    core = lax.axis_index("core")
    side = lax.axis_index("xl")
    col = lax.axis_index(COL)
    group = lax.axis_index(ZXH)
    me = lax.axis_index(ROW) * 8 + col
    local_blocks = cache_keys.shape[1] // BLK
    tokens_here = residual.shape[0]

    matched = block_lists // local_blocks == me
    within = jnp.sum(jnp.where(matched, block_lists % local_blocks, 0), axis=2)
    source = (jnp.arange(KV_HEADS, dtype=jnp.int32)[:, None] * local_blocks + within.T).reshape(-1)

    piece = BLK // 4
    flat_keys = cache_keys.reshape(4 * KV_HEADS * local_blocks, piece, HEAD_DIM)
    flat_values = cache_values.reshape(4 * KV_HEADS * local_blocks, piece, HEAD_DIM)

    def pick(flat, first, count):
        index = 4 * source[:, None] + jnp.arange(first, first + count, dtype=jnp.int32)[None, :]
        return flat[index].reshape(64, count * piece, HEAD_DIM)

    blocked = (KV_HEADS * local_blocks, BLK, HEAD_DIM)
    first = pack(
        within.T, group, cache_keys.reshape(blocked), cache_values.reshape(blocked),
        stretch_keys, stretch_values, 3 * piece,
    )
    first = exchange(first, CHIP)
    second = [pick(flat_keys, 3, 1), pick(flat_values, 3, 1)]
    second = exchange(jnp.concatenate(second, axis=1), CHIP)
    my_list = block_lists[col, group]
    place = jnp.stack([core, col]).astype(jnp.int32)
    other_queries = swap(queries)
    own, send, order = attend((my_list, place), queries, other_queries, first, (), local_blocks, 5)
    own, send = attend((order,), queries, other_queries, second, (own, send), local_blocks, 16)
    attended = exchange(merge(own, swap(send), 8), COL).reshape(8, 2, tokens_here, -1)

    def row_sum(give, mine, pick, weight):
        both = product(mine, (weight,), 512, pick, add=swap(give))
        return jnp.sum(exchange(both.reshape(8, tokens_here, -1), ZXH).astype(f32), axis=0)

    give = product(attended, (out_weight,), 512, 1 - core)
    stream = residual.astype(f32) + row_sum(give, attended, core, out_weight)
    gain = norm_gain.astype(f32)[None, :]
    own_rows = exchange(spread((stream * gain).astype(bf16), 8), ZXH)
    other_rows = swap(own_rows)

    def squares(x):
        plain = x.astype(f32) / gain[None]
        return jnp.sum(plain * plain, axis=2)

    squares = jnp.stack([squares(own_rows), squares(other_rows)], axis=1)

    by_pair = (4, 2, tokens_here, own_rows.shape[-1])
    where = jnp.stack([lax.axis_index("y"), side]).astype(jnp.int32)
    columns = partial_columns(
        where, own_rows.reshape(by_pair), other_rows.reshape(by_pair), gate_weight, up_weight
    )
    columns, squares = lax.optimization_barrier((columns, exchange(squares, COL)))
    theirs, mine = columns[:8], columns[8:]
    arrived = ring_start(theirs)
    sums = ring_middle(theirs, *arrived[:2])
    sums, mine = lax.optimization_barrier((sums, mine))
    halves = ring_end(theirs, arrived, sums)
    own_first, own_second, right, left, go_right, go_left = mine
    from_left, from_right = to_right(go_right), to_left(go_left)
    got = swap(add_halves(*halves), "xl")
    factor = lax.rsqrt(jnp.sum(squares, axis=0).reshape(-1) / D + 1e-05)
    third_left, third_right = to_right(add_pieces(right, from_left)), to_left(add_pieces(left, from_right))
    halves = (own_first, third_left, from_right), (own_second, third_right, from_left)
    hidden = gated(halves, got, factor)
    first, hidden_got = lax.optimization_barrier((gather_start(hidden), swap(hidden, "xl")))
    got_left, got_right = to_right(hidden_got), to_left(hidden_got)
    mine_far = to_right(first[0])
    got_far = to_left(got_right)
    near = (hidden, hidden_got, first[1], got_right, first[0], got_left)
    kept, give = down_product(near, down_weight)
    far_kept, far_give = down_product((mine_far, got_far), down_weight)
    down = join_blocks(where, (kept, swap(give)), (far_kept, swap(far_give)))
    mlp = jnp.sum(exchange(down, ZXH).astype(f32), axis=0)
    return (stream + mlp).astype(bf16)


def solution(mesh):
    mesh = Mesh(mesh.devices.reshape(4, 2, 2, 4, 2), AXES)
    in_specs = (
        P(COL, ROW),
        P(None, ROW + COL, None),
        P(None, ROW + COL, None),
        P(None, COL, None),
        P(None, COL, None),
        P(),
        P(ROW, COL),
        P(ROW, COL),
        P(COL),
        P(COL, ROW),
        P(COL, ROW),
        P(ROW, COL),
    )
    return jax.shard_map(local, mesh=mesh, in_specs=in_specs, out_specs=P(ROW, COL), check_vma=False)
```
